32 devices in a mesh: fsdp: 2 (over x), ctx: 4 (over y, core), tp: 4 (over z).
Axes of the slice: x: 2, y: 2, z: 4, core: 2. Of those that a mesh axis runs over, the one named last changes fastest.
Arguments:
- tokens: bfloat16 [196, 8, 4, 768], P('tp', 'ctx', 'fsdp'), may hold values from -6 to 6
- norm_gains: bfloat16 [3, 768], P(None, 'fsdp'), may hold values from 0.099609375 to 1.8984375
- temporal_qkv: bfloat16 [768, 3, 768], P('fsdp', None, 'tp'), may hold values from -0.21875 to 0.21875
- temporal_proj: bfloat16 [768, 768], P('tp', 'fsdp'), may hold values from -0.3125 to 0.3125
- spatial_qkv: bfloat16 [768, 3, 768], P('fsdp', None, 'tp'), may hold values from -0.21875 to 0.21875
- spatial_proj: bfloat16 [768, 768], P('tp', 'fsdp'), may hold values from -1.5 to 1.5
- up_weight: bfloat16 [768, 3072], P('fsdp', 'tp'), may hold values from -0.21875 to 0.21875
- down_weight: bfloat16 [3072, 768], P('tp', 'fsdp'), may hold values from -0.109375 to 0.109375
- cotangent: bfloat16 [196, 8, 4, 768], P('tp', 'ctx', 'fsdp'), may hold values from -6 to 6
Outputs:
- block_out: bfloat16 [196, 8, 4, 768], P('tp', 'ctx', 'fsdp')
- tokens_grad: float32 [196, 8, 4, 768], P('tp', 'ctx', 'fsdp')
- norm_gains_grad: float32 [3, 768], P(None, 'fsdp')
- temporal_qkv_grad: float32 [768, 3, 768], P('fsdp', None, 'tp')
- temporal_proj_grad: float32 [768, 768], P('tp', 'fsdp')
- spatial_qkv_grad: float32 [768, 3, 768], P('fsdp', None, 'tp')
- spatial_proj_grad: float32 [768, 768], P('tp', 'fsdp')
- up_weight_grad: float32 [768, 3072], P('fsdp', 'tp')
- down_weight_grad: float32 [3072, 768], P('tp', 'fsdp')
The draws below stay inside these ranges and needn't reach their ends.
All inputs are finite; a program needn't handle non-finite values.
Results may differ from the reference program's by a relative error of at most 0.03.
Values may be sent and summed in bfloat16 or wider, within the bound.
No kernel may reach another device: no remote copies, remote signals or barrier semaphores. Data moves between devices by JAX's collectives and lax.ppermute only.
A program may use at most 128 MiB of HBM per device.

```python
import jax
import jax.numpy as jnp
from jax import lax

D = 768
HEADS = 12
HEAD_DIM = 64
FF = 3072
FRAMES = 8
PLACES = 196
CLIPS = 4


def shard_levels(key, extent, cuts, low, top_value):
    def one(position, blocks):
        steps = jax.random.uniform(jax.random.fold_in(jax.random.fold_in(key, 6), position), (blocks,), jnp.float32, low / len(cuts), top_value / len(cuts))
        return jnp.repeat(jnp.exp(steps), extent[position] // blocks).reshape((-1,) + (1,) * (len(extent) - position - 1))

    gain = one(*cuts[0])
    for cut in cuts[1:]:
        gain = gain * one(*cut)
    return gain


def gaussian(key, shape, width, bound, pieces=(), held_as=jnp.bfloat16):
    factor_of = shard_levels(key, shape, pieces, -0.22, 0.18) if pieces else 1.0
    drawn = jax.random.normal(key, shape, jnp.float32) * width * factor_of
    return jnp.minimum(jnp.maximum(drawn, -bound), bound).astype(held_as)


def setup_inputs(seed: int = 0) -> dict:
    splits = jax.random.split(jax.random.key(seed), 10)
    tokens = gaussian(splits[0], (PLACES, FRAMES, CLIPS, D), 1.0, 6.0, ((0, 4), (1, 4), (2, 2)))
    norm_gains = jnp.clip(1.0 + 0.18 * jax.random.normal(splits[1], (3, D), jnp.float32), 0.099609375, 1.8984375).astype(jnp.bfloat16)
    temporal_qkv = gaussian(splits[2], (D, 3, D), D ** -0.5, 0.21875, ((0, 2), (2, 4)))
    temporal_proj = gaussian(splits[3], (D, D), (D * 4 // FRAMES) ** -0.5, 0.3125, ((0, 4), (1, 2)))
    spatial_qkv = gaussian(splits[4], (D, 3, D), D ** -0.5, 0.21875, ((0, 2), (2, 4)))
    spatial_proj = gaussian(splits[5], (D, D), (D * 4 // PLACES) ** -0.5, 1.5, ((0, 4), (1, 2)))
    up_weight = gaussian(splits[6], (D, FF), D ** -0.5, 0.21875, ((0, 2), (1, 4)))
    down_weight = gaussian(splits[7], (FF, D), FF ** -0.5, 0.109375, ((0, 4), (1, 2)))
    cotangent = gaussian(splits[8], (PLACES, FRAMES, CLIPS, D), 1.0, 6.0, ((0, 4), (1, 4), (2, 2)))
    return {"tokens": tokens, "norm_gains": norm_gains, "temporal_qkv": temporal_qkv, "temporal_proj": temporal_proj, "spatial_qkv": spatial_qkv, "spatial_proj": spatial_proj, "up_weight": up_weight, "down_weight": down_weight, "cotangent": cotangent}


@jax.custom_vjp
def low(v):
    return lax.optimization_barrier(v.astype(jnp.bfloat16)).astype(jnp.float32)

@jax.custom_vjp
def low_back(v):
    return v

def low_keep(v):
    return (low(v), None)

def low_pass(kept, grad):
    return (grad,)

def back_keep(v):
    return (v, None)

def back_low(kept, grad):
    return (low(grad),)
low.defvjp(low_keep, low_pass)
low_back.defvjp(back_keep, back_low)
EPSILON = 1e-06
HIGHEST = lax.Precision.HIGHEST

def layer_norm(values, gain_row):
    center = values - lax.optimization_barrier(jnp.mean(values, axis=-1, keepdims=True))
    spread = lax.optimization_barrier(jnp.mean(center * center, axis=-1, keepdims=True))
    return center * lax.rsqrt(spread + EPSILON) * gain_row

def split_heads(joined_rows):
    return tuple((joined_rows[:, :, member].reshape(PLACES, FRAMES, HEADS, HEAD_DIM) for member in range(3)))

def temporal_core(queries, key_rows, value_rows):
    scores = low_back(jnp.einsum('pfhe,pghe->phfg', queries, key_rows, precision=HIGHEST) * HEAD_DIM ** (-0.5))
    weights = low(jax.nn.softmax(scores, axis=-1))
    return jnp.einsum('phfg,pghe->pfhe', weights, value_rows, precision=HIGHEST)

def spatial_core(queries, key_rows, value_rows):
    scores = low_back(jnp.einsum('pfhe,qfhe->fhpq', queries, key_rows, precision=HIGHEST) * HEAD_DIM ** (-0.5))
    weights = low(jax.nn.softmax(scores, axis=-1))
    return jnp.einsum('fhpq,qfhe->pfhe', weights, value_rows, precision=HIGHEST)

def attention_branch(inputs, gain_row, joined_weight, proj_weight, attend):
    normed = low(layer_norm(inputs, gain_row))
    joined_rows = low(low_back(jnp.einsum('pfd,dke->pfke', normed, joined_weight, precision=HIGHEST)))
    queries, key_rows, value_rows = split_heads(joined_rows)
    heads_out = attend(queries, key_rows, value_rows).reshape(PLACES, FRAMES, D)
    heads_out = low(low_back(heads_out))
    return low_back(jnp.einsum('pfe,ed->pfd', heads_out, proj_weight, precision=HIGHEST))

def forward(inputs, parameters):
    norm_gains, temporal_qkv, temporal_proj, spatial_qkv, spatial_proj, up_weight, down_weight = parameters
    after_time = inputs + attention_branch(inputs, norm_gains[0], temporal_qkv, temporal_proj, temporal_core)
    after_space = after_time + attention_branch(after_time, norm_gains[1], spatial_qkv, spatial_proj, spatial_core)
    normed = low(layer_norm(after_space, norm_gains[2]))
    hidden = low_back(jnp.einsum('pfd,dh->pfh', normed, up_weight, precision=HIGHEST))
    activated = low(jax.nn.gelu(hidden, approximate=False))
    return after_space + low_back(jnp.einsum('pfh,hd->pfd', activated, down_weight, precision=HIGHEST))

def reference(tokens, norm_gains, temporal_qkv, temporal_proj, spatial_qkv, spatial_proj, up_weight, down_weight, cotangent):
    parameters = tuple((member.astype(jnp.float32) for member in (norm_gains, temporal_qkv, temporal_proj, spatial_qkv, spatial_proj, up_weight, down_weight)))
    clip_tokens = jnp.moveaxis(tokens, 2, 0)
    clip_cotangents = jnp.moveaxis(cotangent, 2, 0)

    def one_clip(totals, clip_pair):
        clip_rows, clip_cotangent = clip_pair
        result, pullback = jax.vjp(forward, clip_rows.astype(jnp.float32), parameters)
        input_grad, param_grads = pullback(clip_cotangent.astype(jnp.float32))
        totals = jax.tree.map(lambda running, addend: running + addend, totals, param_grads)
        return (totals, (result.astype(jnp.bfloat16), input_grad))
    zero_grads = tuple((jnp.zeros(member.shape, jnp.float32) for member in parameters))
    totals, (results, input_grads) = lax.scan(one_clip, zero_grads, (clip_tokens, clip_cotangents))
    return (jnp.moveaxis(results, 0, 2), jnp.moveaxis(input_grads, 0, 2), totals[0], totals[1], totals[2], totals[3], totals[4], totals[5], totals[6])
```

```python
import functools

import jax
import jax.numpy as jnp
from jax import lax
from jax.experimental import pallas as pl
from jax.experimental.pallas import tpu as pltpu
from jax.sharding import PartitionSpec as P

HEAD_DIM = 64
EPSILON = 1e-06
SCALE = HEAD_DIM ** (-0.5)
F32 = jnp.float32
LOW = jnp.bfloat16
VMEM = pltpu.VMEM


def dot(a, b, ca, cb):
    return lax.dot_general(a, b, (((ca,), (cb,)), ((), ())), preferred_element_type=F32)


def statistics(rows):
    center = rows - jnp.mean(rows, axis=-1, keepdims=True)
    rate = lax.rsqrt(jnp.mean(center * center, axis=-1, keepdims=True) + EPSILON)
    return center * rate, rate


def norm_back(grad, gain, hat, rate):
    t = grad * gain
    return rate * (
        t
        - jnp.mean(t, axis=-1, keepdims=True)
        - hat * jnp.mean(t * hat, axis=-1, keepdims=True)
    )


def to_blocks(own, pair, frames_cut):
    if not frames_cut:
        return jnp.concatenate((own, pair), axis=0)
    half = own.shape[0] // 2
    return jnp.concatenate((own[:half], pair[:half], own[half:], pair[half:]), axis=0)


def from_blocks(rows, frames_cut):
    if not frames_cut:
        return rows
    q = rows.shape[0] // 4
    return jnp.concatenate((rows[:q], rows[2 * q : 3 * q], rows[q : 2 * q], rows[3 * q :]), axis=0)


def columns(off_ref, piece, width):
    return pl.ds(pl.multiple_of(off_ref[piece], 128), width)


def attend_forward_kernel(pieces, frames_cut, *refs):
    off, own, pair, gain, bias = refs[:5]
    weights = refs[5 : 5 + 2 * pieces]
    part, normed, joined_a, joined_b, out_a, out_b, total = refs[5 + 2 * pieces :]
    rows = to_blocks(own[...].astype(F32), pair[...].astype(F32), frames_cut)
    hat, _ = statistics(rows)
    normed[...] = (hat * gain[...]).astype(LOW)
    width = weights[0].shape[0]
    heads3 = joined_a.shape[1]
    for group, joined in enumerate((joined_a, joined_b)):
        acc = None
        for p in range(pieces):
            w = weights[group * pieces + p]
            term = dot(normed[:, columns(off, p, width)], w[:, :heads3], 1, 0)
            acc = term if acc is None else acc + term
        joined[...] = acc.astype(LOW)
    block = normed.shape[0] // 2
    inner = heads3 // 3

    def one_block(b, carry):
        at = pl.ds(pl.multiple_of(b * block, 16), block)
        for joined, out in ((joined_a, out_a), (joined_b, out_b)):
            rows3 = joined[at, :]
            parts = []
            for h in range(inner // HEAD_DIM):
                lo = h * HEAD_DIM
                q = rows3[:, lo : lo + HEAD_DIM]
                k = rows3[:, inner + lo : inner + lo + HEAD_DIM]
                v = rows3[:, 2 * inner + lo : 2 * inner + lo + HEAD_DIM]
                s = dot(q, k, 1, 1) * SCALE + bias[...]
                e = jnp.exp(s - jnp.max(s, axis=-1, keepdims=True))
                w = (e / jnp.sum(e, axis=-1, keepdims=True)).astype(LOW)
                parts.append(dot(w, v, 1, 0))
            out[at, :] = jnp.concatenate(parts, axis=1).astype(LOW)
        return carry

    lax.fori_loop(0, 2, one_block, 0)
    for p in range(pieces):
        total[:, columns(off, p, width)] = dot(
            out_a[...], weights[p][:, heads3:], 1, 1
        ) + dot(out_b[...], weights[pieces + p][:, heads3:], 1, 1)
    part[...] = from_blocks(total[...], frames_cut).astype(LOW)


def attend_backward_kernel(pieces, frames_cut, *refs):
    n_in = 10 if frames_cut else 2
    off, bias, normed, joined_a, joined_b, out_a, out_b = refs[:7]
    head = refs[7 : 7 + n_in]
    weights = refs[7 + n_in : 7 + n_in + 2 * pieces]
    rest = list(refs[7 + n_in + 2 * pieces :])
    part = rest.pop(0)
    grads = [rest.pop(0) for _ in range(pieces)]
    if frames_cut:
        carried, gain_grad = rest.pop(0), rest.pop(0)
    upstream, djoined_a, djoined_b, dout_a, dout_b, total = rest
    half = upstream.shape[0] // 2
    if frames_cut:
        base_own, base_pair, add_l, add_r, grad_l, grad_r, gain, cot_own, cot_pair, _ = head
        both = []
        for lo, base, cot in ((0, base_own, cot_own), (half, base_pair, cot_pair)):
            at = slice(lo, lo + half)
            rows = base[...].astype(F32) + (add_l[at, :].astype(F32) + add_r[at, :].astype(F32))
            hat, rate = statistics(rows)
            dn = grad_l[at, :].astype(F32) + grad_r[at, :].astype(F32)
            dx = cot[...].astype(F32) + norm_back(dn, gain[...], hat, rate)
            if lo == 0:
                carried[...] = dx
                gain_grad[...] = jnp.sum(dn * hat, axis=0, keepdims=True)
            both.append(dx)
        upstream[...] = to_blocks(both[0], both[1], frames_cut).astype(LOW)
    else:
        upstream[:half, :] = head[0][...]
        upstream[half:, :] = head[1][...]
    width = weights[0].shape[0]
    heads3 = joined_a.shape[1]
    inner = heads3 // 3
    for group, (out, dout) in enumerate(((out_a, dout_a), (out_b, dout_b))):
        acc = None
        for p in range(pieces):
            w = weights[group * pieces + p]
            dy = upstream[:, columns(off, p, width)]
            term = dot(dy, w[:, heads3:], 1, 0)
            acc = term if acc is None else acc + term
            grads[p][group, :, heads3:] = dot(dy, out[...], 0, 0).astype(LOW)
        dout[...] = acc.astype(LOW)

    def one_block(b, carry):
        at = pl.ds(pl.multiple_of(b * half, 16), half)
        for joined, dout, djoined in (
            (joined_a, dout_a, djoined_a),
            (joined_b, dout_b, djoined_b),
        ):
            rows3 = joined[at, :]
            do3 = dout[at, :]
            dqs, dks, dvs = [], [], []
            for h in range(inner // HEAD_DIM):
                lo = h * HEAD_DIM
                q = rows3[:, lo : lo + HEAD_DIM]
                k = rows3[:, inner + lo : inner + lo + HEAD_DIM]
                v = rows3[:, 2 * inner + lo : 2 * inner + lo + HEAD_DIM]
                do = do3[:, lo : lo + HEAD_DIM]
                s = dot(q, k, 1, 1) * SCALE + bias[...]
                e = jnp.exp(s - jnp.max(s, axis=-1, keepdims=True))
                w = e / jnp.sum(e, axis=-1, keepdims=True)
                dw = dot(do, v, 1, 1)
                ds = (w * (dw - jnp.sum(w * dw, axis=-1, keepdims=True))).astype(LOW)
                dqs.append(dot(ds, k, 1, 0) * SCALE)
                dks.append(dot(ds, q, 0, 0) * SCALE)
                dvs.append(dot(w.astype(LOW), do, 0, 0))
            djoined[at, :] = jnp.concatenate(dqs + dks + dvs, axis=1).astype(LOW)
        return carry

    lax.fori_loop(0, 2, one_block, 0)
    for p in range(pieces):
        cols = columns(off, p, width)
        wide = normed[:, cols]
        for group, djoined in enumerate((djoined_a, djoined_b)):
            grads[p][group, :, :heads3] = dot(wide, djoined[...], 0, 0).astype(LOW)
        total[:, cols] = dot(djoined_a[...], weights[p][:, :heads3], 1, 1) + dot(
            djoined_b[...], weights[pieces + p][:, :heads3], 1, 1
        )
    part[...] = from_blocks(total[...], frames_cut).astype(LOW)


def feed_kernel(pieces, chunks, packed, *refs):
    off, base_own, base_pair, add_l, add_r, gain, cot_own, cot_pair = refs[:8]
    at = 8
    n_w = chunks * pieces * (1 if packed else 2)
    weights = refs[at : at + n_w]
    at += n_w
    out_part, dn_part = refs[at : at + 2]
    at += 2
    grads = refs[at : at + n_w // 2]
    at += n_w // 2
    normed, cot, total, dtotal = refs[at:]
    half = normed.shape[0] // 2
    for lo, base, c in ((0, base_own, cot_own), (half, base_pair, cot_pair)):
        rows_at = slice(lo, lo + half)
        rows = base[...].astype(F32) + (
            add_l[rows_at, :].astype(F32) + add_r[rows_at, :].astype(F32)
        )
        hat, _ = statistics(rows)
        normed[rows_at, :] = (hat * gain[...]).astype(LOW)
        cot[rows_at, :] = c[...]
    for c in range(chunks):
        group, side = c % 2, c // 2
        ups, downs, up_grads, down_grads = [], [], [], []
        for p in range(pieces):
            k = side * pieces + p
            if packed:
                w, g = weights[c * pieces + p], grads[k]
                wide = w.shape[0] // 2
                ups.append(w[:wide, :])
                downs.append(w[wide:, :])
                up_grads.append(g.at[group, :wide, :])
                down_grads.append(g.at[group, wide:, :])
            else:
                ups.append(weights[2 * (c * pieces + p)][...])
                downs.append(weights[2 * (c * pieces + p) + 1][...])
                up_grads.append(grads[2 * k].at[group])
                down_grads.append(grads[2 * k + 1].at[group])
        width = ups[0].shape[0]
        hidden = dact = None
        for p in range(pieces):
            cols = columns(off, p, width)
            term = dot(normed[:, cols], ups[p], 1, 0)
            dterm = dot(cot[:, cols], downs[p], 1, 1)
            hidden = term if hidden is None else hidden + term
            dact = dterm if dact is None else dact + dterm
        cdf = 0.5 * (1.0 + lax.erf(hidden * (2.0**-0.5)))
        act = (hidden * cdf).astype(LOW)
        slope = cdf + hidden * (jnp.exp(-0.5 * hidden * hidden) * (2.0 * jnp.pi) ** -0.5)
        dhid = (dact * slope).astype(LOW)
        for p in range(pieces):
            cols = columns(off, p, width)
            term = dot(act, downs[p], 1, 0)
            dterm = dot(dhid, ups[p], 1, 1)
            if c == 0:
                total[:, cols] = term
                dtotal[:, cols] = dterm
            else:
                total[:, cols] += term
                dtotal[:, cols] += dterm
            up_grads[p][...] = dot(normed[:, cols], dhid, 0, 0).astype(LOW)
            down_grads[p][...] = dot(act, cot[:, cols], 0, 0).astype(LOW)
    out_part[...] = total[...].astype(LOW)
    dn_part[...] = dtotal[...].astype(LOW)


def norm_back_kernel(part, received, base, gain, carried, out, gain_grad):
    hat, rate = statistics(base[...].astype(F32))
    dn = part[: base.shape[0], :].astype(F32) + received[...].astype(F32)
    out[...] = (carried[...].astype(F32) + norm_back(dn, gain[...], hat, rate)).astype(out.dtype)
    gain_grad[...] = jnp.sum(dn * hat, axis=0, keepdims=True)


def in_vmem(n):
    return [pl.BlockSpec(memory_space=VMEM)] * n


def shape_of(shape, dtype):
    return jax.ShapeDtypeStruct(shape, dtype)


def run(kernel, operands, outs, scratch, flops, name):
    moved = sum(o.size * o.dtype.itemsize for o in operands) + sum(
        o.size * o.dtype.itemsize for o in outs
    )
    scalar = operands[0].dtype == jnp.int32
    specs = in_vmem(len(operands))
    if scalar:
        specs[0] = pl.BlockSpec(memory_space=pltpu.SMEM)
    return pl.pallas_call(
        kernel,
        out_shape=outs,
        in_specs=specs,
        out_specs=in_vmem(len(outs)),
        scratch_shapes=scratch,
        compiler_params=pltpu.CompilerParams(vmem_limit_bytes=48 << 20),
        cost_estimate=pl.CostEstimate(flops=flops, bytes_accessed=moved, transcendentals=0),
        name=name,
    )(*operands)


def body(sizes, tokens, norm_gains, temporal_qkv, temporal_proj, spatial_qkv, spatial_proj, up_weight, down_weight, cotangent):
    n_fsdp, n_ctx, n_tp = sizes
    swap = n_fsdp == 2
    d_model = tokens.shape[3]
    d_part = d_model // n_fsdp
    places = tokens.shape[0]
    block = 2 * (-(-places // 4))
    x, i, z = lax.axis_index("fsdp"), lax.axis_index("ctx"), lax.axis_index("tp")
    core, chip = i % 2, i // 2
    is_source = (z // 2) == core

    def permute_ctx(v, bits):
        return lax.ppermute(v, "ctx", [(a, a ^ bits) for a in range(n_ctx)])

    def permute_tp(v, bits):
        return lax.ppermute(v, "tp", [(a, a ^ bits) for a in range(n_tp)])

    def permute_fsdp(v):
        return lax.ppermute(v, "fsdp", [(0, 1), (1, 0)])

    outward, inward = [], []
    for a in range(n_ctx):
        for b in (2 * (a % 2), 2 * (a % 2) + 1):
            outward.append((a * n_tp + b, a * n_tp + (b ^ 2)))
            inward.append((a * n_tp + (b ^ 2), a * n_tp + b))

    def exclusive(parts, bits):
        low, high = (bits & 1) == 1, (bits & 2) == 2
        parts = [jnp.where(low, parts[d ^ 1], parts[d]) for d in range(4)]
        return [jnp.where(high, parts[d ^ 2], parts[d]) for d in range(4)]

    slot_bits = (z & 2) | ((z & 1) ^ core)

    def to_time(rows):
        t = jnp.transpose(rows, (2, 1, 0, 3))
        t = jnp.pad(t, ((0, 0), (0, 0), (0, 2 * block - places), (0, 0)))
        parts = [t[c, :, b * block : (b + 1) * block] for c in range(2) for b in range(2)]
        parts = exclusive(parts, i)
        got = [parts[0]] + [permute_ctx(parts[e], e) for e in range(1, 4)]
        return jnp.stack(exclusive(got, slot_bits))

    def from_time(own):
        parts = exclusive([own[d] for d in range(4)], slot_bits)
        got = [parts[0]] + [permute_ctx(parts[e], e) for e in range(1, 4)]
        got = exclusive(got, i)
        t = jnp.stack(
            [jnp.concatenate((got[2 * c], got[2 * c + 1]), axis=1)[:, :places] for c in range(2)]
        )
        return jnp.transpose(t, (2, 1, 0, 3))

    def time_to_space(own):
        got = [own[0]] + [permute_tp(own[e], e) for e in range(1, 4)]
        return jnp.stack(got, axis=1)

    def space_to_time(own):
        got = [own[:, 0]] + [permute_tp(own[:, e], e) for e in range(1, 4)]
        return jnp.stack(got)

    rows_n = 8 * block
    flat = (rows_n, d_model)
    space_shape = (2, 4, block, d_model)
    time_shape = (4, 2, block, d_model)

    def spread(shard):
        got = lax.ppermute(shard, ("ctx", "tp"), outward)
        first = jnp.where(is_source, shard, got)
        return first, permute_tp(first, 1)

    def attention_pack(qkv, proj):
        return jnp.concatenate((qkv.reshape(d_part, -1), proj.T), axis=1)

    def attention_weights(qkv, proj):
        first, second = spread(attention_pack(qkv, proj))
        if swap:
            return [first, permute_fsdp(first), second, permute_fsdp(second)]
        return [lax.all_gather(v, "fsdp", axis=0, tiled=True) for v in (first, second)]

    hid_half = up_weight.shape[1] // 2

    def feed_weights():
        up = lax.dynamic_slice_in_dim(up_weight, chip * hid_half, hid_half, axis=1)
        down = lax.dynamic_slice_in_dim(down_weight, chip * hid_half, hid_half, axis=0)
        first, second = spread(jnp.concatenate((up, down.reshape(d_part, hid_half)), axis=0))
        if swap:
            mine = [first, permute_fsdp(first), second, permute_fsdp(second)]
            return mine + [permute_ctx(v, 2) for v in mine]
        mine = [first, second]
        full = []
        for v in mine + [permute_ctx(v, 2) for v in mine]:
            every = lax.all_gather(v, "fsdp", axis=0)
            full.append(every[:, :d_part].reshape(d_model, hid_half))
            down_all = every[:, d_part:].reshape(n_fsdp, hid_half, d_part)
            full.append(jnp.transpose(down_all, (1, 0, 2)).reshape(hid_half, d_model))
        return full

    def owner_sum(both):
        mine = both[0] + permute_tp(both[1], 1)
        return mine + lax.ppermute(mine, ("ctx", "tp"), inward)

    def to_both(mine):
        other = permute_ctx(mine, 2)
        low = jnp.where(chip == 0, mine, other)
        high = jnp.where(chip == 0, other, mine)
        pair_low, pair_high = permute_ctx(low, 1), permute_ctx(high, 1)
        return jnp.where(is_source, low, pair_low), jnp.where(is_source, high, pair_high)

    def attention_grads(grads):
        if swap:
            total = grads[0] + permute_fsdp(grads[1])
        else:
            total = lax.psum_scatter(grads[0], "fsdp", scatter_dimension=1, tiled=True)
        half = total.shape[2] // 2
        keep = lax.dynamic_slice_in_dim(total, chip * half, half, axis=2)
        send = lax.dynamic_slice_in_dim(total, (1 - chip) * half, half, axis=2)
        low, high = to_both(owner_sum(keep + permute_ctx(send, 2)))
        full = jnp.concatenate((low, high), axis=1).astype(F32)
        inner = 3 * full.shape[1] // 4
        return full[:, :inner].reshape(d_part, 3, inner // 3), full[:, inner:].T

    def feed_grads(grads):
        n = len(grads) // 2
        here = [grads[k] + permute_ctx(grads[n + k], 2) for k in range(n)]
        if swap:
            total = here[0] + permute_fsdp(here[1])
        else:
            up = lax.psum_scatter(here[0], "fsdp", scatter_dimension=1, tiled=True)
            down = lax.psum_scatter(here[1], "fsdp", scatter_dimension=2, tiled=True)
            total = jnp.concatenate((up, down.reshape(2, d_part, hid_half)), axis=1)
        low, high = to_both(owner_sum(total))
        up = jnp.concatenate((low[:d_part], high[:d_part]), axis=1)
        down = jnp.concatenate(
            [v[d_part:].reshape(hid_half, d_part) for v in (low, high)], axis=0
        )
        return up.astype(F32), down.astype(F32)

    pieces = 2 if swap else 1
    width = d_model // pieces
    if swap:
        offsets = jnp.stack((x * width, (1 - x) * width)).astype(jnp.int32)
    else:
        offsets = jnp.zeros((1,), jnp.int32)

    weights_t = attention_weights(temporal_qkv, temporal_proj)
    start = to_time(tokens).reshape(flat)
    start_pair = permute_ctx(start, 1)
    weights_s = attention_weights(spatial_qkv, spatial_proj)
    weights_f = feed_weights()
    gains = lax.all_gather(norm_gains, "fsdp", axis=1, tiled=True).astype(F32)
    cot_own = time_to_space(to_time(cotangent)).reshape(flat)
    cot_pair = permute_ctx(cot_own, 1)

    at = jnp.arange(rows_n, dtype=jnp.int32)
    far = jnp.float32(-1e30)
    bias_t = jnp.where((at % block)[:, None] == (at % block)[None, :], 0.0, far).astype(F32)
    owner = jnp.where(at < rows_n // 2, core, 1 - core)
    real = owner * block + at % block < places
    bias_s = jnp.broadcast_to(jnp.where(real, 0.0, far).astype(F32)[None], (rows_n, rows_n))

    two = (2 * rows_n, d_model)
    joined = (2 * rows_n, 3 * temporal_qkv.shape[2])
    heads = (2 * rows_n, temporal_qkv.shape[2])
    unit = 2 * rows_n * d_model * d_model

    def attend_forward(own, pair, gain, bias, weights, cut, name):
        outs = [
            shape_of(two, LOW),
            shape_of(two, LOW),
            shape_of(joined, LOW),
            shape_of(joined, LOW),
            shape_of(heads, LOW),
            shape_of(heads, LOW),
        ]
        return run(
            functools.partial(attend_forward_kernel, pieces, cut),
            [offsets, own, pair, gain, bias, *weights],
            outs,
            [VMEM(two, F32)],
            6 * unit,
            name,
        )

    def attend_backward(saved, bias, head, weights, cut, name):
        group = (2, width, d_model)
        outs = [shape_of(two, LOW)] + [shape_of(group, LOW)] * pieces
        if cut:
            outs += [shape_of(flat, F32), shape_of((1, d_model), F32)]
        return run(
            functools.partial(attend_backward_kernel, pieces, cut),
            [offsets, bias, *saved, *head, *weights],
            outs,
            [
                VMEM(two, LOW),
                VMEM(joined, LOW),
                VMEM(joined, LOW),
                VMEM(heads, LOW),
                VMEM(heads, LOW),
                VMEM(two, F32),
            ],
            12 * unit,
            name,
        )

    def norm_backward(part, received, base, gain, carried, out_dtype, name):
        return run(
            norm_back_kernel,
            [part, received, base, gain, carried],
            [shape_of(flat, out_dtype), shape_of((1, d_model), F32)],
            [],
            20 * rows_n * d_model,
            name,
        )

    part_t, *saved_t = attend_forward(
        start, start_pair, gains[0:1], bias_t, weights_t, False, "time_forward"
    )
    back = permute_ctx(part_t[rows_n:], 1)
    after_time = (
        start.astype(F32) + part_t[:rows_n].astype(F32) + back.astype(F32)
    ).astype(LOW)
    own1 = time_to_space(after_time.reshape(time_shape)).reshape(flat)
    pair1 = permute_ctx(own1, 1)

    part_s, *saved_s = attend_forward(
        own1, pair1, gains[1:2], bias_s, weights_s, True, "space_forward"
    )
    got_s = permute_ctx(part_s, 1)
    got_s = jnp.concatenate((got_s[rows_n:], got_s[:rows_n]), axis=0)

    n_w = len(weights_f)
    if swap:
        outs_f = [shape_of((2, 2 * width, hid_half), LOW)] * 4
    else:
        outs_f = [shape_of((2, width, hid_half), LOW), shape_of((2, hid_half, width), LOW)] * 2
    if swap:
        ordered = weights_f
    else:
        ordered = weights_f
    out_part, dn3, *grads_f = run(
        functools.partial(feed_kernel, pieces, 4, swap),
        [offsets, own1, pair1, part_s, got_s, gains[2:3], cot_own, cot_pair, *ordered],
        [shape_of(two, LOW), shape_of(two, LOW), *outs_f],
        [VMEM(two, LOW), VMEM(two, LOW), VMEM(two, F32), VMEM(two, F32)],
        24 * unit,
        "feed",
    )
    del n_w
    got3 = permute_ctx(dn3, 1)
    got3 = jnp.concatenate((got3[rows_n:], got3[:rows_n]), axis=0)
    got_out = permute_ctx(out_part[rows_n:], 1)
    after_space = own1.astype(F32) + (
        part_s[:rows_n].astype(F32) + got_s[:rows_n].astype(F32)
    )
    block_own = (after_space + out_part[:rows_n].astype(F32) + got_out.astype(F32)).astype(LOW)
    block_out = from_time(space_to_time(block_own.reshape(space_shape)))

    dn2, *rest = attend_backward(
        saved_s,
        bias_s,
        [own1, pair1, part_s, got_s, dn3, got3, gains[2:3], cot_own, cot_pair, gains[1:2]],
        weights_s,
        True,
        "space_backward",
    )
    grads_s, (carried2, gain3) = rest[:pieces], rest[pieces:]
    got2 = permute_ctx(dn2[rows_n:], 1)
    carried1, gain2 = norm_backward(dn2, got2, own1, gains[1:2], carried2, LOW, "space_norm")
    own_t = space_to_time(carried1.reshape(space_shape)).reshape(flat)
    pair_t = permute_ctx(own_t, 1)

    dn1, *grads_t = attend_backward(
        saved_t, bias_t, [own_t, pair_t], weights_t, False, "time_backward"
    )
    got1 = permute_ctx(dn1[rows_n:], 1)
    carried0, gain1 = norm_backward(dn1, got1, start, gains[0:1], own_t, LOW, "time_norm")
    tokens_grad = from_time(carried0.reshape(time_shape)).astype(F32)

    gain_all = jnp.concatenate((gain1, gain2, gain3), axis=0)
    for bits in (1, 2):
        gain_all = gain_all + permute_ctx(gain_all, bits)
    for bits in (1, 2):
        gain_all = gain_all + permute_tp(gain_all, bits)
    gain_grads = lax.psum_scatter(gain_all, "fsdp", scatter_dimension=1, tiled=True)
    up_grad, down_grad = feed_grads(grads_f)
    s_qkv, s_proj = attention_grads(grads_s)
    t_qkv, t_proj = attention_grads(grads_t)
    return (
        block_out,
        tokens_grad,
        gain_grads,
        t_qkv,
        t_proj,
        s_qkv,
        s_proj,
        up_grad,
        down_grad,
    )


def solution(mesh):
    rows = P("tp", "ctx", "fsdp", None)
    weights = (
        P(None, "fsdp"),
        P("fsdp", None, "tp"),
        P("tp", "fsdp"),
        P("fsdp", None, "tp"),
        P("tp", "fsdp"),
        P("fsdp", "tp"),
        P("tp", "fsdp"),
    )
    sizes = (mesh.shape["fsdp"], mesh.shape["ctx"], mesh.shape["tp"])
    return jax.shard_map(
        functools.partial(body, sizes),
        mesh=mesh,
        in_specs=(rows, *weights, rows),
        out_specs=(rows, rows, *weights),
        check_vma=False,
    )
```

```python
import functools

import jax
import jax.numpy as jnp
from jax import lax
from jax.experimental import pallas as pl
from jax.experimental.pallas import tpu as pltpu
from jax.sharding import PartitionSpec as P

HEAD_DIM = 64
EPSILON = 1e-06
SCALE = HEAD_DIM ** (-0.5)
F32 = jnp.float32
LOW = jnp.bfloat16
VMEM = pltpu.VMEM


def dot(a, b, ca, cb):
    return lax.dot_general(a, b, (((ca,), (cb,)), ((), ())), preferred_element_type=F32)


def statistics(rows):
    center = rows - jnp.mean(rows, axis=-1, keepdims=True)
    rate = lax.rsqrt(jnp.mean(center * center, axis=-1, keepdims=True) + EPSILON)
    return center * rate, rate


def norm_back(grad, gain, hat, rate):
    t = grad * gain
    return rate * (
        t
        - jnp.mean(t, axis=-1, keepdims=True)
        - hat * jnp.mean(t * hat, axis=-1, keepdims=True)
    )


def to_blocks(own, pair, frames_cut):
    if not frames_cut:
        return jnp.concatenate((own, pair), axis=0)
    n = own.shape[0] // 8
    return jnp.concatenate(
        [
            rows[(2 * d + f) * n : (2 * d + f + 1) * n]
            for f in range(2)
            for rows in (own, pair)
            for d in range(4)
        ],
        axis=0,
    )


def from_blocks(rows, frames_cut):
    half = rows.shape[0] // 2
    if not frames_cut:
        return rows[:half], rows[half:]
    n = half // 8
    return tuple(
        jnp.concatenate(
            [
                rows[f * half + (4 * side + d) * n : f * half + (4 * side + d + 1) * n]
                for d in range(4)
                for f in range(2)
            ],
            axis=0,
        )
        for side in range(2)
    )


def split_store(chip, refs, piece, group, units):
    send_x, keep_x, send_y, keep_y = refs
    to_x = keep_x if piece == 0 else send_x
    to_x[0, group] = jnp.where(chip == 0, units[0], units[1])
    to_x[1, group] = jnp.where(chip == 0, units[1], units[0])
    keep_y[piece, group] = jnp.where(chip == 0, units[2], units[3])
    send_y[piece, group] = jnp.where(chip == 0, units[3], units[2])


def columns(off_ref, piece, width):
    return pl.ds(pl.multiple_of(off_ref[piece], 128), width)


def attend_forward_kernel(pieces, frames_cut, *refs):
    off, own, pair, gain, bias = refs[:5]
    weights = refs[5 : 5 + 2 * pieces]
    rest = list(refs[5 + 2 * pieces :])
    parts_out = [rest.pop(0)] if frames_cut else [rest.pop(0), rest.pop(0)]
    normed, joined_a, joined_b, out_a, out_b, total = rest
    rows = to_blocks(own[...].astype(F32), pair[...].astype(F32), frames_cut)
    hat, _ = statistics(rows)
    normed[...] = (hat * gain[...]).astype(LOW)
    width = weights[0].shape[1]
    heads3 = joined_a.shape[1]
    for group, joined in enumerate((joined_a, joined_b)):
        acc = None
        for p in range(pieces):
            w = weights[group * pieces + p]
            term = dot(normed[:, columns(off, p, width)], w[:heads3, :], 1, 1)
            acc = term if acc is None else acc + term
        joined[...] = acc.astype(LOW)
    block = normed.shape[0] // 2
    inner = heads3 // 3

    def one_block(b, carry):
        at = pl.ds(pl.multiple_of(b * block, 16), block)
        for joined, out in ((joined_a, out_a), (joined_b, out_b)):
            rows3 = joined[at, :]
            parts = []
            for h in range(inner // HEAD_DIM):
                lo = h * HEAD_DIM
                q = rows3[:, lo : lo + HEAD_DIM]
                k = rows3[:, inner + lo : inner + lo + HEAD_DIM]
                v = rows3[:, 2 * inner + lo : 2 * inner + lo + HEAD_DIM]
                s = dot(q, k, 1, 1) * SCALE + bias[...]
                e = jnp.exp(s - jnp.max(s, axis=-1, keepdims=True))
                w = (e / jnp.sum(e, axis=-1, keepdims=True)).astype(LOW)
                parts.append(dot(w, v, 1, 0))
            out[at, :] = jnp.concatenate(parts, axis=1).astype(LOW)
        return carry

    lax.fori_loop(0, 2, one_block, 0)
    for p in range(pieces):
        total[:, columns(off, p, width)] = dot(
            out_a[...], weights[p][heads3:, :], 1, 0
        ) + dot(out_b[...], weights[pieces + p][heads3:, :], 1, 0)
    first, second = from_blocks(total[...], frames_cut)
    if frames_cut:
        parts_out[0][...] = jnp.concatenate((first, second), axis=0).astype(LOW)
    else:
        parts_out[0][...] = first.astype(LOW)
        parts_out[1][...] = second.astype(LOW)


def attend_backward_kernel(pieces, frames_cut, *refs):
    n_in = 10 if frames_cut else 2
    off, bias, normed, joined_a, joined_b, out_a, out_b = refs[:7]
    head = refs[7 : 7 + n_in]
    weights = refs[7 + n_in : 7 + n_in + 2 * pieces]
    rest = list(refs[7 + n_in + 2 * pieces :])
    part_own, part_pair = rest.pop(0), rest.pop(0)
    grads = [rest.pop(0) for _ in range(4 if pieces == 2 else 1)]
    if frames_cut:
        carried, gain_grad = rest.pop(0), rest.pop(0)
    upstream, djoined_a, djoined_b, dout_a, dout_b, total = rest
    half = upstream.shape[0] // 2
    if frames_cut:
        base_own, base_pair, add_l, add_r, grad_l, grad_r, gain, cot_own, cot_pair, _ = head
        both = []
        for lo, base, cot in ((0, base_own, cot_own), (half, base_pair, cot_pair)):
            at = slice(lo, lo + half)
            far = slice(half - lo, 2 * half - lo)
            rows = base[...].astype(F32) + (add_l[at, :].astype(F32) + add_r[far, :].astype(F32))
            hat, rate = statistics(rows)
            dn = grad_l[at, :].astype(F32) + grad_r[far, :].astype(F32)
            dx = cot[...].astype(F32) + norm_back(dn, gain[...], hat, rate)
            if lo == 0:
                carried[...] = dx
                gain_grad[...] = jnp.sum(dn * hat, axis=0, keepdims=True)
            both.append(dx)
        upstream[...] = to_blocks(both[0], both[1], frames_cut).astype(LOW)
    else:
        upstream[:half, :] = head[0][...]
        upstream[half:, :] = head[1][...]
    width = weights[0].shape[1]
    heads3 = joined_a.shape[1]
    inner = heads3 // 3
    for group, (out, dout) in enumerate(((out_a, dout_a), (out_b, dout_b))):
        acc = None
        for p in range(pieces):
            w = weights[group * pieces + p]
            dy = upstream[:, columns(off, p, width)]
            term = dot(dy, w[heads3:, :], 1, 1)
            acc = term if acc is None else acc + term
        dout[...] = acc.astype(LOW)

    def one_block(b, carry):
        at = pl.ds(pl.multiple_of(b * half, 16), half)
        for joined, dout, djoined in (
            (joined_a, dout_a, djoined_a),
            (joined_b, dout_b, djoined_b),
        ):
            rows3 = joined[at, :]
            do3 = dout[at, :]
            dqs, dks, dvs = [], [], []
            for h in range(inner // HEAD_DIM):
                lo = h * HEAD_DIM
                q = rows3[:, lo : lo + HEAD_DIM]
                k = rows3[:, inner + lo : inner + lo + HEAD_DIM]
                v = rows3[:, 2 * inner + lo : 2 * inner + lo + HEAD_DIM]
                do = do3[:, lo : lo + HEAD_DIM]
                s = dot(q, k, 1, 1) * SCALE + bias[...]
                e = jnp.exp(s - jnp.max(s, axis=-1, keepdims=True))
                w = e / jnp.sum(e, axis=-1, keepdims=True)
                dw = dot(do, v, 1, 1)
                ds = (w * (dw - jnp.sum(w * dw, axis=-1, keepdims=True))).astype(LOW)
                dqs.append(dot(ds, k, 1, 0) * SCALE)
                dks.append(dot(ds, q, 0, 0) * SCALE)
                dvs.append(dot(w.astype(LOW), do, 0, 0))
            djoined[at, :] = jnp.concatenate(dqs + dks + dvs, axis=1).astype(LOW)
        return carry

    lax.fori_loop(0, 2, one_block, 0)
    chip = off[pieces]
    for p in range(pieces):
        cols = columns(off, p, width)
        wide = normed[:, cols]
        dy = upstream[:, cols]
        for group, (djoined, out) in enumerate(((djoined_a, out_a), (djoined_b, out_b))):
            value = dot(djoined[...], wide, 0, 0).astype(LOW)
            proj = dot(out[...], dy, 0, 0).astype(LOW)
            if pieces == 2:
                units = [value[u * inner : (u + 1) * inner] for u in range(3)] + [proj]
                split_store(chip, grads, p, group, units)
            else:
                grads[0][group, :heads3] = value
                grads[0][group, heads3:] = proj
        total[:, cols] = dot(djoined_a[...], weights[p][:heads3, :], 1, 0) + dot(
            djoined_b[...], weights[pieces + p][:heads3, :], 1, 0
        )
    first, second = from_blocks(total[...], frames_cut)
    part_own[...] = first.astype(LOW)
    part_pair[...] = second.astype(LOW)


def feed_kernel(pieces, chunks, packed, *refs):
    off, base_own, base_pair, add_l, add_r, gain, cot_own, cot_pair = refs[:8]
    at = 8
    n_w = chunks * pieces * (1 if packed else 2)
    weights = refs[at : at + n_w]
    at += n_w
    out_own, out_pair, dn_part = refs[at : at + 3]
    at += 3
    grads = refs[at : at + 4]
    normed, cot, total, dtotal, base_sum = refs[at + 4 :]
    half = normed.shape[0] // 2
    for lo, base, c in ((0, base_own, cot_own), (half, base_pair, cot_pair)):
        rows_at, far = slice(lo, lo + half), slice(half - lo, 2 * half - lo)
        rows = base[...].astype(F32) + (
            add_l[rows_at, :].astype(F32) + add_r[far, :].astype(F32)
        )
        if lo == 0:
            base_sum[...] = rows
        hat, _ = statistics(rows)
        normed[rows_at, :] = (hat * gain[...]).astype(LOW)
        cot[rows_at, :] = c[...]
    for c in range(chunks):
        group, side = c % 2, c // 2
        ups, downs = [], []
        for p in range(pieces):
            if packed:
                w = weights[c * pieces + p]
                wide = w.shape[0] // 2
                ups.append(w[:wide, :])
                downs.append(w[wide:, :])
            else:
                ups.append(weights[2 * (c * pieces + p)][...])
                downs.append(weights[2 * (c * pieces + p) + 1][...])
        width = ups[0].shape[0]
        hidden = dact = None
        for p in range(pieces):
            cols = columns(off, p, width)
            term = dot(normed[:, cols], ups[p], 1, 0)
            dterm = dot(cot[:, cols], downs[p], 1, 1)
            hidden = term if hidden is None else hidden + term
            dact = dterm if dact is None else dact + dterm
        cdf = 0.5 * (1.0 + lax.erf(hidden * (2.0**-0.5)))
        act = (hidden * cdf).astype(LOW)
        slope = cdf + hidden * (jnp.exp(-0.5 * hidden * hidden) * (2.0 * jnp.pi) ** -0.5)
        dhid = (dact * slope).astype(LOW)
        for p in range(pieces):
            cols = columns(off, p, width)
            term = dot(act, downs[p], 1, 0)
            dterm = dot(dhid, ups[p], 1, 1)
            if c == 0:
                total[:, cols] = term
                dtotal[:, cols] = dterm
            else:
                total[:, cols] += term
                dtotal[:, cols] += dterm
            up_grad = dot(normed[:, cols], dhid, 0, 0).astype(LOW)
            down_grad = dot(act, cot[:, cols], 0, 0).astype(LOW)
            if packed:
                send_x, keep_x, send_y, keep_y = grads
                (keep_x if p == 0 else send_x)[side, group] = up_grad
                (keep_y if side == 0 else send_y)[p, group] = down_grad
            else:
                grads[side][group] = up_grad
                grads[2 + side][group] = down_grad
    out_own[...] = base_sum[...] + total[:half, :]
    out_pair[...] = total[half:, :].astype(LOW)
    dn_part[...] = dtotal[...].astype(LOW)


def store_parts(rows, outs):
    n = rows.shape[0] // len(outs)
    for d, out in enumerate(outs):
        out[...] = rows[d * n : (d + 1) * n].astype(out.dtype)


def norm_back_kernel(part, received, base, gain, carried, *outs):
    hat, rate = statistics(base[...].astype(F32))
    dn = part[...].astype(F32) + received[...].astype(F32)
    store_parts(carried[...].astype(F32) + norm_back(dn, gain[...], hat, rate), outs[:4])
    outs[4][...] = jnp.sum(dn * hat, axis=0, keepdims=True)


def sum_kernel(n, *refs):
    total = refs[n - 1][...].astype(F32)
    for k in range(n - 2, -1, -1):
        total = refs[k][...].astype(F32) + total
    store_parts(total, refs[n:])


def in_vmem(n):
    return [pl.BlockSpec(memory_space=VMEM)] * n


def shape_of(shape, dtype):
    return jax.ShapeDtypeStruct(shape, dtype)


def run(kernel, operands, outs, scratch, flops, name):
    moved = sum(o.size * o.dtype.itemsize for o in operands) + sum(
        o.size * o.dtype.itemsize for o in outs
    )
    scalar = operands[0].dtype == jnp.int32
    specs = in_vmem(len(operands))
    if scalar:
        specs[0] = pl.BlockSpec(memory_space=pltpu.SMEM)
    return pl.pallas_call(
        kernel,
        out_shape=outs,
        in_specs=specs,
        out_specs=in_vmem(len(outs)),
        scratch_shapes=scratch,
        compiler_params=pltpu.CompilerParams(vmem_limit_bytes=20 << 20),
        cost_estimate=pl.CostEstimate(flops=flops, bytes_accessed=moved, transcendentals=0),
        name=name,
    )(*operands)


def after(value, *tokens):
    return lax.optimization_barrier((value, *tokens))[0]


def body(sizes, tokens, norm_gains, temporal_qkv, temporal_proj, spatial_qkv, spatial_proj, up_weight, down_weight, cotangent):
    n_fsdp, n_ctx, n_tp = sizes
    swap = n_fsdp == 2
    d_model = tokens.shape[3]
    d_part = d_model // n_fsdp
    places = tokens.shape[0]
    block = 2 * (-(-places // 4))
    x, i, z = lax.axis_index("fsdp"), lax.axis_index("ctx"), lax.axis_index("tp")
    core, chip = i % 2, i // 2
    is_source = (z // 2) == core

    def permute_ctx(v, bits):
        return lax.ppermute(v, "ctx", [(a, a ^ bits) for a in range(n_ctx)])

    def permute_tp(v, bits):
        return lax.ppermute(v, "tp", [(a, a ^ bits) for a in range(n_tp)])

    def permute_fsdp(v):
        return lax.ppermute(v, "fsdp", [(0, 1), (1, 0)])

    outward, inward = [], []
    for a in range(n_ctx):
        for b in (2 * (a % 2), 2 * (a % 2) + 1):
            outward.append((a * n_tp + b, a * n_tp + (b ^ 2)))
            inward.append((a * n_tp + (b ^ 2), a * n_tp + b))

    def exclusive(parts, bits):
        low, high = (bits & 1) == 1, (bits & 2) == 2
        parts = [jnp.where(low, parts[d ^ 1], parts[d]) for d in range(4)]
        return [jnp.where(high, parts[d ^ 2], parts[d]) for d in range(4)]

    slot_bits = (z & 2) | ((z & 1) ^ core)
    part_rows = 2 * block

    def to_time(rows):
        t = jnp.transpose(rows, (2, 1, 0, 3))
        t = jnp.pad(t, ((0, 0), (0, 0), (0, 2 * block - places), (0, 0)))
        parts = [t[c, :, b * block : (b + 1) * block] for c in range(2) for b in range(2)]
        parts = exclusive([v.reshape(part_rows, d_model) for v in parts], i)
        got = [parts[0]] + [permute_ctx(parts[e], e) for e in range(1, 4)]
        return exclusive(got, slot_bits)

    def from_time(own):
        parts = exclusive(own, slot_bits)
        got = [parts[0]] + [permute_ctx(parts[e], e) for e in range(1, 4)]
        got = [v.reshape(2, block, d_model) for v in exclusive(got, i)]
        t = jnp.stack(
            [jnp.concatenate((got[2 * c], got[2 * c + 1]), axis=1)[:, :places] for c in range(2)]
        )
        return jnp.transpose(t, (2, 1, 0, 3))

    def turn(own):
        return [own[0]] + [permute_tp(own[e], e) for e in range(1, 4)]

    rows_n = 8 * block
    flat = (rows_n, d_model)

    def attention_pack(qkv, proj):
        return jnp.concatenate((jnp.transpose(qkv, (1, 2, 0)).reshape(-1, d_part), proj), axis=0)

    def spread_first(shard):
        return jnp.where(is_source, shard, lax.ppermute(shard, ("ctx", "tp"), outward))

    hid_half = up_weight.shape[1] // 2

    def feed_pack():
        up = lax.dynamic_slice_in_dim(up_weight, chip * hid_half, hid_half, axis=1)
        down = lax.dynamic_slice_in_dim(down_weight, chip * hid_half, hid_half, axis=0)
        return jnp.concatenate((up, down.reshape(d_part, hid_half)), axis=0)

    def feed_full(shard):
        every = lax.all_gather(shard, "fsdp", axis=0)
        up = every[:, :d_part].reshape(d_model, hid_half)
        down = every[:, d_part:].reshape(n_fsdp, hid_half, d_part)
        return [up, jnp.transpose(down, (1, 0, 2)).reshape(hid_half, d_model)]

    def owner_sum(a, b):
        mine = a + permute_tp(b, 1)
        return mine + lax.ppermute(mine, ("ctx", "tp"), inward)

    def ordered(mine, other):
        return jnp.stack((jnp.where(chip == 0, mine, other), jnp.where(chip == 0, other, mine)))

    def to_pair(both):
        return jnp.where(is_source, both, permute_ctx(both, 1))

    def to_both(mine):
        return to_pair(ordered(mine, permute_ctx(mine, 2)))

    def first_sends(grads):
        send_x, _, send_y, _ = grads
        return permute_fsdp(send_x), permute_ctx(send_y, 2)

    def first_sums(grads, got):
        _, keep_x, _, keep_y = grads
        by_x, by_y = keep_x + got[0], keep_y + got[1]
        return (by_x[0], by_y[0]), (by_x[1], by_y[1])

    def second_sends(send):
        return permute_ctx(send[0], 2), permute_fsdp(send[1])

    def second_sums(keep, got):
        by_x, by_y = keep[0] + got[0], keep[1] + got[1]
        return jnp.stack((by_x[0], by_y[0])), jnp.stack((by_x[1], by_y[1]))

    def attention_out(total):
        joined_grad = jnp.stack((total[0, 0], total[1, 0], total[0, 1])).astype(F32)
        return jnp.transpose(joined_grad, (2, 0, 1)), total[1, 1].astype(F32)

    def feed_out(total):
        up = jnp.concatenate((total[0, 0], total[1, 0]), axis=1)
        down = jnp.concatenate((total[0, 1], total[1, 1]), axis=0)
        return up.astype(F32), down.astype(F32)

    def attention_grads_wide(grads):
        total = lax.psum_scatter(grads[0], "fsdp", scatter_dimension=2, tiled=True)
        total = total + permute_ctx(total, 2)
        mine = owner_sum(total[0], total[1])
        full = jnp.where(is_source, mine, permute_ctx(mine, 1)).astype(F32)
        inner = full.shape[0] // 4
        joined_grad = full[: 3 * inner].reshape(3, inner, d_part)
        return jnp.transpose(joined_grad, (2, 0, 1)), full[3 * inner :]

    def feed_grads_wide(grads):
        up = grads[0] + permute_ctx(grads[1], 2)
        down = grads[2] + permute_ctx(grads[3], 2)
        up = lax.psum_scatter(up, "fsdp", scatter_dimension=1, tiled=True)
        down = lax.psum_scatter(down, "fsdp", scatter_dimension=2, tiled=True)
        up = to_both(owner_sum(up[0], up[1]))
        down = to_both(owner_sum(down[0], down[1]))
        return (
            jnp.concatenate((up[0], up[1]), axis=1).astype(F32),
            jnp.concatenate((down[0], down[1]), axis=0).astype(F32),
        )

    pieces = 2 if swap else 1
    width = d_model // pieces
    if swap:
        offsets = jnp.stack((x * width, (1 - x) * width, chip)).astype(jnp.int32)
    else:
        offsets = jnp.stack((0 * chip, chip)).astype(jnp.int32)

    at = jnp.arange(rows_n, dtype=jnp.int32)
    far = jnp.float32(-1e30)
    bias_t = jnp.where((at % block)[:, None] == (at % block)[None, :], 0.0, far).astype(F32)
    owner = jnp.where(at < rows_n // 2, core, 1 - core)
    real = owner * block + at % block < places
    bias_s = jnp.broadcast_to(jnp.where(real, 0.0, far).astype(F32)[None], (rows_n, rows_n))

    two = (2 * rows_n, d_model)
    joined = (2 * rows_n, 3 * temporal_qkv.shape[2])
    heads = (2 * rows_n, temporal_qkv.shape[2])
    unit = 2 * rows_n * d_model * d_model

    def attend_forward(own, pair, gain, bias, weights, cut, name):
        parts = [shape_of(two, LOW)] if cut else [shape_of(flat, LOW)] * 2
        outs = parts + [
            shape_of(two, LOW),
            shape_of(joined, LOW),
            shape_of(joined, LOW),
            shape_of(heads, LOW),
            shape_of(heads, LOW),
        ]
        return run(
            functools.partial(attend_forward_kernel, pieces, cut),
            [offsets, own, pair, gain, bias, *weights],
            outs,
            [VMEM(two, F32)],
            6 * unit,
            name,
        )

    def attend_backward(saved, bias, head, weights, cut, name):
        outs = [shape_of(flat, LOW)] * 2
        if swap:
            outs += [shape_of((2, 2, temporal_qkv.shape[2], width), LOW)] * 4
        else:
            outs += [shape_of((2, 4 * temporal_qkv.shape[2], width), LOW)]
        if cut:
            outs += [shape_of(flat, F32), shape_of((1, d_model), F32)]
        got = run(
            functools.partial(attend_backward_kernel, pieces, cut),
            [offsets, bias, *saved, *head, *weights],
            outs,
            [
                VMEM(two, LOW),
                VMEM(joined, LOW),
                VMEM(joined, LOW),
                VMEM(heads, LOW),
                VMEM(heads, LOW),
                VMEM(two, F32),
            ],
            12 * unit,
            name,
        )
        n = 6 if swap else 3
        return got[0], got[1], got[2:n], got[n:]

    def norm_backward(part, received, base, gain, carried, name):
        *parts, gain_grad = run(
            norm_back_kernel,
            [part, received, base, gain, carried],
            [shape_of((part_rows, d_model), LOW)] * 4 + [shape_of((1, d_model), F32)],
            [],
            20 * rows_n * d_model,
            name,
        )
        return parts, gain_grad

    def sum_parts(terms, name):
        return run(
            functools.partial(sum_kernel, len(terms)),
            list(terms),
            [shape_of((part_rows, d_model), LOW)] * 4,
            [],
            4 * rows_n * d_model,
            name,
        )

    def other_x(v):
        return permute_fsdp(v) if swap else lax.all_gather(v, "fsdp", axis=1, tiled=True)

    def joined_pieces(first, first_x, second, second_x):
        return [first, first_x, second, second_x] if swap else [first_x, second_x]

    barrier = lax.optimization_barrier

    pack_t = attention_pack(temporal_qkv, temporal_proj)
    first_t = spread_first(pack_t)
    start = jnp.concatenate(to_time(tokens), axis=0)
    pack_s = attention_pack(spatial_qkv, spatial_proj)
    pack_f = feed_pack()
    if swap:
        gain_other = permute_fsdp(norm_gains)
        gains = jnp.where(
            x == 0,
            jnp.concatenate((norm_gains, gain_other), axis=1),
            jnp.concatenate((gain_other, norm_gains), axis=1),
        ).astype(F32)
    else:
        gains = lax.all_gather(norm_gains, "fsdp", axis=1, tiled=True).astype(F32)
    first_t, start, pack_s, pack_f, cot = barrier((first_t, start, pack_s, pack_f, cotangent))

    second_t = permute_tp(first_t, 1)
    first_tx = other_x(first_t)
    start_pair = permute_ctx(start, 1)
    cot_time = to_time(cot)
    second_t, first_tx, start_pair, pack_s = barrier((second_t, first_tx, start_pair, pack_s))

    second_tx = other_x(second_t)
    first_s = spread_first(pack_s)
    first_f = spread_first(after(pack_f, second_t))
    second_tx, first_s = barrier((second_tx, first_s))

    second_s = permute_tp(first_s, 1)
    first_sx = other_x(first_s)
    weights_t = joined_pieces(first_t, first_tx, second_t, second_tx)
    part_t, pair_part_t, *saved_t = attend_forward(
        start, start_pair, gains[0:1], bias_t, weights_t, False, "time_forward"
    )
    back_t = permute_ctx(pair_part_t, 1)
    sums = sum_parts((start, part_t, back_t), "time_sum")
    sums, second_s, first_sx, first_f, cot_time = barrier((sums, second_s, first_sx, first_f, cot_time))
    second_sx = other_x(second_s)
    own1 = jnp.concatenate(turn(sums), axis=0)
    if swap:
        first_fy = permute_ctx(first_f, 2)
        own1, second_sx, first_f = barrier((own1, second_sx, first_f))
        first_fx = permute_fsdp(first_f)
    pair1 = permute_ctx(own1, 1)
    second_f = permute_tp(first_f, 1)
    weights_s = joined_pieces(first_s, first_sx, second_s, second_sx)

    part_s, *saved_s = attend_forward(
        own1, pair1, gains[1:2], bias_s, weights_s, True, "space_forward"
    )
    got_s = permute_ctx(part_s, 1)
    if swap:
        got_s, second_f, first_fx, first_fy, cot_time = barrier(
            (got_s, second_f, first_fx, first_fy, cot_time)
        )
        second_fx = permute_fsdp(second_f)
        second_fy = permute_ctx(second_f, 2)
        first_fxy = permute_ctx(first_fx, 2)
        cot_own = jnp.concatenate(turn(cot_time), axis=0)
        cot_pair = permute_ctx(cot_own, 1)
        second_fx, second_fy, cot_pair = barrier((second_fx, second_fy, cot_pair))
        second_fxy = permute_fsdp(second_fy)
        weights_f = [
            first_f,
            first_fx,
            second_f,
            second_fx,
            first_fy,
            first_fxy,
            second_fy,
            second_fxy,
        ]
    else:
        cot_own = jnp.concatenate(turn(cot_time), axis=0)
        cot_pair = permute_ctx(cot_own, 1)
        both_f = (first_f, second_f)
        weights_f = [
            w for v in both_f + tuple(permute_ctx(v, 2) for v in both_f) for w in feed_full(v)
        ]

    if swap:
        outs_f = [shape_of((2, 2, width, hid_half), LOW)] * 4
    else:
        outs_f = [shape_of((2, width, hid_half), LOW)] * 2 + [shape_of((2, hid_half, width), LOW)] * 2
    out_own, out_pair, dn3, *grads_f = run(
        functools.partial(feed_kernel, pieces, 4, swap),
        [offsets, own1, pair1, part_s, got_s, gains[2:3], cot_own, cot_pair, *weights_f],
        [shape_of(flat, F32), shape_of(flat, LOW), shape_of(two, LOW), *outs_f],
        [VMEM(two, LOW), VMEM(two, LOW), VMEM(two, F32), VMEM(two, F32), VMEM(flat, F32)],
        24 * unit,
        "feed",
    )
    got3 = permute_ctx(dn3, 1)
    if swap:
        got_f = first_sends(grads_f)

    dn2, pair_dn2, grads_s, (carried2, gain3) = attend_backward(
        saved_s,
        bias_s,
        [own1, pair1, part_s, got_s, dn3, got3, gains[2:3], cot_own, cot_pair, gains[1:2]],
        weights_s,
        True,
        "space_backward",
    )
    got2 = permute_ctx(pair_dn2, 1)
    parts1, gain2 = norm_backward(dn2, got2, own1, gains[1:2], carried2, "space_norm")
    own_t = jnp.concatenate(turn(parts1), axis=0)
    pair_t = permute_ctx(own_t, 1)
    if swap:
        got_sums_s = first_sends(grads_s)
        own_t, got_f = barrier((own_t, got_f))
        keep_f, send_f = first_sums(grads_f, got_f)
        send_f, own_t, pair_t = barrier((send_f, own_t, pair_t))
        got_f = second_sends(send_f)

    dn1, pair_dn1, grads_t, _ = attend_backward(
        saved_t, bias_t, [own_t, pair_t], weights_t, False, "time_backward"
    )
    if swap:
        grads_t, pair_dn1, got_sums_s, out_pair, gain2 = barrier(
            (grads_t, pair_dn1, got_sums_s, out_pair, gain2)
        )
        got_sums_t = first_sends(grads_t)
    got1 = permute_ctx(pair_dn1, 1)
    parts0, gain1 = norm_backward(dn1, got1, start, gains[0:1], own_t, "time_norm")
    gain_all = jnp.concatenate((gain1, gain2, gain3), axis=0)
    got_out = permute_ctx(out_pair, 1)
    if swap:
        gain_all = gain_all + permute_ctx(gain_all, 1)
        a_f, b_f = second_sums(keep_f, got_f)
        add_f = permute_tp(b_f, 1)
        keep_s, send_s = first_sums(grads_s, got_sums_s)
        got_sums_t, parts0, send_s, gain_all, got_out = barrier(
            (got_sums_t, parts0, send_s, gain_all, got_out)
        )
        keep_t, send_t = first_sums(grads_t, got_sums_t)
        got_sums_t = second_sends(send_t)
        gain_all = gain_all + permute_ctx(gain_all, 2)
        out_parts = sum_parts((out_own, got_out), "feed_sum")
        got_sums_t, send_s, add_f, gain_all, out_parts = barrier(
            (got_sums_t, send_s, add_f, gain_all, out_parts)
        )
        a_t, b_t = second_sums(keep_t, got_sums_t)
        add_t = permute_tp(b_t, 1)
        got_sums_s = second_sends(send_s)
        a_f = a_f + add_f
        add_f = lax.ppermute(a_f, ("ctx", "tp"), inward)
        gain_all = gain_all + permute_tp(gain_all, 1)
        add_t, got_sums_s, parts0, out_parts, gain_all = barrier(
            (add_t, got_sums_s, parts0, out_parts, gain_all)
        )
        a_t = a_t + add_t
        add_t = lax.ppermute(a_t, ("ctx", "tp"), inward)
        a_s, b_s = second_sums(keep_s, got_sums_s)
        add_s = permute_tp(b_s, 1)
        tokens_grad = from_time(parts0).astype(F32)
        add_t, add_s, add_f, out_parts, gain_all, tokens_grad = barrier(
            (add_t, add_s, add_f, out_parts, gain_all, tokens_grad)
        )
        total_t = a_t + add_t
        other_t = permute_ctx(total_t, 2)
        a_s = a_s + add_s
        add_s = lax.ppermute(a_s, ("ctx", "tp"), inward)
        total_f = a_f + add_f
        other_f = permute_ctx(total_f, 2)
        out_time = turn(out_parts)
        other_t, other_f, add_s, out_time, gain_all = barrier(
            (other_t, other_f, add_s, out_time, gain_all)
        )
        total_s = a_s + add_s
        other_s = permute_ctx(total_s, 2)
        t_qkv, t_proj = attention_out(to_pair(ordered(total_t, other_t)))
        up_grad, down_grad = feed_out(to_pair(ordered(total_f, other_f)))
        gain_all = gain_all + permute_tp(gain_all, 2)
        block_out = from_time(out_time)
        s_qkv, s_proj = attention_out(to_pair(ordered(total_s, other_s)))
        keep = lax.dynamic_slice_in_dim(gain_all, x * d_part, d_part, axis=1)
        send = lax.dynamic_slice_in_dim(gain_all, (1 - x) * d_part, d_part, axis=1)
        gain_grads = keep + permute_fsdp(send)
    else:
        tokens_grad = from_time(parts0).astype(F32)
        block_out = from_time(turn(sum_parts((out_own, got_out), "feed_sum")))
        up_grad, down_grad = feed_grads_wide(grads_f)
        s_qkv, s_proj = attention_grads_wide(grads_s)
        t_qkv, t_proj = attention_grads_wide(grads_t)
        for bits in (1, 2):
            gain_all = gain_all + permute_ctx(gain_all, bits)
        for bits in (1, 2):
            gain_all = gain_all + permute_tp(gain_all, bits)
        gain_grads = lax.psum_scatter(gain_all, "fsdp", scatter_dimension=1, tiled=True)
    return (
        block_out,
        tokens_grad,
        gain_grads,
        t_qkv,
        t_proj,
        s_qkv,
        s_proj,
        up_grad,
        down_grad,
    )


def solution(mesh):
    rows = P("tp", "ctx", "fsdp", None)
    weights = (
        P(None, "fsdp"),
        P("fsdp", None, "tp"),
        P("tp", "fsdp"),
        P("fsdp", None, "tp"),
        P("tp", "fsdp"),
        P("fsdp", "tp"),
        P("tp", "fsdp"),
    )
    sizes = (mesh.shape["fsdp"], mesh.shape["ctx"], mesh.shape["tp"])
    return jax.shard_map(
        functools.partial(body, sizes),
        mesh=mesh,
        in_specs=(rows, *weights, rows),
        out_specs=(rows, rows, *weights),
        check_vma=False,
    )
```

```python
import functools

import jax
import jax.numpy as jnp
from jax import lax
from jax.experimental import pallas as pl
from jax.experimental.pallas import tpu as pltpu
from jax.sharding import PartitionSpec as P

HEAD_DIM = 64
EPSILON = 1e-06
SCALE = HEAD_DIM ** (-0.5)
F32 = jnp.float32
LOW = jnp.bfloat16
VMEM = pltpu.VMEM


def dot(a, b, ca, cb):
    return lax.dot_general(a, b, (((ca,), (cb,)), ((), ())), preferred_element_type=F32)


def statistics(rows):
    center = rows - jnp.mean(rows, axis=-1, keepdims=True)
    rate = lax.rsqrt(jnp.mean(center * center, axis=-1, keepdims=True) + EPSILON)
    return center * rate, rate


def norm_back(grad, gain, hat, rate):
    t = grad * gain
    return rate * (
        t
        - jnp.mean(t, axis=-1, keepdims=True)
        - hat * jnp.mean(t * hat, axis=-1, keepdims=True)
    )


def to_blocks(own, pair, frames_cut):
    if not frames_cut:
        return jnp.concatenate((own, pair), axis=0)
    n = own.shape[0] // 8
    return jnp.concatenate(
        [
            rows[(2 * d + f) * n : (2 * d + f + 1) * n]
            for f in range(2)
            for rows in (own, pair)
            for d in range(4)
        ],
        axis=0,
    )


def from_blocks(rows, frames_cut):
    half = rows.shape[0] // 2
    if not frames_cut:
        return rows[:half], rows[half:]
    n = half // 8
    return tuple(
        jnp.concatenate(
            [
                rows[f * half + (4 * side + d) * n : f * half + (4 * side + d + 1) * n]
                for d in range(4)
                for f in range(2)
            ],
            axis=0,
        )
        for side in range(2)
    )


def split_store(chip, refs, piece, group, units):
    send_x, keep_x, send_y, keep_y = refs
    to_x = keep_x if piece == 0 else send_x
    to_x[0, group] = jnp.where(chip == 0, units[0], units[1])
    to_x[1, group] = jnp.where(chip == 0, units[1], units[0])
    keep_y[piece, group] = jnp.where(chip == 0, units[2], units[3])
    send_y[piece, group] = jnp.where(chip == 0, units[3], units[2])


def columns(off_ref, piece, width):
    return pl.ds(pl.multiple_of(off_ref[piece], 128), width)


def store_partial(total, outs, frames_cut):
    n, halves = total.shape[0], len(outs) - 1
    first, second = from_blocks(total[: n // halves, :], frames_cut)
    outs[0][...] = first.astype(LOW)
    if halves == 1:
        outs[1][...] = second.astype(LOW)
        return
    half = n // 4
    outs[2][:half, :] = second.astype(LOW)
    first, second = from_blocks(total[n // 2 :, :], frames_cut)
    outs[1][...] = first.astype(LOW)
    outs[2][half:, :] = second.astype(LOW)


def attend_forward_kernel(pieces, halves, groups, frames_cut, *refs):
    off = refs[0]
    rows_in = refs[1 : 1 + 2 * halves]
    rest = list(refs[1 + 2 * halves :])
    gain, bias = rest.pop(0), rest.pop(0)
    weights = [[rest.pop(0) for _ in range(pieces)] for _ in range(groups)]
    parts_out = [rest.pop(0) for _ in range(1 + halves)]
    saved_at = [rest.pop(0) for _ in range(1 + 2 * groups)]
    kept_at = [rest.pop(0) for _ in range(groups * pieces)]
    normed = rest.pop(0)
    joined, out = [rest.pop(0) for _ in range(groups)], [rest.pop(0) for _ in range(groups)]
    total, sems = rest
    copies = []

    def leave(source, target):
        copy = pltpu.make_async_copy(source, target, sems.at[len(copies)])
        copy.start()
        copies.append(copy)

    for g in range(groups):
        for p in range(pieces):
            leave(weights[g][p], kept_at[g * pieces + p])
    two = normed.shape[0] // halves
    for h in range(halves):
        rows = to_blocks(
            rows_in[2 * h][...].astype(F32), rows_in[2 * h + 1][...].astype(F32), frames_cut
        )
        hat, _ = statistics(rows)
        normed[h * two : (h + 1) * two, :] = (hat * gain[...]).astype(LOW)
    leave(normed, saved_at[0])
    width = weights[0][0].shape[1]
    heads3 = joined[0].shape[1]
    for g in range(groups):
        acc = None
        for p in range(pieces):
            term = dot(normed[:, columns(off, p, width)], weights[g][p][:heads3, :], 1, 1)
            acc = term if acc is None else acc + term
        joined[g][...] = acc.astype(LOW)
        leave(joined[g], saved_at[1 + g])
    block = two // 2
    inner = heads3 // 3

    def one_block(b, carry):
        at = pl.ds(pl.multiple_of(b * block, 16), block)
        for g in range(groups):
            rows3 = joined[g][at, :]
            parts = []
            for h in range(inner // HEAD_DIM):
                lo = h * HEAD_DIM
                q = rows3[:, lo : lo + HEAD_DIM]
                k = rows3[:, inner + lo : inner + lo + HEAD_DIM]
                v = rows3[:, 2 * inner + lo : 2 * inner + lo + HEAD_DIM]
                s = dot(q, k, 1, 1) * SCALE + bias[...]
                e = jnp.exp(s - jnp.max(s, axis=-1, keepdims=True))
                w = (e / jnp.sum(e, axis=-1, keepdims=True)).astype(LOW)
                parts.append(dot(w, v, 1, 0))
            out[g][at, :] = jnp.concatenate(parts, axis=1).astype(LOW)
        return carry

    lax.fori_loop(0, 2 * halves, one_block, 0)
    for g in range(groups):
        leave(out[g], saved_at[1 + groups + g])
    for p in range(pieces):
        acc = dot(out[0][...], weights[0][p][heads3:, :], 1, 0)
        for g in range(1, groups):
            acc = acc + dot(out[g][...], weights[g][p][heads3:, :], 1, 0)
        total[:, columns(off, p, width)] = acc
    store_partial(total, parts_out, frames_cut)
    for copy in copies:
        copy.wait()


def attend_backward_kernel(pieces, halves, groups, frames_cut, *refs):
    off, bias, normed = refs[:3]
    rest = list(refs[3:])
    joined, out = [rest.pop(0) for _ in range(groups)], [rest.pop(0) for _ in range(groups)]
    n_head = 9 if frames_cut else 2 * halves
    head = [rest.pop(0) for _ in range(n_head)]
    weights = [[rest.pop(0) for _ in range(pieces)] for _ in range(groups)]
    parts_out = [rest.pop(0) for _ in range(1 + halves)]
    grads = [rest.pop(0) for _ in range(4 if pieces == 2 else 1)]
    if frames_cut:
        carried, gain_grad = rest.pop(0), rest.pop(0)
    upstream = rest.pop(0)
    djoined, dout = [rest.pop(0) for _ in range(groups)], [rest.pop(0) for _ in range(groups)]
    total = rest.pop(0)
    two = upstream.shape[0] // halves
    half = two // 2
    if frames_cut:
        base_own, base_pair, grad_l, grad_r, far_own, far_pair, gain, cot_own, cot_pair = head
        both = []
        for lo, base, far_sum, cot in (
            (0, base_own, far_own, cot_own),
            (half, base_pair, far_pair, cot_pair),
        ):
            at = slice(lo, lo + half)
            far = slice(half - lo, 2 * half - lo)
            hat, rate = statistics(base[...].astype(F32))
            dn = grad_l[at, :].astype(F32) + grad_r[far, :].astype(F32) + far_sum[...].astype(F32)
            dx = cot[...].astype(F32) + norm_back(dn, gain[...], hat, rate)
            if lo == 0:
                carried[...] = dx
                gain_grad[...] = jnp.sum(dn * hat, axis=0, keepdims=True)
            both.append(dx)
        upstream[...] = to_blocks(both[0], both[1], frames_cut).astype(LOW)
    else:
        for r in range(2 * halves):
            upstream[r * half : (r + 1) * half, :] = head[r][...]
    width = weights[0][0].shape[1]
    heads3 = joined[0].shape[1]
    inner = heads3 // 3
    for g in range(groups):
        acc = None
        for p in range(pieces):
            term = dot(upstream[:, columns(off, p, width)], weights[g][p][heads3:, :], 1, 1)
            acc = term if acc is None else acc + term
        dout[g][...] = acc.astype(LOW)

    def one_block(b, carry):
        at = pl.ds(pl.multiple_of(b * half, 16), half)
        for g in range(groups):
            rows3 = joined[g][at, :]
            do3 = dout[g][at, :]
            dqs, dks, dvs = [], [], []
            for h in range(inner // HEAD_DIM):
                lo = h * HEAD_DIM
                q = rows3[:, lo : lo + HEAD_DIM]
                k = rows3[:, inner + lo : inner + lo + HEAD_DIM]
                v = rows3[:, 2 * inner + lo : 2 * inner + lo + HEAD_DIM]
                do = do3[:, lo : lo + HEAD_DIM]
                s = dot(q, k, 1, 1) * SCALE + bias[...]
                e = jnp.exp(s - jnp.max(s, axis=-1, keepdims=True))
                w = e / jnp.sum(e, axis=-1, keepdims=True)
                dw = dot(do, v, 1, 1)
                ds = (w * (dw - jnp.sum(w * dw, axis=-1, keepdims=True))).astype(LOW)
                dqs.append(dot(ds, k, 1, 0) * SCALE)
                dks.append(dot(ds, q, 0, 0) * SCALE)
                dvs.append(dot(w.astype(LOW), do, 0, 0))
            djoined[g][at, :] = jnp.concatenate(dqs + dks + dvs, axis=1).astype(LOW)
        return carry

    lax.fori_loop(0, 2 * halves, one_block, 0)
    chip = off[pieces]
    for p in range(pieces):
        cols = columns(off, p, width)
        wide = normed[:, cols]
        dy = upstream[:, cols]
        acc = None
        for g in range(groups):
            value = dot(djoined[g][...], wide, 0, 0).astype(LOW)
            proj = dot(out[g][...], dy, 0, 0).astype(LOW)
            if pieces == 2:
                units = [value[u * inner : (u + 1) * inner] for u in range(3)] + [proj]
                split_store(chip, grads, p, g, units)
            else:
                grads[0][g, :heads3] = value
                grads[0][g, heads3:] = proj
            term = dot(djoined[g][...], weights[g][p][:heads3, :], 1, 0)
            acc = term if acc is None else acc + term
        total[:, cols] = acc
    store_partial(total, parts_out, frames_cut)


def feed_kernel(pieces, packed, *refs):
    off, gain = refs[:2]
    rows_in, cots = refs[2:6], refs[6:10]
    at = 10
    n_w = 2 * pieces * (1 if packed else 2)
    weights = refs[at : at + n_w]
    at += n_w
    out_own, out_send, out_far, dn_near, dn_send, dn_far = refs[at : at + 6]
    at += 6
    n_g = 4 if packed else 2
    grads = refs[at : at + n_g]
    normed, cot, total, dtotal = refs[at + n_g :]
    n = rows_in[0].shape[0]
    for r in range(4):
        rows_at = slice(r * n, (r + 1) * n)
        hat, _ = statistics(rows_in[r][...].astype(F32))
        normed[rows_at, :] = (hat * gain[...]).astype(LOW)
        cot[rows_at, :] = cots[r][...]
    for c in range(2):
        ups, downs = [], []
        for p in range(pieces):
            if packed:
                w = weights[c * pieces + p]
                wide = w.shape[0] // 2
                ups.append(w[:wide, :])
                downs.append(w[wide:, :])
            else:
                ups.append(weights[2 * (c * pieces + p)][...])
                downs.append(weights[2 * (c * pieces + p) + 1][...])
        width = ups[0].shape[0]
        hidden = dact = None
        for p in range(pieces):
            cols = columns(off, p, width)
            term = dot(normed[:, cols], ups[p], 1, 0)
            dterm = dot(cot[:, cols], downs[p], 1, 1)
            hidden = term if hidden is None else hidden + term
            dact = dterm if dact is None else dact + dterm
        cdf = 0.5 * (1.0 + lax.erf(hidden * (2.0**-0.5)))
        act = (hidden * cdf).astype(LOW)
        slope = cdf + hidden * (jnp.exp(-0.5 * hidden * hidden) * (2.0 * jnp.pi) ** -0.5)
        dhid = (dact * slope).astype(LOW)
        for p in range(pieces):
            cols = columns(off, p, width)
            term = dot(act, downs[p], 1, 0)
            dterm = dot(dhid, ups[p], 1, 1)
            if c == 0:
                total[:, cols] = term
                dtotal[:, cols] = dterm
            else:
                total[:, cols] += term
                dtotal[:, cols] += dterm
            up_grad = dot(normed[:, cols], dhid, 0, 0).astype(LOW)
            down_grad = dot(act, cot[:, cols], 0, 0).astype(LOW)
            if packed:
                grads[2 * p + c][:width, :] = up_grad
                grads[2 * p + c][width:, :] = down_grad
            else:
                grads[0][c] = up_grad
                grads[1][c] = down_grad
    out_own[...] = rows_in[0][...].astype(F32) + total[:n, :]
    out_send[:n, :] = total[n : 2 * n, :].astype(LOW)
    out_send[n:, :] = total[3 * n :, :].astype(LOW)
    out_far[...] = total[2 * n : 3 * n, :].astype(LOW)
    dn_near[...] = dtotal[: 2 * n, :].astype(LOW)
    dn_far[...] = dtotal[2 * n : 3 * n, :].astype(LOW)
    dn_send[...] = dtotal[3 * n :, :].astype(LOW)


def store_parts(rows, outs):
    n = rows.shape[0] // len(outs)
    for d, out in enumerate(outs):
        out[...] = rows[d * n : (d + 1) * n].astype(out.dtype)


def norm_back_kernel(n, firsts, *refs):
    base, gain, carried = refs[n : n + 3]
    outs = refs[n + 3 :]
    rows = base.shape[0]
    hat, rate = statistics(base[...].astype(F32))
    dn = refs[n - 1][firsts[n - 1] : firsts[n - 1] + rows, :].astype(F32)
    for k in range(n - 2, -1, -1):
        dn = refs[k][firsts[k] : firsts[k] + rows, :].astype(F32) + dn
    store_parts(carried[...].astype(F32) + norm_back(dn, gain[...], hat, rate), outs[:-1])
    outs[-1][...] = jnp.sum(dn * hat, axis=0, keepdims=True)


def sum_kernel(n, firsts, *refs):
    outs = refs[n:]
    rows = outs[0].shape[0] * len(outs)
    total = refs[n - 1][firsts[n - 1] : firsts[n - 1] + rows, :].astype(F32)
    for k in range(n - 2, -1, -1):
        total = refs[k][firsts[k] : firsts[k] + rows, :].astype(F32) + total
    store_parts(total, outs)


def in_vmem(n):
    return [pl.BlockSpec(memory_space=VMEM)] * n


def shape_of(shape, dtype):
    return jax.ShapeDtypeStruct(shape, dtype)


def run(kernel, operands, outs, scratch, flops, name, vmem=12, anywhere=0):
    moved = sum(o.size * o.dtype.itemsize for o in operands) + sum(
        o.size * o.dtype.itemsize for o in outs
    )
    scalar = operands[0].dtype == jnp.int32
    specs = in_vmem(len(operands))
    if scalar:
        specs[0] = pl.BlockSpec(memory_space=pltpu.SMEM)
    return pl.pallas_call(
        kernel,
        out_shape=outs,
        in_specs=specs,
        out_specs=in_vmem(len(outs) - anywhere)
        + [pl.BlockSpec(memory_space=pl.ANY)] * anywhere,
        scratch_shapes=scratch,
        compiler_params=pltpu.CompilerParams(vmem_limit_bytes=vmem << 20),
        cost_estimate=pl.CostEstimate(flops=flops, bytes_accessed=moved, transcendentals=0),
        name=name,
    )(*operands)


def after(value, *tokens):
    return lax.optimization_barrier((value, *tokens))[0]


def body(sizes, tokens, norm_gains, temporal_qkv, temporal_proj, spatial_qkv, spatial_proj, up_weight, down_weight, cotangent):
    n_fsdp, n_ctx, n_tp = sizes
    swap = n_fsdp == 2
    d_model = tokens.shape[3]
    d_part = d_model // n_fsdp
    places = tokens.shape[0]
    block = 2 * (-(-places // 4))
    x, i, z = lax.axis_index("fsdp"), lax.axis_index("ctx"), lax.axis_index("tp")
    core, chip = i % 2, i // 2
    is_source = (z // 2) == core

    def permute_ctx(v, bits):
        return lax.ppermute(v, "ctx", [(a, a ^ bits) for a in range(n_ctx)])

    def permute_tp(v, bits):
        return lax.ppermute(v, "tp", [(a, a ^ bits) for a in range(n_tp)])

    def permute_fsdp(v):
        return lax.ppermute(v, "fsdp", [(0, 1), (1, 0)])

    def along(v, bits, back=False):
        pairs = []
        for a in range(n_ctx):
            for b in (2 * (a % 2), 2 * (a % 2) + 1):
                there, here = a * n_tp + (b ^ bits), a * n_tp + b
                pairs.append((there, here) if back else (here, there))
        return lax.ppermute(v, ("ctx", "tp"), pairs)

    def exclusive(parts, bits):
        low, high = (bits & 1) == 1, (bits & 2) == 2
        parts = [jnp.where(low, parts[d ^ 1], parts[d]) for d in range(4)]
        return [jnp.where(high, parts[d ^ 2], parts[d]) for d in range(4)]

    slot_bits = (z & 2) | ((z & 1) ^ core)
    part_rows = 2 * block

    def to_time(rows):
        t = jnp.transpose(rows, (2, 1, 0, 3))
        t = jnp.pad(t, ((0, 0), (0, 0), (0, 2 * block - places), (0, 0)))
        parts = [t[c, :, b * block : (b + 1) * block] for c in range(2) for b in range(2)]
        parts = exclusive([v.reshape(part_rows, d_model) for v in parts], i)
        got = [parts[0]] + [permute_ctx(parts[e], e) for e in range(1, 4)]
        return exclusive(got, slot_bits)

    def time_sends(own):
        parts = exclusive(own, slot_bits)
        return [parts[0]] + [permute_ctx(parts[e], e) for e in range(1, 4)]

    def time_finish(got):
        got = [v.reshape(2, block, d_model) for v in exclusive(got, i)]
        t = jnp.stack(
            [jnp.concatenate((got[2 * c], got[2 * c + 1]), axis=1)[:, :places] for c in range(2)]
        )
        return jnp.transpose(t, (2, 1, 0, 3))

    def turn(own):
        return [own[0]] + [permute_tp(own[e], e) for e in range(1, 4)]

    rows_n = 8 * block
    flat = (rows_n, d_model)

    def attention_pack(qkv, proj):
        return jnp.concatenate((jnp.transpose(qkv, (1, 2, 0)).reshape(-1, d_part), proj), axis=0)

    def spread_first(shard):
        return jnp.where(is_source, shard, along(shard, 2))

    hid_half = up_weight.shape[1] // 2

    def feed_pack():
        up = lax.dynamic_slice_in_dim(up_weight, chip * hid_half, hid_half, axis=1)
        down = lax.dynamic_slice_in_dim(down_weight, chip * hid_half, hid_half, axis=0)
        return jnp.concatenate((up, down.reshape(d_part, hid_half)), axis=0)

    def feed_full(shard):
        every = lax.all_gather(shard, "fsdp", axis=0)
        up = every[:, :d_part].reshape(d_model, hid_half)
        down = every[:, d_part:].reshape(n_fsdp, hid_half, d_part)
        return [up, jnp.transpose(down, (1, 0, 2)).reshape(hid_half, d_model)]

    def owner_sum(a, b):
        mine = a + permute_tp(b, 1)
        return mine + along(mine, 2, True)

    def owner_sends(a, b):
        return along(a, 2, True), along(b, 3, True), along(b, 1)

    def ordered(mine, other):
        return jnp.stack((jnp.where(chip == 0, mine, other), jnp.where(chip == 0, other, mine)))

    def to_pair(both):
        return jnp.where(is_source, both, permute_ctx(both, 1))

    def to_both(mine):
        return to_pair(ordered(mine, permute_ctx(mine, 2)))

    def first_sends(grads):
        send_x, _, send_y, _ = grads
        return permute_fsdp(send_x), permute_ctx(send_y, 2)

    def first_sums(grads, got):
        _, keep_x, _, keep_y = grads
        by_x, by_y = keep_x + got[0], keep_y + got[1]
        return (by_x[0], by_y[0]), (by_x[1], by_y[1])

    def second_sends(send):
        return permute_ctx(send[0], 2), permute_fsdp(send[1])

    def second_sums(keep, got):
        by_x, by_y = keep[0] + got[0], keep[1] + got[1]
        return [jnp.stack((by_x[g], by_y[g])) for g in range(by_x.shape[0])]

    def attention_out(total):
        joined_grad = jnp.stack((total[0, 0], total[1, 0], total[0, 1])).astype(F32)
        return jnp.transpose(joined_grad, (2, 0, 1)), total[1, 1].astype(F32)

    def feed_out(total):
        up = jnp.concatenate((total[0, :d_part], total[1, :d_part]), axis=1)
        down = jnp.concatenate((total[0, d_part:], total[1, d_part:]), axis=0)
        return up.astype(F32), down.astype(F32)

    def attention_grads_wide(grads):
        total = lax.psum_scatter(grads[0], "fsdp", scatter_dimension=2, tiled=True)
        total = total + permute_ctx(total, 2)
        if total.shape[0] == 2:
            mine = owner_sum(total[0], total[1])
        else:
            mine = total[0] + along(total[0], 2, True)
        full = jnp.where(is_source, mine, permute_ctx(mine, 1)).astype(F32)
        inner = full.shape[0] // 4
        joined_grad = full[: 3 * inner].reshape(3, inner, d_part)
        return jnp.transpose(joined_grad, (2, 0, 1)), full[3 * inner :]

    def feed_grads_wide(grads):
        up = lax.psum_scatter(grads[0], "fsdp", scatter_dimension=1, tiled=True)
        down = lax.psum_scatter(grads[1], "fsdp", scatter_dimension=2, tiled=True)
        up = to_both(owner_sum(up[0], up[1]))
        down = to_both(owner_sum(down[0], down[1]))
        return (
            jnp.concatenate((up[0], up[1]), axis=1).astype(F32),
            jnp.concatenate((down[0], down[1]), axis=0).astype(F32),
        )

    pieces = 2 if swap else 1
    width = d_model // pieces
    if swap:
        offsets = jnp.stack((x * width, (1 - x) * width, chip)).astype(jnp.int32)
    else:
        offsets = jnp.stack((0 * chip, chip)).astype(jnp.int32)

    at = jnp.arange(rows_n, dtype=jnp.int32)
    far = jnp.float32(-1e30)
    bias_t = jnp.where((at % block)[:, None] == (at % block)[None, :], 0.0, far).astype(F32)
    owner = jnp.where(at < rows_n // 2, core, 1 - core)
    real = owner * block + at % block < places
    bias_s = jnp.broadcast_to(jnp.where(real, 0.0, far).astype(F32)[None], (rows_n, rows_n))

    two = (2 * rows_n, d_model)
    unit = 2 * rows_n * d_model * d_model

    inner = temporal_qkv.shape[2]

    def shapes(rows, groups):
        all_rows = len(rows) * rows_n
        return (all_rows, d_model), [(all_rows, 3 * inner)] * groups, [(all_rows, inner)] * groups

    def part_shapes(rows):
        if len(rows) == 2:
            return [shape_of(flat, LOW)] * 2
        return [shape_of(flat, LOW)] * 2 + [shape_of(two, LOW)]

    def attend_forward(rows, gain, bias, weights, cut, name):
        groups = len(weights) // pieces
        wide, joined, heads = shapes(rows, groups)
        kept = [shape_of(s, LOW) for s in (wide, *joined, *heads)]
        kept += [shape_of(w.shape, LOW) for w in weights]
        outs = part_shapes(rows) + kept
        got = run(
            functools.partial(attend_forward_kernel, pieces, len(rows) // 2, groups, cut),
            [offsets, *rows, gain, bias, *weights],
            outs,
            [VMEM(s, LOW) for s in (wide, *joined, *heads)]
            + [VMEM(wide, F32), pltpu.SemaphoreType.DMA((len(kept),))],
            6 * unit,
            name,
            16,
            len(kept),
        )
        n = len(part_shapes(rows))
        m = n + 1 + 2 * groups
        return got[:n], got[n:m], got[m:]

    def attend_backward(rows, saved, bias, head, weights, cut, name):
        groups = len(weights) // pieces
        wide, joined, heads = shapes(rows, groups)
        outs = part_shapes(rows)
        n = len(outs)
        if swap:
            outs += [shape_of((2, groups, inner, width), LOW)] * 4
        else:
            outs += [shape_of((groups, 4 * inner, width), LOW)]
        m = len(outs)
        if cut:
            outs += [shape_of(flat, F32), shape_of((1, d_model), F32)]
        got = run(
            functools.partial(attend_backward_kernel, pieces, len(rows) // 2, groups, cut),
            [offsets, bias, *saved, *head, *weights],
            outs,
            [VMEM(s, LOW) for s in (wide, *joined, *heads)] + [VMEM(wide, F32)],
            12 * unit,
            name,
        )
        return got[:n], got[n:m], got[m:]

    def norm_backward(terms, base, gain, carried, name):
        *parts, gain_grad = run(
            functools.partial(norm_back_kernel, len(terms), [lo for _, lo in terms]),
            [v for v, _ in terms] + [base, gain, carried],
            [shape_of((part_rows, d_model), LOW)] * 4 + [shape_of((1, d_model), F32)],
            [],
            20 * rows_n * d_model,
            name,
        )
        return parts, gain_grad

    def sum_parts(terms, name, n=4):
        return run(
            functools.partial(sum_kernel, len(terms), [lo for _, lo in terms]),
            [v for v, _ in terms],
            [shape_of((rows_n // n, d_model), LOW)] * n,
            [],
            4 * rows_n * d_model,
            name,
        )

    def other_x(v):
        return permute_fsdp(v) if swap else lax.all_gather(v, "fsdp", axis=1, tiled=True)

    def joined_pieces(first, first_x, second, second_x):
        return [first, first_x, second, second_x] if swap else [first_x, second_x]

    barrier = lax.optimization_barrier

    pack_t = attention_pack(temporal_qkv, temporal_proj)
    got_first_t = along(pack_t, 2)
    pack_s = attention_pack(spatial_qkv, spatial_proj)
    pack_f = feed_pack()
    if swap:
        gain_other = permute_fsdp(norm_gains)
        gains = jnp.where(
            x == 0,
            jnp.concatenate((norm_gains, gain_other), axis=1),
            jnp.concatenate((gain_other, norm_gains), axis=1),
        ).astype(F32)
    else:
        gains = lax.all_gather(norm_gains, "fsdp", axis=1, tiled=True).astype(F32)
    start = jnp.concatenate(to_time(tokens), axis=0)
    got_first_t, start, pack_s, pack_f, gains, cot = barrier(
        (got_first_t, start, pack_s, pack_f, gains, cotangent)
    )
    first_t = jnp.where(is_source, pack_t, got_first_t)
    first_tx = other_x(first_t)
    weights_t = [first_t, first_tx] if swap else [first_tx]
    near_start = permute_tp(start, 1)
    rows_t = [start, permute_ctx(start, 1), near_start, permute_ctx(near_start, 1)]
    got_first_s = along(pack_s, 2)
    cot_time = jnp.concatenate(to_time(cot), axis=0)
    first_tx, rows_t, got_first_s, cot_time = barrier((first_tx, rows_t, got_first_s, cot_time))
    first_s = jnp.where(is_source, pack_s, got_first_s)
    weights_t = [first_t, first_tx] if swap else [first_tx]

    second_s = permute_tp(first_s, 1)
    first_sx = other_x(first_s)
    parts_t, saved_t, weights_t = attend_forward(
        rows_t, gains[0:1], bias_t, weights_t, False, "time_forward"
    )
    parts_t, second_s, first_sx, pack_f, cot_time = barrier(
        (parts_t, second_s, first_sx, pack_f, cot_time)
    )
    got_t = permute_ctx(parts_t[2], 1)
    (chip_t,) = sum_parts(((parts_t[1], 0), (got_t, rows_n)), "time_near", 1)
    near_t = permute_tp(chip_t, 1)
    far_cot_time = permute_ctx(after(cot_time, chip_t), 2)
    got_first_f = along(after(pack_f, chip_t), 2)
    second_sx = other_x(second_s)
    sums = sum_parts(((start, 0), (parts_t[0], 0), (got_t, 0), (near_t, 0)), "time_sum")
    sums, far_cot_time, got_first_f = barrier((sums, far_cot_time, got_first_f))
    own1 = jnp.concatenate(turn(sums), axis=0)
    own1, second_sx = barrier((own1, second_sx))
    pair1 = permute_ctx(own1, 1)
    first_f = jnp.where(is_source, pack_f, got_first_f)
    pair1, first_f = barrier((pair1, first_f))
    weights_s = joined_pieces(first_s, first_sx, second_s, second_sx)

    second_f = permute_tp(first_f, 1)
    if swap:
        first_fx = permute_fsdp(first_f)
    parts_s, saved_s, weights_s = attend_forward(
        [own1, pair1], gains[1:2], bias_s, weights_s, True, "space_forward"
    )
    back_s = permute_ctx(parts_s[1], 1)
    (own2,) = sum_parts(((own1, 0), (parts_s[0], 0), (back_s, 0)), "space_sum", 1)
    if swap:
        second_f, first_fx, own2 = barrier((second_f, first_fx, own2))
        second_fx = permute_fsdp(second_f)
        weights_f = [first_f, first_fx, second_f, second_fx]
    else:
        weights_f = [w for v in (first_f, second_f) for w in feed_full(v)]
    far_own2 = permute_ctx(own2, 2)
    rows_f = [own2, permute_ctx(own2, 1), far_own2, permute_ctx(far_own2, 1)]

    both_cot = []
    for d in range(4):
        at_d = slice(d * part_rows, (d + 1) * part_rows)
        both_cot.append(jnp.concatenate((cot_time[at_d], far_cot_time[at_d]), axis=0))
    both_cot = turn(after(both_cot, own2))
    if swap:
        both_cot, second_fx = barrier((both_cot, second_fx))
        weights_f = [first_f, first_fx, second_f, second_fx]
    cot_own = jnp.concatenate([v[:part_rows] for v in both_cot], axis=0)
    far_cot = jnp.concatenate([v[part_rows:] for v in both_cot], axis=0)
    cots = [cot_own, permute_ctx(cot_own, 1), far_cot, permute_ctx(far_cot, 1)]

    if swap:
        outs_f = [shape_of((2 * width, hid_half), LOW)] * 4
    else:
        outs_f = [shape_of((2, width, hid_half), LOW), shape_of((2, hid_half, width), LOW)]
    four = (4 * rows_n, d_model)
    out_own, out_send, out_far, dn3, dn3_send, dn3_far, *grads_f = run(
        functools.partial(feed_kernel, pieces, swap),
        [offsets, gains[2:3], *rows_f, *cots, *weights_f],
        [
            shape_of(flat, F32),
            shape_of(two, LOW),
            shape_of(flat, LOW),
            shape_of(two, LOW),
            shape_of(flat, LOW),
            shape_of(flat, LOW),
            *outs_f,
        ],
        [VMEM(four, LOW), VMEM(four, LOW), VMEM(four, F32), VMEM(four, F32)],
        24 * unit,
        "feed",
        20,
    )
    (chip_sum,) = sum_parts(((dn3_far, 0), (permute_ctx(dn3_send, 1), 0)), "feed_near", 1)
    far3 = permute_ctx(chip_sum, 2)
    far3_pair = permute_ctx(far3, 1)
    got3 = permute_ctx(dn3, 1)
    if swap:
        got_f = permute_fsdp(grads_f[3])
        got_f, far3_pair = barrier((got_f, far3_pair))
        b_f = grads_f[1] + got_f
        got_f = permute_fsdp(grads_f[2])
        add_f = permute_tp(b_f, 1)
    got_out = permute_ctx(out_send, 1)
    (chip_out,) = sum_parts(((out_far, 0), (got_out, rows_n)), "feed_out_near", 1)
    far_out = permute_ctx(after(chip_out, far3), 2)

    parts_s, grads_s, (carried2, gain3) = attend_backward(
        [own1, pair1],
        saved_s,
        bias_s,
        [rows_f[0], rows_f[1], dn3, got3, far3, far3_pair, gains[2:3], cots[0], cots[1]],
        weights_s,
        True,
        "space_backward",
    )
    if swap:
        parts_s, far_out, got_f, add_f = barrier((parts_s, far_out, got_f, add_f))
    got2 = permute_ctx(parts_s[1], 1)
    parts1, gain2 = norm_backward(
        ((parts_s[0], 0), (got2, 0)), own1, gains[1:2], carried2, "space_norm"
    )
    own_t = jnp.concatenate(turn(parts1), axis=0)
    near_own_t = permute_tp(own_t, 1)
    head_t = [own_t, permute_ctx(own_t, 1), near_own_t, permute_ctx(near_own_t, 1)]
    out_parts = sum_parts(((out_own, 0), (got_out, 0), (far_out, 0)), "feed_sum")
    out_time = turn(after(out_parts, own_t))
    if swap:
        got_sums_s = first_sends(grads_s)
        keep_s, send_s = first_sums(grads_s, after(got_sums_s, own_t))
        got_sums_s = second_sends(send_s)
        near_own_t, got_sums_s = barrier((near_own_t, got_sums_s))
        sums_s = second_sums(keep_s, got_sums_s)
        add_s = permute_tp(sums_s[1], 1)
        a_f = grads_f[0] + got_f + add_f
        add_f = along(after(a_f, near_own_t), 2, True)

    parts_t, grads_t, _ = attend_backward(
        rows_t, saved_t, bias_t, head_t, weights_t, False, "time_backward"
    )
    if swap:
        parts_t, grads_t, add_s, add_f, gain2, out_time = barrier(
            (parts_t, grads_t, add_s, add_f, gain2, out_time)
        )
        got_sums_t = first_sends(grads_t)
    got1 = permute_ctx(parts_t[2], 1)
    (chip1,) = sum_parts(((parts_t[1], 0), (got1, rows_n)), "time_back_near", 1)
    near1 = permute_tp(chip1, 1)
    if swap:
        got_sums_t, near1 = barrier((got_sums_t, near1))
        keep_t, send_t = first_sums(grads_t, got_sums_t)
        got_sums_t = second_sends(send_t)
    parts0, gain1 = norm_backward(
        ((parts_t[0], 0), (got1, 0), (near1, 0)), start, gains[0:1], own_t, "time_norm"
    )
    gain_all = jnp.concatenate((gain1, gain2, gain3), axis=0)
    if swap:
        a_s = sums_s[0] + add_s
        add_s = along(after(a_s, near1), 2, True)
        total_f = a_f + add_f
        gain_got = permute_ctx(gain_all, 1)
        got_sums_t, add_s, total_f, gain_got = barrier((got_sums_t, add_s, total_f, gain_got))
        (a_t,) = second_sums(keep_t, got_sums_t)
        got_t = along(a_t, 2, True)
        total_s = a_s + add_s
        other_s = permute_ctx(total_s, 2)
        other_f = permute_ctx(total_f, 2)
        gain_all = gain_all + gain_got
        gain_got = permute_fsdp(gain_all)
        got_t, other_f, other_s, gain_got, parts0, out_time = barrier(
            (got_t, other_f, other_s, gain_got, parts0, out_time)
        )
        total_t = a_t + got_t
        other_t = permute_ctx(total_t, 2)
        gain_all = gain_all + gain_got
        gain_got = permute_tp(gain_all, 1)
        both_f, both_s = ordered(total_f, other_f), ordered(total_s, other_s)
        up_grad, down_grad = feed_out(to_pair(both_f))
        s_qkv, s_proj = attention_out(to_pair(both_s))
        both_rows = [jnp.concatenate(pair, axis=0) for pair in zip(out_time, parts0)]
        other_t, gain_got, both_rows, up_grad, down_grad, s_qkv, s_proj = barrier(
            (other_t, gain_got, both_rows, up_grad, down_grad, s_qkv, s_proj)
        )
        got_both = time_sends(both_rows)
        both_t = ordered(total_t, other_t)
        pair_t = permute_ctx(both_t, 1)
        gain_all = gain_all + gain_got
        here = [(a, b) for a in range(n_ctx) for b in range(n_tp)]
        gain_got = [
            lax.ppermute(
                gain_all,
                ("ctx", "tp"),
                [(a * n_tp + b, (a ^ da) * n_tp + (b ^ db)) for a, b in here],
            )
            for da, db in ((0, 2), (2, 0), (2, 2))
        ]
        gain_all = gain_all + gain_got[0] + (gain_got[1] + gain_got[2])
        block_out = time_finish([v[:part_rows] for v in got_both])
        tokens_grad = time_finish([v[part_rows:] for v in got_both]).astype(F32)
        t_qkv, t_proj = attention_out(jnp.where(is_source, both_t, pair_t))
        gain_grads = lax.dynamic_slice_in_dim(gain_all, x * d_part, d_part, axis=1)
    else:
        tokens_grad = time_finish(time_sends(parts0)).astype(F32)
        block_out = time_finish(time_sends(out_time))
        up_grad, down_grad = feed_grads_wide(grads_f)
        s_qkv, s_proj = attention_grads_wide(grads_s)
        t_qkv, t_proj = attention_grads_wide(grads_t)
        for bits in (1, 2):
            gain_all = gain_all + permute_ctx(gain_all, bits)
        for bits in (1, 2):
            gain_all = gain_all + permute_tp(gain_all, bits)
        gain_grads = lax.psum_scatter(gain_all, "fsdp", scatter_dimension=1, tiled=True)
    return (
        block_out,
        tokens_grad,
        gain_grads,
        t_qkv,
        t_proj,
        s_qkv,
        s_proj,
        up_grad,
        down_grad,
    )


def solution(mesh):
    rows = P("tp", "ctx", "fsdp", None)
    weights = (
        P(None, "fsdp"),
        P("fsdp", None, "tp"),
        P("tp", "fsdp"),
        P("fsdp", None, "tp"),
        P("tp", "fsdp"),
        P("fsdp", "tp"),
        P("tp", "fsdp"),
    )
    sizes = (mesh.shape["fsdp"], mesh.shape["ctx"], mesh.shape["tp"])
    return jax.shard_map(
        functools.partial(body, sizes),
        mesh=mesh,
        in_specs=(rows, *weights, rows),
        out_specs=(rows, rows, *weights),
        check_vma=False,
    )
```

```python
import functools

import jax
import jax.numpy as jnp
from jax import lax
from jax.experimental import pallas as pl
from jax.experimental.pallas import tpu as pltpu
from jax.sharding import PartitionSpec as P

HEAD_DIM = 64
EPSILON = 1e-06
SCALE = HEAD_DIM ** (-0.5)
F32 = jnp.float32
LOW = jnp.bfloat16
VMEM = pltpu.VMEM


def dot(a, b, ca, cb):
    return lax.dot_general(a, b, (((ca,), (cb,)), ((), ())), preferred_element_type=F32)


def statistics(rows):
    center = rows - jnp.mean(rows, axis=-1, keepdims=True)
    rate = lax.rsqrt(jnp.mean(center * center, axis=-1, keepdims=True) + EPSILON)
    return center * rate, rate


def norm_back(grad, gain, hat, rate):
    t = grad * gain
    return rate * (
        t
        - jnp.mean(t, axis=-1, keepdims=True)
        - hat * jnp.mean(t * hat, axis=-1, keepdims=True)
    )


def to_blocks(own, pair, frames_cut):
    if not frames_cut:
        return jnp.concatenate((own, pair), axis=0)
    n = own.shape[0] // 8
    return jnp.concatenate(
        [
            rows[(2 * d + f) * n : (2 * d + f + 1) * n]
            for f in range(2)
            for rows in (own, pair)
            for d in range(4)
        ],
        axis=0,
    )


def from_blocks(rows, frames_cut):
    half = rows.shape[0] // 2
    if not frames_cut:
        return rows[:half], rows[half:]
    n = half // 8
    return tuple(
        jnp.concatenate(
            [
                rows[f * half + (4 * side + d) * n : f * half + (4 * side + d + 1) * n]
                for d in range(4)
                for f in range(2)
            ],
            axis=0,
        )
        for side in range(2)
    )


def split_store(chip, refs, piece, group, units):
    send_x, keep_x, send_y, keep_y = refs
    to_x = keep_x if piece == 0 else send_x
    to_x[0, group] = jnp.where(chip == 0, units[0], units[1])
    to_x[1, group] = jnp.where(chip == 0, units[1], units[0])
    keep_y[piece, group] = jnp.where(chip == 0, units[2], units[3])
    send_y[piece, group] = jnp.where(chip == 0, units[3], units[2])


def columns(off_ref, piece, width):
    return pl.ds(pl.multiple_of(off_ref[piece], 128), width)


def store_partial(total, outs, frames_cut):
    n, halves = total.shape[0], len(outs) - 1
    first, second = from_blocks(total[: n // halves, :], frames_cut)
    outs[0][...] = first.astype(LOW)
    if halves == 1:
        outs[1][...] = second.astype(LOW)
        return
    half = n // 4
    outs[2][:half, :] = second.astype(LOW)
    first, second = from_blocks(total[n // 2 :, :], frames_cut)
    outs[1][...] = first.astype(LOW)
    outs[2][half:, :] = second.astype(LOW)


def attend_forward_kernel(pieces, halves, groups, frames_cut, *refs):
    off = refs[0]
    rows_in = refs[1 : 1 + 2 * halves]
    rest = list(refs[1 + 2 * halves :])
    gain, bias = rest.pop(0), rest.pop(0)
    weights = [[rest.pop(0) for _ in range(pieces)] for _ in range(groups)]
    parts_out = [rest.pop(0) for _ in range(1 + halves)]
    saved_at = [rest.pop(0) for _ in range(1 + 2 * groups)]
    kept_at = [rest.pop(0) for _ in range(groups * pieces)]
    normed = rest.pop(0)
    joined, out = [rest.pop(0) for _ in range(groups)], [rest.pop(0) for _ in range(groups)]
    total, sems = rest
    copies = []

    def leave(source, target):
        copy = pltpu.make_async_copy(source, target, sems.at[len(copies)])
        copy.start()
        copies.append(copy)

    for g in range(groups):
        for p in range(pieces):
            leave(weights[g][p], kept_at[g * pieces + p])
    two = normed.shape[0] // halves
    for h in range(halves):
        rows = to_blocks(
            rows_in[2 * h][...].astype(F32), rows_in[2 * h + 1][...].astype(F32), frames_cut
        )
        hat, _ = statistics(rows)
        normed[h * two : (h + 1) * two, :] = (hat * gain[...]).astype(LOW)
    leave(normed, saved_at[0])
    width = weights[0][0].shape[1]
    heads3 = joined[0].shape[1]
    for g in range(groups):
        acc = None
        for p in range(pieces):
            term = dot(normed[:, columns(off, p, width)], weights[g][p][:heads3, :], 1, 1)
            acc = term if acc is None else acc + term
        joined[g][...] = acc.astype(LOW)
        leave(joined[g], saved_at[1 + g])
    block = two // 2
    inner = heads3 // 3

    def one_block(b, carry):
        at = pl.ds(pl.multiple_of(b * block, 16), block)
        for g in range(groups):
            rows3 = joined[g][at, :]
            parts = []
            for h in range(inner // HEAD_DIM):
                lo = h * HEAD_DIM
                q = rows3[:, lo : lo + HEAD_DIM]
                k = rows3[:, inner + lo : inner + lo + HEAD_DIM]
                v = rows3[:, 2 * inner + lo : 2 * inner + lo + HEAD_DIM]
                s = dot(q, k, 1, 1) * SCALE + bias[...]
                e = jnp.exp(s - jnp.max(s, axis=-1, keepdims=True))
                w = (e / jnp.sum(e, axis=-1, keepdims=True)).astype(LOW)
                parts.append(dot(w, v, 1, 0))
            out[g][at, :] = jnp.concatenate(parts, axis=1).astype(LOW)
        return carry

    lax.fori_loop(0, 2 * halves, one_block, 0)
    for g in range(groups):
        leave(out[g], saved_at[1 + groups + g])
    for p in range(pieces):
        acc = dot(out[0][...], weights[0][p][heads3:, :], 1, 0)
        for g in range(1, groups):
            acc = acc + dot(out[g][...], weights[g][p][heads3:, :], 1, 0)
        total[:, columns(off, p, width)] = acc
    store_partial(total, parts_out, frames_cut)
    for copy in copies:
        copy.wait()


def attend_backward_kernel(pieces, halves, groups, frames_cut, *refs):
    off, bias, normed = refs[:3]
    rest = list(refs[3:])
    joined, out = [rest.pop(0) for _ in range(groups)], [rest.pop(0) for _ in range(groups)]
    n_head = 9 if frames_cut else 2 * halves
    head = [rest.pop(0) for _ in range(n_head)]
    weights = [[rest.pop(0) for _ in range(pieces)] for _ in range(groups)]
    parts_out = [rest.pop(0) for _ in range(1 + halves)]
    grads = [rest.pop(0) for _ in range(4 if pieces == 2 else 1)]
    if frames_cut:
        carried, gain_grad = rest.pop(0), rest.pop(0)
    upstream = rest.pop(0)
    djoined, dout = [rest.pop(0) for _ in range(groups)], [rest.pop(0) for _ in range(groups)]
    total = rest.pop(0)
    two = upstream.shape[0] // halves
    half = two // 2
    if frames_cut:
        base_own, base_pair, grad_l, grad_r, far_own, far_pair, gain, cot_own, cot_pair = head
        both = []
        for lo, base, far_sum, cot in (
            (0, base_own, far_own, cot_own),
            (half, base_pair, far_pair, cot_pair),
        ):
            at = slice(lo, lo + half)
            far = slice(half - lo, 2 * half - lo)
            hat, rate = statistics(base[...].astype(F32))
            dn = grad_l[at, :].astype(F32) + grad_r[far, :].astype(F32) + far_sum[...].astype(F32)
            dx = cot[...].astype(F32) + norm_back(dn, gain[...], hat, rate)
            if lo == 0:
                carried[...] = dx
                gain_grad[...] = jnp.sum(dn * hat, axis=0, keepdims=True)
            both.append(dx)
        upstream[...] = to_blocks(both[0], both[1], frames_cut).astype(LOW)
    else:
        for r in range(2 * halves):
            upstream[r * half : (r + 1) * half, :] = head[r][...]
    width = weights[0][0].shape[1]
    heads3 = joined[0].shape[1]
    inner = heads3 // 3
    for g in range(groups):
        acc = None
        for p in range(pieces):
            term = dot(upstream[:, columns(off, p, width)], weights[g][p][heads3:, :], 1, 1)
            acc = term if acc is None else acc + term
        dout[g][...] = acc.astype(LOW)

    def one_block(b, carry):
        at = pl.ds(pl.multiple_of(b * half, 16), half)
        for g in range(groups):
            rows3 = joined[g][at, :]
            do3 = dout[g][at, :]
            dqs, dks, dvs = [], [], []
            for h in range(inner // HEAD_DIM):
                lo = h * HEAD_DIM
                q = rows3[:, lo : lo + HEAD_DIM]
                k = rows3[:, inner + lo : inner + lo + HEAD_DIM]
                v = rows3[:, 2 * inner + lo : 2 * inner + lo + HEAD_DIM]
                do = do3[:, lo : lo + HEAD_DIM]
                s = dot(q, k, 1, 1) * SCALE + bias[...]
                e = jnp.exp(s - jnp.max(s, axis=-1, keepdims=True))
                w = e / jnp.sum(e, axis=-1, keepdims=True)
                dw = dot(do, v, 1, 1)
                ds = (w * (dw - jnp.sum(w * dw, axis=-1, keepdims=True))).astype(LOW)
                dqs.append(dot(ds, k, 1, 0) * SCALE)
                dks.append(dot(ds, q, 0, 0) * SCALE)
                dvs.append(dot(w.astype(LOW), do, 0, 0))
            djoined[g][at, :] = jnp.concatenate(dqs + dks + dvs, axis=1).astype(LOW)
        return carry

    lax.fori_loop(0, 2 * halves, one_block, 0)
    chip = off[pieces]
    for p in range(pieces):
        cols = columns(off, p, width)
        wide = normed[:, cols]
        dy = upstream[:, cols]
        acc = None
        for g in range(groups):
            value = dot(djoined[g][...], wide, 0, 0).astype(LOW)
            proj = dot(out[g][...], dy, 0, 0).astype(LOW)
            if pieces == 2:
                units = [value[u * inner : (u + 1) * inner] for u in range(3)] + [proj]
                split_store(chip, grads, p, g, units)
            else:
                grads[0][g, :heads3] = value
                grads[0][g, heads3:] = proj
            term = dot(djoined[g][...], weights[g][p][:heads3, :], 1, 0)
            acc = term if acc is None else acc + term
        total[:, cols] = acc
    store_partial(total, parts_out, frames_cut)


def feed_kernel(pieces, packed, *refs):
    off, gain = refs[:2]
    rows_in, cots = refs[2:6], refs[6:10]
    at = 10
    n_w = 2 * pieces * (1 if packed else 2)
    weights = refs[at : at + n_w]
    at += n_w
    out_own, out_send, out_far, dn_near, dn_send, dn_far = refs[at : at + 6]
    at += 6
    n_g = 4 if packed else 2
    grads = refs[at : at + n_g]
    normed, cot, total, dtotal = refs[at + n_g :]
    n = rows_in[0].shape[0]
    for r in range(4):
        rows_at = slice(r * n, (r + 1) * n)
        hat, _ = statistics(rows_in[r][...].astype(F32))
        normed[rows_at, :] = (hat * gain[...]).astype(LOW)
        cot[rows_at, :] = cots[r][...]
    for c in range(2):
        ups, downs = [], []
        for p in range(pieces):
            if packed:
                w = weights[c * pieces + p]
                wide = w.shape[0] // 2
                ups.append(w[:wide, :])
                downs.append(w[wide:, :])
            else:
                ups.append(weights[2 * (c * pieces + p)][...])
                downs.append(weights[2 * (c * pieces + p) + 1][...])
        width = ups[0].shape[0]
        hidden = dact = None
        for p in range(pieces):
            cols = columns(off, p, width)
            term = dot(normed[:, cols], ups[p], 1, 0)
            dterm = dot(cot[:, cols], downs[p], 1, 1)
            hidden = term if hidden is None else hidden + term
            dact = dterm if dact is None else dact + dterm
        cdf = 0.5 * (1.0 + lax.erf(hidden * (2.0**-0.5)))
        act = (hidden * cdf).astype(LOW)
        slope = cdf + hidden * (jnp.exp(-0.5 * hidden * hidden) * (2.0 * jnp.pi) ** -0.5)
        dhid = (dact * slope).astype(LOW)
        for p in range(pieces):
            cols = columns(off, p, width)
            term = dot(act, downs[p], 1, 0)
            dterm = dot(dhid, ups[p], 1, 1)
            if c == 0:
                total[:, cols] = term
                dtotal[:, cols] = dterm
            else:
                total[:, cols] += term
                dtotal[:, cols] += dterm
            up_grad = dot(normed[:, cols], dhid, 0, 0).astype(LOW)
            down_grad = dot(act, cot[:, cols], 0, 0).astype(LOW)
            if packed:
                grads[2 * p + c][:width, :] = up_grad
                grads[2 * p + c][width:, :] = down_grad
            else:
                grads[0][c] = up_grad
                grads[1][c] = down_grad
    out_own[...] = rows_in[0][...].astype(F32) + total[:n, :]
    out_send[:n, :] = total[n : 2 * n, :].astype(LOW)
    out_send[n:, :] = total[3 * n :, :].astype(LOW)
    out_far[...] = total[2 * n : 3 * n, :].astype(LOW)
    dn_near[...] = dtotal[: 2 * n, :].astype(LOW)
    dn_far[...] = dtotal[2 * n : 3 * n, :].astype(LOW)
    dn_send[...] = dtotal[3 * n :, :].astype(LOW)


def store_parts(rows, outs):
    n = rows.shape[0] // len(outs)
    for d, out in enumerate(outs):
        out[...] = rows[d * n : (d + 1) * n].astype(out.dtype)


def norm_back_kernel(n, firsts, *refs):
    base, gain, carried = refs[n : n + 3]
    outs = refs[n + 3 :]
    rows = base.shape[0]
    hat, rate = statistics(base[...].astype(F32))
    dn = refs[n - 1][firsts[n - 1] : firsts[n - 1] + rows, :].astype(F32)
    for k in range(n - 2, -1, -1):
        dn = refs[k][firsts[k] : firsts[k] + rows, :].astype(F32) + dn
    store_parts(carried[...].astype(F32) + norm_back(dn, gain[...], hat, rate), outs[:-1])
    outs[-1][...] = jnp.sum(dn * hat, axis=0, keepdims=True)


def sum_kernel(n, firsts, *refs):
    outs = refs[n:]
    rows = outs[0].shape[0] * len(outs)
    total = refs[n - 1][firsts[n - 1] : firsts[n - 1] + rows, :].astype(F32)
    for k in range(n - 2, -1, -1):
        total = refs[k][firsts[k] : firsts[k] + rows, :].astype(F32) + total
    store_parts(total, outs)


def in_vmem(n):
    return [pl.BlockSpec(memory_space=VMEM)] * n


def shape_of(shape, dtype):
    return jax.ShapeDtypeStruct(shape, dtype)


def run(kernel, operands, outs, scratch, flops, name, vmem=12, anywhere=0):
    moved = sum(o.size * o.dtype.itemsize for o in operands) + sum(
        o.size * o.dtype.itemsize for o in outs
    )
    scalar = operands[0].dtype == jnp.int32
    specs = in_vmem(len(operands))
    if scalar:
        specs[0] = pl.BlockSpec(memory_space=pltpu.SMEM)
    return pl.pallas_call(
        kernel,
        out_shape=outs,
        in_specs=specs,
        out_specs=in_vmem(len(outs) - anywhere)
        + [pl.BlockSpec(memory_space=pl.ANY)] * anywhere,
        scratch_shapes=scratch,
        compiler_params=pltpu.CompilerParams(vmem_limit_bytes=vmem << 20),
        cost_estimate=pl.CostEstimate(flops=flops, bytes_accessed=moved, transcendentals=0),
        name=name,
    )(*operands)


def after(value, *tokens):
    return lax.optimization_barrier((value, *tokens))[0]


def body(sizes, tokens, norm_gains, temporal_qkv, temporal_proj, spatial_qkv, spatial_proj, up_weight, down_weight, cotangent):
    n_fsdp, n_ctx, n_tp = sizes
    swap = n_fsdp == 2
    d_model = tokens.shape[3]
    d_part = d_model // n_fsdp
    places = tokens.shape[0]
    block = 2 * (-(-places // 4))
    x, i, z = lax.axis_index("fsdp"), lax.axis_index("ctx"), lax.axis_index("tp")
    core, chip = i % 2, i // 2
    is_source = (z // 2) == core

    def permute_ctx(v, bits):
        return lax.ppermute(v, "ctx", [(a, a ^ bits) for a in range(n_ctx)])

    def permute_tp(v, bits):
        return lax.ppermute(v, "tp", [(a, a ^ bits) for a in range(n_tp)])

    def permute_fsdp(v):
        return lax.ppermute(v, "fsdp", [(0, 1), (1, 0)])

    def along(v, bits, back=False):
        pairs = []
        for a in range(n_ctx):
            for b in (2 * (a % 2), 2 * (a % 2) + 1):
                there, here = a * n_tp + (b ^ bits), a * n_tp + b
                pairs.append((there, here) if back else (here, there))
        return lax.ppermute(v, ("ctx", "tp"), pairs)

    def exclusive(parts, bits):
        low, high = (bits & 1) == 1, (bits & 2) == 2
        parts = [jnp.where(low, parts[d ^ 1], parts[d]) for d in range(4)]
        return [jnp.where(high, parts[d ^ 2], parts[d]) for d in range(4)]

    slot_bits = (z & 2) | ((z & 1) ^ core)
    part_rows = 2 * block

    def to_time(rows):
        t = jnp.transpose(rows, (2, 1, 0, 3))
        t = jnp.pad(t, ((0, 0), (0, 0), (0, 2 * block - places), (0, 0)))
        parts = [t[c, :, b * block : (b + 1) * block] for c in range(2) for b in range(2)]
        parts = exclusive([v.reshape(part_rows, d_model) for v in parts], i)
        got = [parts[0]] + [permute_ctx(parts[e], e) for e in range(1, 4)]
        return exclusive(got, slot_bits)

    def time_sends(own):
        parts = exclusive(own, slot_bits)
        return [parts[0]] + [permute_ctx(parts[e], e) for e in range(1, 4)]

    def time_finish(got):
        got = [v.reshape(2, block, d_model) for v in exclusive(got, i)]
        t = jnp.stack(
            [jnp.concatenate((got[2 * c], got[2 * c + 1]), axis=1)[:, :places] for c in range(2)]
        )
        return jnp.transpose(t, (2, 1, 0, 3))

    def turn(own):
        return [own[0]] + [permute_tp(own[e], e) for e in range(1, 4)]

    rows_n = 8 * block
    flat = (rows_n, d_model)

    def attention_pack(qkv, proj):
        return jnp.concatenate((jnp.transpose(qkv, (1, 2, 0)).reshape(-1, d_part), proj), axis=0)

    def spread_first(shard):
        return jnp.where(is_source, shard, along(shard, 2))

    hid_half = up_weight.shape[1] // 2

    def feed_pack():
        up = lax.dynamic_slice_in_dim(up_weight, chip * hid_half, hid_half, axis=1)
        down = lax.dynamic_slice_in_dim(down_weight, chip * hid_half, hid_half, axis=0)
        return jnp.concatenate((up, down.reshape(d_part, hid_half)), axis=0)

    def feed_full(shard):
        every = lax.all_gather(shard, "fsdp", axis=0)
        up = every[:, :d_part].reshape(d_model, hid_half)
        down = every[:, d_part:].reshape(n_fsdp, hid_half, d_part)
        return [up, jnp.transpose(down, (1, 0, 2)).reshape(hid_half, d_model)]

    def owner_sum(a, b):
        mine = a + permute_tp(b, 1)
        return mine + along(mine, 2, True)

    def other_half(v):
        pairs = []
        for a in range(n_ctx):
            for b in (2 * (a % 2), 2 * (a % 2) + 1):
                pairs.append((a * n_tp + b, (a ^ 2) * n_tp + b))
        return lax.ppermute(v, ("ctx", "tp"), pairs)

    def owner_sends(a, b):
        return along(a, 2, True), along(b, 3, True), along(b, 1)

    def ordered(mine, other):
        return jnp.stack((jnp.where(chip == 0, mine, other), jnp.where(chip == 0, other, mine)))

    def to_pair(both):
        return jnp.where(is_source, both, permute_ctx(both, 1))

    def to_both(mine):
        return to_pair(ordered(mine, permute_ctx(mine, 2)))

    def first_sends(grads):
        send_x, _, send_y, _ = grads
        return permute_fsdp(send_x), permute_ctx(send_y, 2)

    def first_sums(grads, got):
        _, keep_x, _, keep_y = grads
        by_x, by_y = keep_x + got[0], keep_y + got[1]
        return (by_x[0], by_y[0]), (by_x[1], by_y[1])

    def second_sends(send):
        return permute_ctx(send[0], 2), permute_fsdp(send[1])

    def second_sums(keep, got):
        by_x, by_y = keep[0] + got[0], keep[1] + got[1]
        return [jnp.stack((by_x[g], by_y[g])) for g in range(by_x.shape[0])]

    def attention_out(total):
        joined_grad = jnp.stack((total[0, 0], total[1, 0], total[0, 1])).astype(F32)
        return jnp.transpose(joined_grad, (2, 0, 1)), total[1, 1].astype(F32)

    def feed_out(total):
        up = jnp.concatenate((total[0, :d_part], total[1, :d_part]), axis=1)
        down = jnp.concatenate((total[0, d_part:], total[1, d_part:]), axis=0)
        return up.astype(F32), down.astype(F32)

    def attention_grads_wide(grads):
        total = lax.psum_scatter(grads[0], "fsdp", scatter_dimension=2, tiled=True)
        total = total + permute_ctx(total, 2)
        if total.shape[0] == 2:
            mine = owner_sum(total[0], total[1])
        else:
            mine = total[0] + along(total[0], 2, True)
        full = jnp.where(is_source, mine, permute_ctx(mine, 1)).astype(F32)
        inner = full.shape[0] // 4
        joined_grad = full[: 3 * inner].reshape(3, inner, d_part)
        return jnp.transpose(joined_grad, (2, 0, 1)), full[3 * inner :]

    def feed_grads_wide(grads):
        up = lax.psum_scatter(grads[0], "fsdp", scatter_dimension=1, tiled=True)
        down = lax.psum_scatter(grads[1], "fsdp", scatter_dimension=2, tiled=True)
        up = to_both(owner_sum(up[0], up[1]))
        down = to_both(owner_sum(down[0], down[1]))
        return (
            jnp.concatenate((up[0], up[1]), axis=1).astype(F32),
            jnp.concatenate((down[0], down[1]), axis=0).astype(F32),
        )

    pieces = 2 if swap else 1
    width = d_model // pieces
    if swap:
        offsets = jnp.stack((x * width, (1 - x) * width, chip)).astype(jnp.int32)
    else:
        offsets = jnp.stack((0 * chip, chip)).astype(jnp.int32)

    at = jnp.arange(rows_n, dtype=jnp.int32)
    far = jnp.float32(-1e30)
    bias_t = jnp.where((at % block)[:, None] == (at % block)[None, :], 0.0, far).astype(F32)
    owner = jnp.where(at < rows_n // 2, core, 1 - core)
    real = owner * block + at % block < places
    bias_s = jnp.broadcast_to(jnp.where(real, 0.0, far).astype(F32)[None], (rows_n, rows_n))

    two = (2 * rows_n, d_model)
    unit = 2 * rows_n * d_model * d_model

    inner = temporal_qkv.shape[2]

    def shapes(rows, groups):
        all_rows = len(rows) * rows_n
        return (all_rows, d_model), [(all_rows, 3 * inner)] * groups, [(all_rows, inner)] * groups

    def part_shapes(rows):
        if len(rows) == 2:
            return [shape_of(flat, LOW)] * 2
        return [shape_of(flat, LOW)] * 2 + [shape_of(two, LOW)]

    def attend_forward(rows, gain, bias, weights, cut, name):
        groups = len(weights) // pieces
        wide, joined, heads = shapes(rows, groups)
        kept = [shape_of(s, LOW) for s in (wide, *joined, *heads)]
        kept += [shape_of(w.shape, LOW) for w in weights]
        outs = part_shapes(rows) + kept
        got = run(
            functools.partial(attend_forward_kernel, pieces, len(rows) // 2, groups, cut),
            [offsets, *rows, gain, bias, *weights],
            outs,
            [VMEM(s, LOW) for s in (wide, *joined, *heads)]
            + [VMEM(wide, F32), pltpu.SemaphoreType.DMA((len(kept),))],
            6 * unit,
            name,
            16,
            len(kept),
        )
        n = len(part_shapes(rows))
        m = n + 1 + 2 * groups
        return got[:n], got[n:m], got[m:]

    def attend_backward(rows, saved, bias, head, weights, cut, name):
        groups = len(weights) // pieces
        wide, joined, heads = shapes(rows, groups)
        outs = part_shapes(rows)
        n = len(outs)
        if swap:
            outs += [shape_of((2, groups, inner, width), LOW)] * 4
        else:
            outs += [shape_of((groups, 4 * inner, width), LOW)]
        m = len(outs)
        if cut:
            outs += [shape_of(flat, F32), shape_of((1, d_model), F32)]
        got = run(
            functools.partial(attend_backward_kernel, pieces, len(rows) // 2, groups, cut),
            [offsets, bias, *saved, *head, *weights],
            outs,
            [VMEM(s, LOW) for s in (wide, *joined, *heads)] + [VMEM(wide, F32)],
            12 * unit,
            name,
        )
        return got[:n], got[n:m], got[m:]

    def norm_backward(terms, base, gain, carried, name):
        *parts, gain_grad = run(
            functools.partial(norm_back_kernel, len(terms), [lo for _, lo in terms]),
            [v for v, _ in terms] + [base, gain, carried],
            [shape_of((part_rows, d_model), LOW)] * 4 + [shape_of((1, d_model), F32)],
            [],
            20 * rows_n * d_model,
            name,
        )
        return parts, gain_grad

    def sum_parts(terms, name, n=4):
        return run(
            functools.partial(sum_kernel, len(terms), [lo for _, lo in terms]),
            [v for v, _ in terms],
            [shape_of((rows_n // n, d_model), LOW)] * n,
            [],
            4 * rows_n * d_model,
            name,
        )

    def other_x(v):
        return permute_fsdp(v) if swap else lax.all_gather(v, "fsdp", axis=1, tiled=True)

    def joined_pieces(first, first_x, second, second_x):
        return [first, first_x, second, second_x] if swap else [first_x, second_x]

    barrier = lax.optimization_barrier

    pack_t = attention_pack(temporal_qkv, temporal_proj)
    got_first_t = along(pack_t, 2)
    pack_s = attention_pack(spatial_qkv, spatial_proj)
    pack_f = feed_pack()
    if swap:
        gain_other = permute_fsdp(norm_gains)
        gains = jnp.where(
            x == 0,
            jnp.concatenate((norm_gains, gain_other), axis=1),
            jnp.concatenate((gain_other, norm_gains), axis=1),
        ).astype(F32)
    else:
        gains = lax.all_gather(norm_gains, "fsdp", axis=1, tiled=True).astype(F32)
    start = jnp.concatenate(to_time(tokens), axis=0)
    got_first_t, start, pack_s, pack_f, gains, cot = barrier(
        (got_first_t, start, pack_s, pack_f, gains, cotangent)
    )
    first_t = jnp.where(is_source, pack_t, got_first_t)
    first_tx = other_x(first_t)
    weights_t = [first_t, first_tx] if swap else [first_tx]
    near_start = permute_tp(start, 1)
    rows_t = [start, permute_ctx(start, 1), near_start, permute_ctx(near_start, 1)]
    got_first_s = along(pack_s, 2)
    cot_time = jnp.concatenate(to_time(cot), axis=0)
    first_tx, rows_t, got_first_s, cot_time = barrier((first_tx, rows_t, got_first_s, cot_time))
    first_s = jnp.where(is_source, pack_s, got_first_s)
    weights_t = [first_t, first_tx] if swap else [first_tx]

    second_s = permute_tp(first_s, 1)
    first_sx = other_x(first_s)
    parts_t, saved_t, weights_t = attend_forward(
        rows_t, gains[0:1], bias_t, weights_t, False, "time_forward"
    )
    parts_t, second_s, first_sx, pack_f, cot_time = barrier(
        (parts_t, second_s, first_sx, pack_f, cot_time)
    )
    got_t = permute_ctx(parts_t[2], 1)
    (chip_t,) = sum_parts(((parts_t[1], 0), (got_t, rows_n)), "time_near", 1)
    near_t = permute_tp(chip_t, 1)
    far_cot_time = permute_ctx(after(cot_time, chip_t), 2)
    got_first_f = along(after(pack_f, chip_t), 2)
    second_sx = other_x(second_s)
    sums = sum_parts(((start, 0), (parts_t[0], 0), (got_t, 0), (near_t, 0)), "time_sum")
    sums, far_cot_time, got_first_f = barrier((sums, far_cot_time, got_first_f))
    own1 = jnp.concatenate(turn(sums), axis=0)
    own1, second_sx = barrier((own1, second_sx))
    pair1 = permute_ctx(own1, 1)
    first_f = jnp.where(is_source, pack_f, got_first_f)
    pair1, first_f = barrier((pair1, first_f))
    weights_s = joined_pieces(first_s, first_sx, second_s, second_sx)

    second_f = permute_tp(first_f, 1)
    if swap:
        first_fx = permute_fsdp(first_f)
    parts_s, saved_s, weights_s = attend_forward(
        [own1, pair1], gains[1:2], bias_s, weights_s, True, "space_forward"
    )
    back_s = permute_ctx(parts_s[1], 1)
    (own2,) = sum_parts(((own1, 0), (parts_s[0], 0), (back_s, 0)), "space_sum", 1)
    if swap:
        second_f, first_fx, own2 = barrier((second_f, first_fx, own2))
        second_fx = permute_fsdp(second_f)
        weights_f = [first_f, first_fx, second_f, second_fx]
    else:
        weights_f = [w for v in (first_f, second_f) for w in feed_full(v)]
    far_own2 = permute_ctx(own2, 2)
    rows_f = [own2, permute_ctx(own2, 1), far_own2, permute_ctx(far_own2, 1)]

    both_cot = []
    for d in range(4):
        at_d = slice(d * part_rows, (d + 1) * part_rows)
        both_cot.append(jnp.concatenate((cot_time[at_d], far_cot_time[at_d]), axis=0))
    both_cot = turn(after(both_cot, own2))
    if swap:
        both_cot, second_fx = barrier((both_cot, second_fx))
        weights_f = [first_f, first_fx, second_f, second_fx]
    cot_own = jnp.concatenate([v[:part_rows] for v in both_cot], axis=0)
    far_cot = jnp.concatenate([v[part_rows:] for v in both_cot], axis=0)
    cots = [cot_own, permute_ctx(cot_own, 1), far_cot, permute_ctx(far_cot, 1)]

    if swap:
        outs_f = [shape_of((2 * width, hid_half), LOW)] * 4
    else:
        outs_f = [shape_of((2, width, hid_half), LOW), shape_of((2, hid_half, width), LOW)]
    four = (4 * rows_n, d_model)
    out_own, out_send, out_far, dn3, dn3_send, dn3_far, *grads_f = run(
        functools.partial(feed_kernel, pieces, swap),
        [offsets, gains[2:3], *rows_f, *cots, *weights_f],
        [
            shape_of(flat, F32),
            shape_of(two, LOW),
            shape_of(flat, LOW),
            shape_of(two, LOW),
            shape_of(flat, LOW),
            shape_of(flat, LOW),
            *outs_f,
        ],
        [VMEM(four, LOW), VMEM(four, LOW), VMEM(four, F32), VMEM(four, F32)],
        24 * unit,
        "feed",
        20,
    )
    (chip_sum,) = sum_parts(((dn3_far, 0), (permute_ctx(dn3_send, 1), 0)), "feed_near", 1)
    far3 = permute_ctx(chip_sum, 2)
    far3_pair = permute_ctx(far3, 1)
    got3 = permute_ctx(dn3, 1)
    if swap:
        got_f = permute_fsdp(grads_f[3])
        got_f, far3_pair = barrier((got_f, far3_pair))
        b_f = grads_f[1] + got_f
        got_f = permute_fsdp(grads_f[2])
        add_f = permute_tp(b_f, 1)
    got_out = permute_ctx(out_send, 1)
    (chip_out,) = sum_parts(((out_far, 0), (got_out, rows_n)), "feed_out_near", 1)
    far_out = permute_ctx(after(chip_out, far3), 2)

    parts_s, grads_s, (carried2, gain3) = attend_backward(
        [own1, pair1],
        saved_s,
        bias_s,
        [rows_f[0], rows_f[1], dn3, got3, far3, far3_pair, gains[2:3], cots[0], cots[1]],
        weights_s,
        True,
        "space_backward",
    )
    if swap:
        parts_s, far_out, got_f, add_f = barrier((parts_s, far_out, got_f, add_f))
    got2 = permute_ctx(parts_s[1], 1)
    parts1, gain2 = norm_backward(
        ((parts_s[0], 0), (got2, 0)), own1, gains[1:2], carried2, "space_norm"
    )
    own_t = jnp.concatenate(turn(parts1), axis=0)
    near_own_t = permute_tp(own_t, 1)
    head_t = [own_t, permute_ctx(own_t, 1), near_own_t, permute_ctx(near_own_t, 1)]
    out_parts = sum_parts(((out_own, 0), (got_out, 0), (far_out, 0)), "feed_sum")
    if not swap:
        out_time = turn(out_parts)
    if swap:
        got_sums_s = first_sends(grads_s)
        keep_s, send_s = first_sums(grads_s, after(got_sums_s, own_t))
        got_sums_s = second_sends(send_s)
        a_f = grads_f[0] + got_f + add_f
        add_f = along(after(a_f, near_own_t), 2, True)

    parts_t, grads_t, _ = attend_backward(
        rows_t, saved_t, bias_t, head_t, weights_t, False, "time_backward"
    )
    if swap:
        parts_t, grads_t, got_sums_s, add_f, gain2, out_parts = barrier(
            (parts_t, grads_t, got_sums_s, add_f, gain2, out_parts)
        )
        got_sums_t = first_sends(grads_t)
        sums_s = second_sums(keep_s, got_sums_s)
        add_s = permute_tp(sums_s[1], 1)
    got1 = permute_ctx(parts_t[2], 1)
    (chip1,) = sum_parts(((parts_t[1], 0), (got1, rows_n)), "time_back_near", 1)
    near1 = permute_tp(chip1, 1)
    if swap:
        got_sums_t, near1, add_s = barrier((got_sums_t, near1, add_s))
        keep_t, send_t = first_sums(grads_t, got_sums_t)
        got_sums_t = second_sends(send_t)
    parts0, gain1 = norm_backward(
        ((parts_t[0], 0), (got1, 0), (near1, 0)), start, gains[0:1], own_t, "time_norm"
    )
    gain_all = jnp.concatenate((gain1, gain2, gain3), axis=0)
    if swap:
        a_s = sums_s[0] + add_s
        add_s = along(a_s, 2, True)
        total_f = a_f + add_f
        other_f = other_half(total_f)
        gain_got = permute_ctx(gain_all, 1)
        got_sums_t, add_s, other_f, gain_got = barrier((got_sums_t, add_s, other_f, gain_got))

        def across(v, axes, first, second):
            n = (n_fsdp if axes[0] == "fsdp" else n_ctx, n_tp)
            cells = [(a, b) for a in range(n[0]) for b in range(n[1])]
            pairs = [(a * n[1] + b, (a ^ first) * n[1] + (b ^ second)) for a, b in cells]
            return lax.ppermute(v, axes, pairs)

        (a_t,) = second_sums(keep_t, got_sums_t)
        got_t = along(a_t, 2, True)
        total_s = a_s + add_s
        other_s = other_half(total_s)
        gain_all = gain_all + gain_got
        gain_got = [across(gain_all, ("fsdp", "tp"), *d) for d in ((0, 1), (1, 0), (1, 1))]
        out_time = turn(out_parts)
        got_t, other_s, gain_got, parts0, out_time = barrier(
            (got_t, other_s, gain_got, parts0, out_time)
        )
        total_t = a_t + got_t
        other_t = other_half(total_t)
        gain_all = gain_all + gain_got[0] + (gain_got[1] + gain_got[2])
        gain_got = [across(gain_all, ("ctx", "tp"), *d) for d in ((0, 2), (2, 0), (2, 2))]
        both_f, both_s = ordered(total_f, other_f), ordered(total_s, other_s)
        up_grad, down_grad = feed_out(to_pair(both_f))
        s_qkv, s_proj = attention_out(to_pair(both_s))
        both_rows = [jnp.concatenate(pair, axis=0) for pair in zip(out_time, parts0)]
        got_both = time_sends(both_rows)
        other_t, gain_got, got_both, up_grad, down_grad, s_qkv, s_proj = barrier(
            (other_t, gain_got, got_both, up_grad, down_grad, s_qkv, s_proj)
        )
        both_t = ordered(total_t, other_t)
        pair_t = permute_ctx(both_t, 1)
        gain_all = gain_all + gain_got[0] + (gain_got[1] + gain_got[2])
        block_out = time_finish([v[:part_rows] for v in got_both])
        tokens_grad = time_finish([v[part_rows:] for v in got_both]).astype(F32)
        t_qkv, t_proj = attention_out(jnp.where(is_source, both_t, pair_t))
        gain_grads = lax.dynamic_slice_in_dim(gain_all, x * d_part, d_part, axis=1)
    else:
        tokens_grad = time_finish(time_sends(parts0)).astype(F32)
        block_out = time_finish(time_sends(out_time))
        up_grad, down_grad = feed_grads_wide(grads_f)
        s_qkv, s_proj = attention_grads_wide(grads_s)
        t_qkv, t_proj = attention_grads_wide(grads_t)
        for bits in (1, 2):
            gain_all = gain_all + permute_ctx(gain_all, bits)
        for bits in (1, 2):
            gain_all = gain_all + permute_tp(gain_all, bits)
        gain_grads = lax.psum_scatter(gain_all, "fsdp", scatter_dimension=1, tiled=True)
    return (
        block_out,
        tokens_grad,
        gain_grads,
        t_qkv,
        t_proj,
        s_qkv,
        s_proj,
        up_grad,
        down_grad,
    )


def solution(mesh):
    rows = P("tp", "ctx", "fsdp", None)
    weights = (
        P(None, "fsdp"),
        P("fsdp", None, "tp"),
        P("tp", "fsdp"),
        P("fsdp", None, "tp"),
        P("tp", "fsdp"),
        P("fsdp", "tp"),
        P("tp", "fsdp"),
    )
    sizes = (mesh.shape["fsdp"], mesh.shape["ctx"], mesh.shape["tp"])
    return jax.shard_map(
        functools.partial(body, sizes),
        mesh=mesh,
        in_specs=(rows, *weights, rows),
        out_specs=(rows, rows, *weights),
        check_vma=False,
    )
```

```python
import functools

import jax
import jax.numpy as jnp
from jax import lax
from jax.experimental import pallas as pl
from jax.experimental.pallas import tpu as pltpu
from jax.sharding import PartitionSpec as P

HEAD_DIM = 64
EPSILON = 1e-06
SCALE = HEAD_DIM ** (-0.5)
F32 = jnp.float32
LOW = jnp.bfloat16
VMEM = pltpu.VMEM


def dot(a, b, ca, cb):
    return lax.dot_general(a, b, (((ca,), (cb,)), ((), ())), preferred_element_type=F32)


def statistics(rows):
    center = rows - jnp.mean(rows, axis=-1, keepdims=True)
    rate = lax.rsqrt(jnp.mean(center * center, axis=-1, keepdims=True) + EPSILON)
    return center * rate, rate


def norm_back(grad, gain, hat, rate):
    t = grad * gain
    return rate * (
        t
        - jnp.mean(t, axis=-1, keepdims=True)
        - hat * jnp.mean(t * hat, axis=-1, keepdims=True)
    )


def to_blocks(own, pair, frames_cut):
    if not frames_cut:
        return jnp.concatenate((own, pair), axis=0)
    n = own.shape[0] // 8
    return jnp.concatenate(
        [
            rows[(2 * d + f) * n : (2 * d + f + 1) * n]
            for f in range(2)
            for rows in (own, pair)
            for d in range(4)
        ],
        axis=0,
    )


def from_blocks(rows, frames_cut):
    half = rows.shape[0] // 2
    if not frames_cut:
        return rows[:half], rows[half:]
    n = half // 8
    return tuple(
        jnp.concatenate(
            [
                rows[f * half + (4 * side + d) * n : f * half + (4 * side + d + 1) * n]
                for d in range(4)
                for f in range(2)
            ],
            axis=0,
        )
        for side in range(2)
    )


def split_store(chip, refs, piece, group, units):
    send_x, keep_x, send_y, keep_y = refs
    to_x = keep_x if piece == 0 else send_x
    to_x[0, group] = jnp.where(chip == 0, units[0], units[1])
    to_x[1, group] = jnp.where(chip == 0, units[1], units[0])
    keep_y[piece, group] = jnp.where(chip == 0, units[2], units[3])
    send_y[piece, group] = jnp.where(chip == 0, units[3], units[2])


def rows_of(step, size, first=0):
    return pl.ds(pl.multiple_of(first + step * size, 16), size)


def columns(off_ref, piece, width):
    return pl.ds(pl.multiple_of(off_ref[piece], 128), width)


def store_partial(total, outs, frames_cut):
    n, halves = total.shape[0], len(outs) - 1
    first, second = from_blocks(total[: n // halves, :], frames_cut)
    outs[0][...] = first.astype(LOW)
    if halves == 1:
        outs[1][...] = second.astype(LOW)
        return
    half = n // 4
    outs[2][:half, :] = second.astype(LOW)
    first, second = from_blocks(total[n // 2 :, :], frames_cut)
    outs[1][...] = first.astype(LOW)
    outs[2][half:, :] = second.astype(LOW)


def attend_forward_kernel(pieces, halves, groups, frames_cut, *refs):
    off = refs[0]
    rows_in = refs[1 : 1 + 2 * halves]
    rest = list(refs[1 + 2 * halves :])
    gain, bias = rest.pop(0), rest.pop(0)
    weights = [[rest.pop(0) for _ in range(pieces)] for _ in range(groups)]
    parts_out = [rest.pop(0) for _ in range(1 + halves)]
    saved_at = [rest.pop(0) for _ in range(3)]
    kept_at = [rest.pop(0) for _ in range(groups * pieces)]
    normed, joined, out, total, sems = rest
    copies = []

    def leave(source, target):
        copy = pltpu.make_async_copy(source, target, sems.at[len(copies)])
        copy.start()
        copies.append(copy)

    for g in range(groups):
        for p in range(pieces):
            leave(weights[g][p], kept_at[g * pieces + p])
    n = normed.shape[0]
    two = n // halves
    for h in range(halves):
        rows = to_blocks(
            rows_in[2 * h][...].astype(F32), rows_in[2 * h + 1][...].astype(F32), frames_cut
        )
        hat, _ = statistics(rows)
        normed[h * two : (h + 1) * two, :] = (hat * gain[...]).astype(LOW)
    leave(normed, saved_at[0])
    width = weights[0][0].shape[1]
    heads3 = joined.shape[1]

    def project(h, carry):
        for g in range(groups):
            acc = None
            for p in range(pieces):
                wide = normed[rows_of(h, two), columns(off, p, width)]
                term = dot(wide, weights[g][p][:heads3, :], 1, 1)
                acc = term if acc is None else acc + term
            joined[rows_of(h, two, g * n), :] = acc.astype(LOW)
        return carry

    lax.fori_loop(0, halves, project, 0)
    leave(joined, saved_at[1])
    block = two // 2
    inner = heads3 // 3

    def one_block(b, carry):
        at = rows_of(b, block)
        rows3 = joined[at, :]
        parts = []
        for h in range(inner // HEAD_DIM):
            lo = h * HEAD_DIM
            q = rows3[:, lo : lo + HEAD_DIM]
            k = rows3[:, inner + lo : inner + lo + HEAD_DIM]
            v = rows3[:, 2 * inner + lo : 2 * inner + lo + HEAD_DIM]
            s = dot(q * LOW(SCALE), k, 1, 1) + bias[...]
            e = jnp.exp(s - jnp.max(s, axis=-1, keepdims=True))
            w = (e * (1.0 / jnp.sum(e, axis=-1, keepdims=True))).astype(LOW)
            parts.append(dot(w, v, 1, 0))
        out[at, :] = jnp.concatenate(parts, axis=1).astype(LOW)
        return carry

    lax.fori_loop(0, 2 * halves * groups, one_block, 0, unroll=groups)
    leave(out, saved_at[2])

    def finish(h, carry):
        for p in range(pieces):
            acc = None
            for g in range(groups):
                term = dot(out[rows_of(h, two, g * n), :], weights[g][p][heads3:, :], 1, 0)
                acc = term if acc is None else acc + term
            total[rows_of(h, two), columns(off, p, width)] = acc
        return carry

    lax.fori_loop(0, halves, finish, 0)
    store_partial(total, parts_out, frames_cut)
    for copy in copies:
        copy.wait()


def attend_backward_kernel(pieces, halves, groups, frames_cut, *refs):
    off, bias, normed = refs[:3]
    rest = list(refs[3:])
    joined, out = rest.pop(0), rest.pop(0)
    n_head = 9 if frames_cut else 2 * halves
    head = [rest.pop(0) for _ in range(n_head)]
    weights = [[rest.pop(0) for _ in range(pieces)] for _ in range(groups)]
    parts_out = [rest.pop(0) for _ in range(1 + halves)]
    grads = [rest.pop(0) for _ in range(4 if pieces == 2 else 1)]
    if frames_cut:
        carried, gain_grad = rest.pop(0), rest.pop(0)
    upstream = rest.pop(0)
    djoined, dout = rest.pop(0), rest.pop(0)
    total = rest.pop(0)
    n = upstream.shape[0]
    two = n // halves
    half = two // 2
    if frames_cut:
        base_own, base_pair, grad_l, grad_r, far_own, far_pair, gain, cot_own, cot_pair = head
        both = []
        for lo, base, far_sum, cot in (
            (0, base_own, far_own, cot_own),
            (half, base_pair, far_pair, cot_pair),
        ):
            at = slice(lo, lo + half)
            far = slice(half - lo, 2 * half - lo)
            hat, rate = statistics(base[...].astype(F32))
            dn = grad_l[at, :].astype(F32) + grad_r[far, :].astype(F32) + far_sum[...].astype(F32)
            dx = cot[...].astype(F32) + norm_back(dn, gain[...], hat, rate)
            if lo == 0:
                carried[...] = dx
                gain_grad[...] = jnp.sum(dn * hat, axis=0, keepdims=True)
            both.append(dx)
        upstream[...] = to_blocks(both[0], both[1], frames_cut).astype(LOW)
    else:
        for r in range(2 * halves):
            upstream[r * half : (r + 1) * half, :] = head[r][...]
    width = weights[0][0].shape[1]
    heads3 = joined.shape[1]
    inner = heads3 // 3

    def unproject(h, carry):
        for g in range(groups):
            acc = None
            for p in range(pieces):
                dy = upstream[rows_of(h, two), columns(off, p, width)]
                term = dot(dy, weights[g][p][heads3:, :], 1, 1)
                acc = term if acc is None else acc + term
            dout[rows_of(h, two, g * n), :] = acc.astype(LOW)
        return carry

    lax.fori_loop(0, halves, unproject, 0)

    def one_block(b, carry):
        at = rows_of(b, half)
        rows3 = joined[at, :]
        do3 = dout[at, :]
        dqs, dks, dvs = [], [], []
        for h in range(inner // HEAD_DIM):
            lo = h * HEAD_DIM
            q = rows3[:, lo : lo + HEAD_DIM]
            k = rows3[:, inner + lo : inner + lo + HEAD_DIM]
            v = rows3[:, 2 * inner + lo : 2 * inner + lo + HEAD_DIM]
            do = do3[:, lo : lo + HEAD_DIM]
            s = dot(q * LOW(SCALE), k, 1, 1) + bias[...]
            e = jnp.exp(s - jnp.max(s, axis=-1, keepdims=True))
            w = e * (1.0 / jnp.sum(e, axis=-1, keepdims=True))
            dw = dot(do, v, 1, 1)
            ds = (w * (dw - jnp.sum(w * dw, axis=-1, keepdims=True))).astype(LOW)
            dqs.append(dot(ds, k, 1, 0) * SCALE)
            dks.append(dot(ds, q, 0, 0) * SCALE)
            dvs.append(dot(w.astype(LOW), do, 0, 0))
        djoined[at, :] = jnp.concatenate(dqs + dks + dvs, axis=1).astype(LOW)
        return carry

    lax.fori_loop(0, 2 * halves * groups, one_block, 0, unroll=groups)
    chip = off[pieces]
    for p in range(pieces):
        cols = columns(off, p, width)
        wide = normed[:, cols]
        dy = upstream[:, cols]
        for g in range(groups):
            here = slice(g * n, (g + 1) * n)
            value = dot(djoined[here, :], wide, 0, 0).astype(LOW)
            proj = dot(out[here, :], dy, 0, 0).astype(LOW)
            if pieces == 2:
                units = [value[u * inner : (u + 1) * inner] for u in range(3)] + [proj]
                split_store(chip, grads, p, g, units)
            else:
                grads[0][g, :heads3] = value
                grads[0][g, heads3:] = proj

    def finish(h, carry):
        for p in range(pieces):
            acc = None
            for g in range(groups):
                term = dot(djoined[rows_of(h, two, g * n), :], weights[g][p][:heads3, :], 1, 0)
                acc = term if acc is None else acc + term
            total[rows_of(h, two), columns(off, p, width)] = acc
        return carry

    lax.fori_loop(0, halves, finish, 0)
    store_partial(total, parts_out, frames_cut)


def feed_kernel(pieces, packed, *refs):
    off, gain = refs[:2]
    rows_in, cots = refs[2:6], refs[6:10]
    at = 10
    n_w = 2 * pieces * (1 if packed else 2)
    weights = refs[at : at + n_w]
    at += n_w
    out_own, out_send, out_far, dn_near, dn_send, dn_far = refs[at : at + 6]
    at += 6
    n_g = 4 if packed else 2
    grads = refs[at : at + n_g]
    normed, cot, total, dtotal, acts, dhids = refs[at + n_g :]
    n = rows_in[0].shape[0]
    for r in range(4):
        rows_at = slice(r * n, (r + 1) * n)
        hat, _ = statistics(rows_in[r][...].astype(F32))
        normed[rows_at, :] = (hat * gain[...]).astype(LOW)
        cot[rows_at, :] = cots[r][...]
    for c in range(2):
        ups, downs = [], []
        for p in range(pieces):
            if packed:
                w = weights[c * pieces + p]
                wide = w.shape[0] // 2
                ups.append(w[:wide, :])
                downs.append(w[wide:, :])
            else:
                ups.append(weights[2 * (c * pieces + p)][...])
                downs.append(weights[2 * (c * pieces + p) + 1][...])
        width = ups[0].shape[0]
        part = normed.shape[0] // 2

        def some_rows(h, carry):
            here = rows_of(h, part)
            hidden = dact = None
            for p in range(pieces):
                cols = columns(off, p, width)
                term = dot(normed[here, cols], ups[p], 1, 0)
                dterm = dot(cot[here, cols], downs[p], 1, 1)
                hidden = term if hidden is None else hidden + term
                dact = dterm if dact is None else dact + dterm
            cdf = 0.5 * (1.0 + lax.erf(hidden * (2.0**-0.5)))
            act = (hidden * cdf).astype(LOW)
            slope = cdf + hidden * (jnp.exp(-0.5 * hidden * hidden) * (2.0 * jnp.pi) ** -0.5)
            dhid = (dact * slope).astype(LOW)
            acts[here, :] = act
            dhids[here, :] = dhid
            for p in range(pieces):
                cols = columns(off, p, width)
                term = dot(act, downs[p], 1, 0)
                dterm = dot(dhid, ups[p], 1, 1)
                if c == 0:
                    total[here, cols] = term
                    dtotal[here, cols] = dterm
                else:
                    total[here, cols] += term
                    dtotal[here, cols] += dterm
            return carry

        lax.fori_loop(0, 2, some_rows, 0)
        for p in range(pieces):
            cols = columns(off, p, width)
            up_grad = dot(normed[:, cols], dhids[...], 0, 0).astype(LOW)
            down_grad = dot(acts[...], cot[:, cols], 0, 0).astype(LOW)
            if packed:
                grads[2 * p + c][:width, :] = up_grad
                grads[2 * p + c][width:, :] = down_grad
            else:
                grads[0][c] = up_grad
                grads[1][c] = down_grad
    out_own[...] = rows_in[0][...].astype(F32) + total[:n, :]
    out_send[:n, :] = total[n : 2 * n, :].astype(LOW)
    out_send[n:, :] = total[3 * n :, :].astype(LOW)
    out_far[...] = total[2 * n : 3 * n, :].astype(LOW)
    dn_near[...] = dtotal[: 2 * n, :].astype(LOW)
    dn_far[...] = dtotal[2 * n : 3 * n, :].astype(LOW)
    dn_send[...] = dtotal[3 * n :, :].astype(LOW)


def store_parts(rows, outs):
    n = rows.shape[0] // len(outs)
    for d, out in enumerate(outs):
        out[...] = rows[d * n : (d + 1) * n].astype(out.dtype)


def norm_back_kernel(n, firsts, *refs):
    base, gain, carried = refs[n : n + 3]
    outs = refs[n + 3 :]
    rows = base.shape[0]
    hat, rate = statistics(base[...].astype(F32))
    dn = refs[n - 1][firsts[n - 1] : firsts[n - 1] + rows, :].astype(F32)
    for k in range(n - 2, -1, -1):
        dn = refs[k][firsts[k] : firsts[k] + rows, :].astype(F32) + dn
    store_parts(carried[...].astype(F32) + norm_back(dn, gain[...], hat, rate), outs[:-1])
    outs[-1][...] = jnp.sum(dn * hat, axis=0, keepdims=True)


def sum_kernel(n, firsts, *refs):
    outs = refs[n:]
    rows = outs[0].shape[0] * len(outs)
    total = refs[n - 1][firsts[n - 1] : firsts[n - 1] + rows, :].astype(F32)
    for k in range(n - 2, -1, -1):
        total = refs[k][firsts[k] : firsts[k] + rows, :].astype(F32) + total
    store_parts(total, outs)


def in_vmem(n):
    return [pl.BlockSpec(memory_space=VMEM)] * n


def shape_of(shape, dtype):
    return jax.ShapeDtypeStruct(shape, dtype)


def run(kernel, operands, outs, scratch, flops, name, vmem=12, anywhere=0):
    moved = sum(o.size * o.dtype.itemsize for o in operands) + sum(
        o.size * o.dtype.itemsize for o in outs
    )
    scalar = operands[0].dtype == jnp.int32
    specs = in_vmem(len(operands))
    if scalar:
        specs[0] = pl.BlockSpec(memory_space=pltpu.SMEM)
    return pl.pallas_call(
        kernel,
        out_shape=outs,
        in_specs=specs,
        out_specs=in_vmem(len(outs) - anywhere)
        + [pl.BlockSpec(memory_space=pl.ANY)] * anywhere,
        scratch_shapes=scratch,
        compiler_params=pltpu.CompilerParams(vmem_limit_bytes=vmem << 20),
        cost_estimate=pl.CostEstimate(flops=flops, bytes_accessed=moved, transcendentals=0),
        name=name,
    )(*operands)


def after(value, *tokens):
    return lax.optimization_barrier((value, *tokens))[0]


def body(sizes, tokens, norm_gains, temporal_qkv, temporal_proj, spatial_qkv, spatial_proj, up_weight, down_weight, cotangent):
    n_fsdp, n_ctx, n_tp = sizes
    swap = n_fsdp == 2
    d_model = tokens.shape[3]
    d_part = d_model // n_fsdp
    places = tokens.shape[0]
    block = 2 * (-(-places // 4))
    x, i, z = lax.axis_index("fsdp"), lax.axis_index("ctx"), lax.axis_index("tp")
    core, chip = i % 2, i // 2
    is_source = (z // 2) == core

    def permute_ctx(v, bits):
        return lax.ppermute(v, "ctx", [(a, a ^ bits) for a in range(n_ctx)])

    def permute_tp(v, bits):
        return lax.ppermute(v, "tp", [(a, a ^ bits) for a in range(n_tp)])

    def permute_fsdp(v):
        return lax.ppermute(v, "fsdp", [(0, 1), (1, 0)])

    def along(v, bits, back=False):
        pairs = []
        for a in range(n_ctx):
            for b in (2 * (a % 2), 2 * (a % 2) + 1):
                there, here = a * n_tp + (b ^ bits), a * n_tp + b
                pairs.append((there, here) if back else (here, there))
        return lax.ppermute(v, ("ctx", "tp"), pairs)

    def exclusive(parts, bits):
        low, high = (bits & 1) == 1, (bits & 2) == 2
        parts = [jnp.where(low, parts[d ^ 1], parts[d]) for d in range(4)]
        return [jnp.where(high, parts[d ^ 2], parts[d]) for d in range(4)]

    slot_bits = (z & 2) | ((z & 1) ^ core)
    part_rows = 2 * block

    def to_time(rows):
        t = jnp.transpose(rows, (2, 1, 0, 3))
        t = jnp.pad(t, ((0, 0), (0, 0), (0, 2 * block - places), (0, 0)))
        parts = [t[c, :, b * block : (b + 1) * block] for c in range(2) for b in range(2)]
        parts = exclusive([v.reshape(part_rows, d_model) for v in parts], i)
        got = [parts[0]] + [permute_ctx(parts[e], e) for e in range(1, 4)]
        return exclusive(got, slot_bits)

    def time_sends(own):
        parts = exclusive(own, slot_bits)
        return [parts[0]] + [permute_ctx(parts[e], e) for e in range(1, 4)]

    def time_finish(got):
        got = [v.reshape(2, block, d_model) for v in exclusive(got, i)]
        t = jnp.stack(
            [jnp.concatenate((got[2 * c], got[2 * c + 1]), axis=1)[:, :places] for c in range(2)]
        )
        return jnp.transpose(t, (2, 1, 0, 3))

    def turn(own):
        return [own[0]] + [permute_tp(own[e], e) for e in range(1, 4)]

    rows_n = 8 * block
    flat = (rows_n, d_model)

    def attention_pack(qkv, proj):
        return jnp.concatenate((jnp.transpose(qkv, (1, 2, 0)).reshape(-1, d_part), proj), axis=0)

    def spread_first(shard):
        return jnp.where(is_source, shard, along(shard, 2))

    hid_half = up_weight.shape[1] // 2

    def feed_pack():
        up = lax.dynamic_slice_in_dim(up_weight, chip * hid_half, hid_half, axis=1)
        down = lax.dynamic_slice_in_dim(down_weight, chip * hid_half, hid_half, axis=0)
        return jnp.concatenate((up, down.reshape(d_part, hid_half)), axis=0)

    def feed_full(shard):
        every = lax.all_gather(shard, "fsdp", axis=0)
        up = every[:, :d_part].reshape(d_model, hid_half)
        down = every[:, d_part:].reshape(n_fsdp, hid_half, d_part)
        return [up, jnp.transpose(down, (1, 0, 2)).reshape(hid_half, d_model)]

    def owner_sum(a, b):
        mine = a + permute_tp(b, 1)
        return mine + along(mine, 2, True)

    def other_half(v):
        pairs = []
        for a in range(n_ctx):
            for b in (2 * (a % 2), 2 * (a % 2) + 1):
                pairs.append((a * n_tp + b, (a ^ 2) * n_tp + b))
        return lax.ppermute(v, ("ctx", "tp"), pairs)

    def owner_sends(a, b):
        return along(a, 2, True), along(b, 3, True), along(b, 1)

    def ordered(mine, other):
        return jnp.stack((jnp.where(chip == 0, mine, other), jnp.where(chip == 0, other, mine)))

    def to_pair(both):
        return jnp.where(is_source, both, permute_ctx(both, 1))

    def to_both(mine):
        return to_pair(ordered(mine, permute_ctx(mine, 2)))

    def first_sends(grads):
        send_x, _, send_y, _ = grads
        return permute_fsdp(send_x), permute_ctx(send_y, 2)

    def first_sums(grads, got):
        _, keep_x, _, keep_y = grads
        by_x, by_y = keep_x + got[0], keep_y + got[1]
        return (by_x[0], by_y[0]), (by_x[1], by_y[1])

    def second_sends(send):
        return permute_ctx(send[0], 2), permute_fsdp(send[1])

    def second_sums(keep, got):
        by_x, by_y = keep[0] + got[0], keep[1] + got[1]
        return [jnp.stack((by_x[g], by_y[g])) for g in range(by_x.shape[0])]

    def attention_out(total):
        joined_grad = jnp.stack((total[0, 0], total[1, 0], total[0, 1])).astype(F32)
        return jnp.transpose(joined_grad, (2, 0, 1)), total[1, 1].astype(F32)

    def feed_out(total):
        up = jnp.concatenate((total[0, :d_part], total[1, :d_part]), axis=1)
        down = jnp.concatenate((total[0, d_part:], total[1, d_part:]), axis=0)
        return up.astype(F32), down.astype(F32)

    def attention_grads_wide(grads):
        total = lax.psum_scatter(grads[0], "fsdp", scatter_dimension=2, tiled=True)
        total = total + permute_ctx(total, 2)
        if total.shape[0] == 2:
            mine = owner_sum(total[0], total[1])
        else:
            mine = total[0] + along(total[0], 2, True)
        full = jnp.where(is_source, mine, permute_ctx(mine, 1)).astype(F32)
        inner = full.shape[0] // 4
        joined_grad = full[: 3 * inner].reshape(3, inner, d_part)
        return jnp.transpose(joined_grad, (2, 0, 1)), full[3 * inner :]

    def feed_grads_wide(grads):
        up = lax.psum_scatter(grads[0], "fsdp", scatter_dimension=1, tiled=True)
        down = lax.psum_scatter(grads[1], "fsdp", scatter_dimension=2, tiled=True)
        up = to_both(owner_sum(up[0], up[1]))
        down = to_both(owner_sum(down[0], down[1]))
        return (
            jnp.concatenate((up[0], up[1]), axis=1).astype(F32),
            jnp.concatenate((down[0], down[1]), axis=0).astype(F32),
        )

    pieces = 2 if swap else 1
    width = d_model // pieces
    if swap:
        offsets = jnp.stack((x * width, (1 - x) * width, chip)).astype(jnp.int32)
    else:
        offsets = jnp.stack((0 * chip, chip)).astype(jnp.int32)

    at = jnp.arange(rows_n, dtype=jnp.int32)
    far = jnp.float32(-1e30)
    bias_t = jnp.where((at % block)[:, None] == (at % block)[None, :], 0.0, far).astype(F32)
    owner = jnp.where(at < rows_n // 2, core, 1 - core)
    real = owner * block + at % block < places
    bias_s = jnp.broadcast_to(jnp.where(real, 0.0, far).astype(F32)[None], (rows_n, rows_n))

    two = (2 * rows_n, d_model)
    unit = 2 * rows_n * d_model * d_model

    inner = temporal_qkv.shape[2]

    def shapes(rows, groups):
        all_rows = len(rows) * rows_n
        return (all_rows, d_model), [(groups * all_rows, 3 * inner)], [(groups * all_rows, inner)]

    def part_shapes(rows):
        if len(rows) == 2:
            return [shape_of(flat, LOW)] * 2
        return [shape_of(flat, LOW)] * 2 + [shape_of(two, LOW)]

    def attend_forward(rows, gain, bias, weights, cut, name):
        groups = len(weights) // pieces
        wide, joined, heads = shapes(rows, groups)
        kept = [shape_of(s, LOW) for s in (wide, *joined, *heads)]
        kept += [shape_of(w.shape, LOW) for w in weights]
        outs = part_shapes(rows) + kept
        got = run(
            functools.partial(attend_forward_kernel, pieces, len(rows) // 2, groups, cut),
            [offsets, *rows, gain, bias, *weights],
            outs,
            [VMEM(s, LOW) for s in (wide, *joined, *heads)]
            + [VMEM(wide, F32), pltpu.SemaphoreType.DMA((len(kept),))],
            6 * unit,
            name,
            16,
            len(kept),
        )
        n = len(part_shapes(rows))
        m = n + 3
        return got[:n], got[n:m], got[m:]

    def attend_backward(rows, saved, bias, head, weights, cut, name):
        groups = len(weights) // pieces
        wide, joined, heads = shapes(rows, groups)
        outs = part_shapes(rows)
        n = len(outs)
        if swap:
            outs += [shape_of((2, groups, inner, width), LOW)] * 4
        else:
            outs += [shape_of((groups, 4 * inner, width), LOW)]
        m = len(outs)
        if cut:
            outs += [shape_of(flat, F32), shape_of((1, d_model), F32)]
        got = run(
            functools.partial(attend_backward_kernel, pieces, len(rows) // 2, groups, cut),
            [offsets, bias, *saved, *head, *weights],
            outs,
            [VMEM(s, LOW) for s in (wide, *joined, *heads)] + [VMEM(wide, F32)],
            12 * unit,
            name,
        )
        return got[:n], got[n:m], got[m:]

    def norm_backward(terms, base, gain, carried, name):
        *parts, gain_grad = run(
            functools.partial(norm_back_kernel, len(terms), [lo for _, lo in terms]),
            [v for v, _ in terms] + [base, gain, carried],
            [shape_of((part_rows, d_model), LOW)] * 4 + [shape_of((1, d_model), F32)],
            [],
            20 * rows_n * d_model,
            name,
        )
        return parts, gain_grad

    def sum_parts(terms, name, n=4):
        return run(
            functools.partial(sum_kernel, len(terms), [lo for _, lo in terms]),
            [v for v, _ in terms],
            [shape_of((rows_n // n, d_model), LOW)] * n,
            [],
            4 * rows_n * d_model,
            name,
        )

    def other_x(v):
        return permute_fsdp(v) if swap else lax.all_gather(v, "fsdp", axis=1, tiled=True)

    def joined_pieces(first, first_x, second, second_x):
        return [first, first_x, second, second_x] if swap else [first_x, second_x]

    barrier = lax.optimization_barrier

    pack_t = attention_pack(temporal_qkv, temporal_proj)
    got_first_t = along(pack_t, 2)
    pack_s = attention_pack(spatial_qkv, spatial_proj)
    pack_f = feed_pack()
    if swap:
        gain_other = permute_fsdp(norm_gains)
        gains = jnp.where(
            x == 0,
            jnp.concatenate((norm_gains, gain_other), axis=1),
            jnp.concatenate((gain_other, norm_gains), axis=1),
        ).astype(F32)
    else:
        gains = lax.all_gather(norm_gains, "fsdp", axis=1, tiled=True).astype(F32)
    start = jnp.concatenate(to_time(tokens), axis=0)
    got_first_t, start, pack_s, pack_f, gains, cot = barrier(
        (got_first_t, start, pack_s, pack_f, gains, cotangent)
    )
    first_t = jnp.where(is_source, pack_t, got_first_t)
    first_tx = other_x(first_t)
    weights_t = [first_t, first_tx] if swap else [first_tx]
    near_start = permute_tp(start, 1)
    rows_t = [start, permute_ctx(start, 1), near_start, permute_ctx(near_start, 1)]
    got_first_s = along(pack_s, 2)
    cot_time = jnp.concatenate(to_time(cot), axis=0)
    first_tx, rows_t, got_first_s, cot_time = barrier((first_tx, rows_t, got_first_s, cot_time))
    first_s = jnp.where(is_source, pack_s, got_first_s)
    weights_t = [first_t, first_tx] if swap else [first_tx]

    second_s = permute_tp(first_s, 1)
    first_sx = other_x(first_s)
    parts_t, saved_t, weights_t = attend_forward(
        rows_t, gains[0:1], bias_t, weights_t, False, "time_forward"
    )
    parts_t, second_s, first_sx, pack_f, cot_time = barrier(
        (parts_t, second_s, first_sx, pack_f, cot_time)
    )
    got_t = permute_ctx(parts_t[2], 1)
    (chip_t,) = sum_parts(((parts_t[1], 0), (got_t, rows_n)), "time_near", 1)
    near_t = permute_tp(chip_t, 1)
    far_cot_time = permute_ctx(after(cot_time, chip_t), 2)
    got_first_f = along(after(pack_f, chip_t), 2)
    second_sx = other_x(second_s)
    sums = sum_parts(((start, 0), (parts_t[0], 0), (got_t, 0), (near_t, 0)), "time_sum")
    sums, far_cot_time, got_first_f = barrier((sums, far_cot_time, got_first_f))
    own1 = jnp.concatenate(turn(sums), axis=0)
    own1, second_sx = barrier((own1, second_sx))
    pair1 = permute_ctx(own1, 1)
    first_f = jnp.where(is_source, pack_f, got_first_f)
    pair1, first_f = barrier((pair1, first_f))
    weights_s = joined_pieces(first_s, first_sx, second_s, second_sx)

    second_f = permute_tp(first_f, 1)
    if swap:
        first_fx = permute_fsdp(first_f)
    parts_s, saved_s, weights_s = attend_forward(
        [own1, pair1], gains[1:2], bias_s, weights_s, True, "space_forward"
    )
    back_s = permute_ctx(parts_s[1], 1)
    (own2,) = sum_parts(((own1, 0), (parts_s[0], 0), (back_s, 0)), "space_sum", 1)
    if swap:
        second_f, first_fx, own2 = barrier((second_f, first_fx, own2))
        second_fx = permute_fsdp(second_f)
        weights_f = [first_f, first_fx, second_f, second_fx]
    else:
        weights_f = [w for v in (first_f, second_f) for w in feed_full(v)]
    far_own2 = permute_ctx(own2, 2)
    rows_f = [own2, permute_ctx(own2, 1), far_own2, permute_ctx(far_own2, 1)]

    both_cot = []
    for d in range(4):
        at_d = slice(d * part_rows, (d + 1) * part_rows)
        both_cot.append(jnp.concatenate((cot_time[at_d], far_cot_time[at_d]), axis=0))
    both_cot = turn(after(both_cot, own2))
    if swap:
        both_cot, second_fx = barrier((both_cot, second_fx))
        weights_f = [first_f, first_fx, second_f, second_fx]
    cot_own = jnp.concatenate([v[:part_rows] for v in both_cot], axis=0)
    far_cot = jnp.concatenate([v[part_rows:] for v in both_cot], axis=0)
    cots = [cot_own, permute_ctx(cot_own, 1), far_cot, permute_ctx(far_cot, 1)]

    if swap:
        outs_f = [shape_of((2 * width, hid_half), LOW)] * 4
    else:
        outs_f = [shape_of((2, width, hid_half), LOW), shape_of((2, hid_half, width), LOW)]
    four = (4 * rows_n, d_model)
    out_own, out_send, out_far, dn3, dn3_send, dn3_far, *grads_f = run(
        functools.partial(feed_kernel, pieces, swap),
        [offsets, gains[2:3], *rows_f, *cots, *weights_f],
        [
            shape_of(flat, F32),
            shape_of(two, LOW),
            shape_of(flat, LOW),
            shape_of(two, LOW),
            shape_of(flat, LOW),
            shape_of(flat, LOW),
            *outs_f,
        ],
        [VMEM(four, LOW), VMEM(four, LOW), VMEM(four, F32), VMEM(four, F32)]
        + [VMEM((4 * rows_n, hid_half), LOW)] * 2,
        24 * unit,
        "feed",
        20,
    )
    (chip_sum,) = sum_parts(((dn3_far, 0), (permute_ctx(dn3_send, 1), 0)), "feed_near", 1)
    far3 = permute_ctx(chip_sum, 2)
    far3_pair = permute_ctx(far3, 1)
    got3 = permute_ctx(dn3, 1)
    if swap:
        got_f = permute_fsdp(grads_f[3])
        got_f, far3_pair = barrier((got_f, far3_pair))
        b_f = grads_f[1] + got_f
        got_f = permute_fsdp(grads_f[2])
        add_f = permute_tp(b_f, 1)
    got_out = permute_ctx(out_send, 1)
    (chip_out,) = sum_parts(((out_far, 0), (got_out, rows_n)), "feed_out_near", 1)
    far_out = permute_ctx(after(chip_out, far3), 2)

    parts_s, grads_s, (carried2, gain3) = attend_backward(
        [own1, pair1],
        saved_s,
        bias_s,
        [rows_f[0], rows_f[1], dn3, got3, far3, far3_pair, gains[2:3], cots[0], cots[1]],
        weights_s,
        True,
        "space_backward",
    )
    if swap:
        parts_s, far_out, got_f, add_f = barrier((parts_s, far_out, got_f, add_f))
    got2 = permute_ctx(parts_s[1], 1)
    parts1, gain2 = norm_backward(
        ((parts_s[0], 0), (got2, 0)), own1, gains[1:2], carried2, "space_norm"
    )
    own_t = jnp.concatenate(turn(parts1), axis=0)
    near_own_t = permute_tp(own_t, 1)
    head_t = [own_t, permute_ctx(own_t, 1), near_own_t, permute_ctx(near_own_t, 1)]
    out_parts = sum_parts(((out_own, 0), (got_out, 0), (far_out, 0)), "feed_sum")
    if not swap:
        out_time = turn(out_parts)
    if swap:
        got_sums_s = first_sends(grads_s)
        keep_s, send_s = first_sums(grads_s, after(got_sums_s, own_t))
        got_sums_s = second_sends(send_s)
        a_f = grads_f[0] + got_f + add_f
        add_f = along(after(a_f, near_own_t), 2, True)

    parts_t, grads_t, _ = attend_backward(
        rows_t, saved_t, bias_t, head_t, weights_t, False, "time_backward"
    )
    if swap:
        parts_t, grads_t, got_sums_s, add_f, gain2, out_parts = barrier(
            (parts_t, grads_t, got_sums_s, add_f, gain2, out_parts)
        )
        got_sums_t = first_sends(grads_t)
        sums_s = second_sums(keep_s, got_sums_s)
        add_s = permute_tp(sums_s[1], 1)
    got1 = permute_ctx(parts_t[2], 1)
    (chip1,) = sum_parts(((parts_t[1], 0), (got1, rows_n)), "time_back_near", 1)
    near1 = permute_tp(chip1, 1)
    if swap:
        got_sums_t, near1, add_s = barrier((got_sums_t, near1, add_s))
        keep_t, send_t = first_sums(grads_t, got_sums_t)
        got_sums_t = second_sends(send_t)
    parts0, gain1 = norm_backward(
        ((parts_t[0], 0), (got1, 0), (near1, 0)), start, gains[0:1], own_t, "time_norm"
    )
    gain_all = jnp.concatenate((gain1, gain2, gain3), axis=0)
    if swap:
        a_s = sums_s[0] + add_s
        add_s = along(a_s, 2, True)
        total_f = a_f + add_f
        other_f = other_half(total_f)
        gain_got = permute_ctx(gain_all, 1)
        got_sums_t, add_s, other_f, gain_got = barrier((got_sums_t, add_s, other_f, gain_got))

        def across(v, axes, first, second):
            n = (n_fsdp if axes[0] == "fsdp" else n_ctx, n_tp)
            cells = [(a, b) for a in range(n[0]) for b in range(n[1])]
            pairs = [(a * n[1] + b, (a ^ first) * n[1] + (b ^ second)) for a, b in cells]
            return lax.ppermute(v, axes, pairs)

        (a_t,) = second_sums(keep_t, got_sums_t)
        got_t = along(a_t, 2, True)
        total_s = a_s + add_s
        other_s = other_half(total_s)
        gain_all = gain_all + gain_got
        gain_got = [across(gain_all, ("fsdp", "tp"), *d) for d in ((0, 1), (1, 0), (1, 1))]
        out_time = turn(out_parts)
        got_t, other_s, gain_got, parts0, out_time = barrier(
            (got_t, other_s, gain_got, parts0, out_time)
        )
        total_t = a_t + got_t
        other_t = other_half(total_t)
        gain_all = gain_all + gain_got[0] + (gain_got[1] + gain_got[2])
        gain_got = [across(gain_all, ("ctx", "tp"), *d) for d in ((0, 2), (2, 0), (2, 2))]
        both_f, both_s = ordered(total_f, other_f), ordered(total_s, other_s)
        up_grad, down_grad = feed_out(to_pair(both_f))
        s_qkv, s_proj = attention_out(to_pair(both_s))
        both_rows = [jnp.concatenate(pair, axis=0) for pair in zip(out_time, parts0)]
        got_both = time_sends(both_rows)
        other_t, gain_got, got_both, up_grad, down_grad, s_qkv, s_proj = barrier(
            (other_t, gain_got, got_both, up_grad, down_grad, s_qkv, s_proj)
        )
        both_t = ordered(total_t, other_t)
        pair_t = permute_ctx(both_t, 1)
        gain_all = gain_all + gain_got[0] + (gain_got[1] + gain_got[2])
        block_out = time_finish([v[:part_rows] for v in got_both])
        tokens_grad = time_finish([v[part_rows:] for v in got_both]).astype(F32)
        t_qkv, t_proj = attention_out(jnp.where(is_source, both_t, pair_t))
        gain_grads = lax.dynamic_slice_in_dim(gain_all, x * d_part, d_part, axis=1)
    else:
        tokens_grad = time_finish(time_sends(parts0)).astype(F32)
        block_out = time_finish(time_sends(out_time))
        up_grad, down_grad = feed_grads_wide(grads_f)
        s_qkv, s_proj = attention_grads_wide(grads_s)
        t_qkv, t_proj = attention_grads_wide(grads_t)
        for bits in (1, 2):
            gain_all = gain_all + permute_ctx(gain_all, bits)
        for bits in (1, 2):
            gain_all = gain_all + permute_tp(gain_all, bits)
        gain_grads = lax.psum_scatter(gain_all, "fsdp", scatter_dimension=1, tiled=True)
    return (
        block_out,
        tokens_grad,
        gain_grads,
        t_qkv,
        t_proj,
        s_qkv,
        s_proj,
        up_grad,
        down_grad,
    )


def solution(mesh):
    rows = P("tp", "ctx", "fsdp", None)
    weights = (
        P(None, "fsdp"),
        P("fsdp", None, "tp"),
        P("tp", "fsdp"),
        P("fsdp", None, "tp"),
        P("tp", "fsdp"),
        P("fsdp", "tp"),
        P("tp", "fsdp"),
    )
    sizes = (mesh.shape["fsdp"], mesh.shape["ctx"], mesh.shape["tp"])
    return jax.shard_map(
        functools.partial(body, sizes),
        mesh=mesh,
        in_specs=(rows, *weights, rows),
        out_specs=(rows, rows, *weights),
        check_vma=False,
    )
```

```python
import functools

import jax
import jax.numpy as jnp
from jax import lax
from jax.experimental import pallas as pl
from jax.experimental.pallas import tpu as pltpu
from jax.sharding import PartitionSpec as P

HEAD_DIM = 64
EPSILON = 1e-06
SCALE = HEAD_DIM ** (-0.5)
F32 = jnp.float32
LOW = jnp.bfloat16
VMEM = pltpu.VMEM


def dot(a, b, ca, cb):
    return lax.dot_general(a, b, (((ca,), (cb,)), ((), ())), preferred_element_type=F32)


def statistics(rows):
    center = rows - jnp.mean(rows, axis=-1, keepdims=True)
    rate = lax.rsqrt(jnp.mean(center * center, axis=-1, keepdims=True) + EPSILON)
    return center * rate, rate


def norm_back(grad, gain, hat, rate):
    t = grad * gain
    return rate * (
        t
        - jnp.mean(t, axis=-1, keepdims=True)
        - hat * jnp.mean(t * hat, axis=-1, keepdims=True)
    )


def to_blocks(own, pair, frames_cut):
    if not frames_cut:
        return jnp.concatenate((own, pair), axis=0)
    n = own.shape[0] // 8
    return jnp.concatenate(
        [
            rows[(2 * d + f) * n : (2 * d + f + 1) * n]
            for f in range(2)
            for rows in (own, pair)
            for d in range(4)
        ],
        axis=0,
    )


def from_blocks(rows, frames_cut):
    half = rows.shape[0] // 2
    if not frames_cut:
        return rows[:half], rows[half:]
    n = half // 8
    return tuple(
        jnp.concatenate(
            [
                rows[f * half + (4 * side + d) * n : f * half + (4 * side + d + 1) * n]
                for d in range(4)
                for f in range(2)
            ],
            axis=0,
        )
        for side in range(2)
    )


def split_store(chip, refs, piece, group, units):
    send_x, keep_x, send_y, keep_y = refs
    to_x = keep_x if piece == 0 else send_x
    to_x[0, group] = jnp.where(chip == 0, units[0], units[1])
    to_x[1, group] = jnp.where(chip == 0, units[1], units[0])
    keep_y[piece, group] = jnp.where(chip == 0, units[2], units[3])
    send_y[piece, group] = jnp.where(chip == 0, units[3], units[2])


def columns(off_ref, piece, width):
    return pl.ds(pl.multiple_of(off_ref[piece], 128), width)


def store_partial(total, outs, frames_cut):
    n, halves = total.shape[0], len(outs) - 1
    first, second = from_blocks(total[: n // halves, :], frames_cut)
    outs[0][...] = first.astype(LOW)
    if halves == 1:
        outs[1][...] = second.astype(LOW)
        return
    half = n // 4
    outs[2][:half, :] = second.astype(LOW)
    first, second = from_blocks(total[n // 2 :, :], frames_cut)
    outs[1][...] = first.astype(LOW)
    outs[2][half:, :] = second.astype(LOW)


def attend_forward_kernel(pieces, halves, groups, frames_cut, *refs):
    off = refs[0]
    rows_in = refs[1 : 1 + 2 * halves]
    rest = list(refs[1 + 2 * halves :])
    gain, bias = rest.pop(0), rest.pop(0)
    weights = [[rest.pop(0) for _ in range(pieces)] for _ in range(groups)]
    parts_out = [rest.pop(0) for _ in range(1 + halves)]
    saved_at = [rest.pop(0) for _ in range(1 + 2 * groups)]
    kept_at = [rest.pop(0) for _ in range(groups * pieces)]
    normed = rest.pop(0)
    joined, out = [rest.pop(0) for _ in range(groups)], [rest.pop(0) for _ in range(groups)]
    total, sems = rest
    copies = []

    def leave(source, target):
        copy = pltpu.make_async_copy(source, target, sems.at[len(copies)])
        copy.start()
        copies.append(copy)

    for g in range(groups):
        for p in range(pieces):
            leave(weights[g][p], kept_at[g * pieces + p])
    two = normed.shape[0] // halves
    for h in range(halves):
        rows = to_blocks(
            rows_in[2 * h][...].astype(F32), rows_in[2 * h + 1][...].astype(F32), frames_cut
        )
        hat, _ = statistics(rows)
        normed[h * two : (h + 1) * two, :] = (hat * gain[...]).astype(LOW)
    leave(normed, saved_at[0])
    width = weights[0][0].shape[1]
    heads3 = joined[0].shape[1]
    for g in range(groups):
        acc = None
        for p in range(pieces):
            term = dot(normed[:, columns(off, p, width)], weights[g][p][:heads3, :], 1, 1)
            acc = term if acc is None else acc + term
        joined[g][...] = acc.astype(LOW)
        leave(joined[g], saved_at[1 + g])
    block = two // 2
    inner = heads3 // 3

    def one_block(b, carry):
        at = pl.ds(pl.multiple_of(b * block, 16), block)
        for g in range(groups):
            rows3 = joined[g][at, :]
            parts = []
            for h in range(inner // HEAD_DIM):
                lo = h * HEAD_DIM
                q = rows3[:, lo : lo + HEAD_DIM]
                k = rows3[:, inner + lo : inner + lo + HEAD_DIM]
                v = rows3[:, 2 * inner + lo : 2 * inner + lo + HEAD_DIM]
                s = dot(q * LOW(SCALE), k, 1, 1) + bias[...]
                e = jnp.exp(s - jnp.max(s, axis=-1, keepdims=True))
                w = (e * (1.0 / jnp.sum(e, axis=-1, keepdims=True))).astype(LOW)
                parts.append(dot(w, v, 1, 0))
            out[g][at, :] = jnp.concatenate(parts, axis=1).astype(LOW)
        return carry

    lax.fori_loop(0, 2 * halves, one_block, 0, unroll=halves)
    for g in range(groups):
        leave(out[g], saved_at[1 + groups + g])
    for p in range(pieces):
        acc = dot(out[0][...], weights[0][p][heads3:, :], 1, 0)
        for g in range(1, groups):
            acc = acc + dot(out[g][...], weights[g][p][heads3:, :], 1, 0)
        total[:, columns(off, p, width)] = acc
    store_partial(total, parts_out, frames_cut)
    for copy in copies:
        copy.wait()


def attend_backward_kernel(pieces, halves, groups, frames_cut, *refs):
    off, bias, normed = refs[:3]
    rest = list(refs[3:])
    joined, out = [rest.pop(0) for _ in range(groups)], [rest.pop(0) for _ in range(groups)]
    n_head = 9 if frames_cut else 2 * halves
    head = [rest.pop(0) for _ in range(n_head)]
    weights = [[rest.pop(0) for _ in range(pieces)] for _ in range(groups)]
    parts_out = [rest.pop(0) for _ in range(1 + halves)]
    grads = [rest.pop(0) for _ in range(4 if pieces == 2 else 1)]
    if frames_cut:
        carried, gain_grad = rest.pop(0), rest.pop(0)
    upstream = rest.pop(0)
    djoined, dout = [rest.pop(0) for _ in range(groups)], [rest.pop(0) for _ in range(groups)]
    total = rest.pop(0)
    two = upstream.shape[0] // halves
    half = two // 2
    if frames_cut:
        base_own, base_pair, grad_l, grad_r, far_own, far_pair, gain, cot_own, cot_pair = head
        both = []
        for lo, base, far_sum, cot in (
            (0, base_own, far_own, cot_own),
            (half, base_pair, far_pair, cot_pair),
        ):
            at = slice(lo, lo + half)
            far = slice(half - lo, 2 * half - lo)
            hat, rate = statistics(base[...].astype(F32))
            dn = grad_l[at, :].astype(F32) + grad_r[far, :].astype(F32) + far_sum[...].astype(F32)
            dx = cot[...].astype(F32) + norm_back(dn, gain[...], hat, rate)
            if lo == 0:
                carried[...] = dx
                gain_grad[...] = jnp.sum(dn * hat, axis=0, keepdims=True)
            both.append(dx)
        upstream[...] = to_blocks(both[0], both[1], frames_cut).astype(LOW)
    else:
        for r in range(2 * halves):
            upstream[r * half : (r + 1) * half, :] = head[r][...]
    width = weights[0][0].shape[1]
    heads3 = joined[0].shape[1]
    inner = heads3 // 3
    for g in range(groups):
        acc = None
        for p in range(pieces):
            term = dot(upstream[:, columns(off, p, width)], weights[g][p][heads3:, :], 1, 1)
            acc = term if acc is None else acc + term
        dout[g][...] = acc.astype(LOW)

    def one_block(b, carry):
        at = pl.ds(pl.multiple_of(b * half, 16), half)
        for g in range(groups):
            rows3 = joined[g][at, :]
            do3 = dout[g][at, :]
            dqs, dks, dvs = [], [], []
            for h in range(inner // HEAD_DIM):
                lo = h * HEAD_DIM
                q = rows3[:, lo : lo + HEAD_DIM]
                k = rows3[:, inner + lo : inner + lo + HEAD_DIM]
                v = rows3[:, 2 * inner + lo : 2 * inner + lo + HEAD_DIM]
                do = do3[:, lo : lo + HEAD_DIM]
                s = dot(q * LOW(SCALE), k, 1, 1) + bias[...]
                e = jnp.exp(s - jnp.max(s, axis=-1, keepdims=True))
                w = e * (1.0 / jnp.sum(e, axis=-1, keepdims=True))
                dw = dot(do, v, 1, 1)
                ds = (w * (dw - jnp.sum(w * dw, axis=-1, keepdims=True))).astype(LOW)
                dqs.append(dot(ds, k, 1, 0) * SCALE)
                dks.append(dot(ds, q, 0, 0) * SCALE)
                dvs.append(dot(w.astype(LOW), do, 0, 0))
            djoined[g][at, :] = jnp.concatenate(dqs + dks + dvs, axis=1).astype(LOW)
        return carry

    lax.fori_loop(0, 2 * halves, one_block, 0, unroll=3 - halves)
    chip = off[pieces]
    for p in range(pieces):
        cols = columns(off, p, width)
        wide = normed[:, cols]
        dy = upstream[:, cols]
        acc = None
        for g in range(groups):
            value = dot(djoined[g][...], wide, 0, 0).astype(LOW)
            proj = dot(out[g][...], dy, 0, 0).astype(LOW)
            if pieces == 2:
                units = [value[u * inner : (u + 1) * inner] for u in range(3)] + [proj]
                split_store(chip, grads, p, g, units)
            else:
                grads[0][g, :heads3] = value
                grads[0][g, heads3:] = proj
            term = dot(djoined[g][...], weights[g][p][:heads3, :], 1, 0)
            acc = term if acc is None else acc + term
        total[:, cols] = acc
    store_partial(total, parts_out, frames_cut)


def feed_kernel(pieces, packed, *refs):
    off, gain = refs[:2]
    rows_in, cots = refs[2:6], refs[6:10]
    at = 10
    n_w = 2 * pieces * (1 if packed else 2)
    weights = refs[at : at + n_w]
    at += n_w
    out_own, out_send, out_far, dn_near, dn_send, dn_far = refs[at : at + 6]
    at += 6
    n_g = 4 if packed else 2
    grads = refs[at : at + n_g]
    normed, cot, total, dtotal = refs[at + n_g :]
    n = rows_in[0].shape[0]
    for r in range(4):
        rows_at = slice(r * n, (r + 1) * n)
        hat, _ = statistics(rows_in[r][...].astype(F32))
        normed[rows_at, :] = (hat * gain[...]).astype(LOW)
        cot[rows_at, :] = cots[r][...]
    for c in range(2):
        ups, downs = [], []
        for p in range(pieces):
            if packed:
                w = weights[c * pieces + p]
                wide = w.shape[0] // 2
                ups.append(w[:wide, :])
                downs.append(w[wide:, :])
            else:
                ups.append(weights[2 * (c * pieces + p)][...])
                downs.append(weights[2 * (c * pieces + p) + 1][...])
        width = ups[0].shape[0]
        hidden = dact = None
        for p in range(pieces):
            cols = columns(off, p, width)
            term = dot(normed[:, cols], ups[p], 1, 0)
            dterm = dot(cot[:, cols], downs[p], 1, 1)
            hidden = term if hidden is None else hidden + term
            dact = dterm if dact is None else dact + dterm
        cdf = 0.5 * (1.0 + lax.erf(hidden * (2.0**-0.5)))
        act = (hidden * cdf).astype(LOW)
        slope = cdf + hidden * (jnp.exp(-0.5 * hidden * hidden) * (2.0 * jnp.pi) ** -0.5)
        dhid = (dact * slope).astype(LOW)
        for p in range(pieces):
            cols = columns(off, p, width)
            term = dot(act, downs[p], 1, 0)
            dterm = dot(dhid, ups[p], 1, 1)
            if c == 0:
                total[:, cols] = term
                dtotal[:, cols] = dterm
            else:
                total[:, cols] += term
                dtotal[:, cols] += dterm
            up_grad = dot(normed[:, cols], dhid, 0, 0).astype(LOW)
            down_grad = dot(act, cot[:, cols], 0, 0).astype(LOW)
            if packed:
                grads[2 * p + c][:width, :] = up_grad
                grads[2 * p + c][width:, :] = down_grad
            else:
                grads[0][c] = up_grad
                grads[1][c] = down_grad
    out_own[...] = rows_in[0][...].astype(F32) + total[:n, :]
    out_send[:n, :] = total[n : 2 * n, :].astype(LOW)
    out_send[n:, :] = total[3 * n :, :].astype(LOW)
    out_far[...] = total[2 * n : 3 * n, :].astype(LOW)
    dn_near[...] = dtotal[: 2 * n, :].astype(LOW)
    dn_far[...] = dtotal[2 * n : 3 * n, :].astype(LOW)
    dn_send[...] = dtotal[3 * n :, :].astype(LOW)


def store_parts(rows, outs):
    n = rows.shape[0] // len(outs)
    for d, out in enumerate(outs):
        out[...] = rows[d * n : (d + 1) * n].astype(out.dtype)


def norm_back_kernel(n, firsts, *refs):
    base, gain, carried = refs[n : n + 3]
    outs = refs[n + 3 :]
    rows = base.shape[0]
    hat, rate = statistics(base[...].astype(F32))
    dn = refs[n - 1][firsts[n - 1] : firsts[n - 1] + rows, :].astype(F32)
    for k in range(n - 2, -1, -1):
        dn = refs[k][firsts[k] : firsts[k] + rows, :].astype(F32) + dn
    store_parts(carried[...].astype(F32) + norm_back(dn, gain[...], hat, rate), outs[:-1])
    outs[-1][...] = jnp.sum(dn * hat, axis=0, keepdims=True)


def sum_kernel(n, firsts, *refs):
    outs = refs[n:]
    rows = outs[0].shape[0] * len(outs)
    total = refs[n - 1][firsts[n - 1] : firsts[n - 1] + rows, :].astype(F32)
    for k in range(n - 2, -1, -1):
        total = refs[k][firsts[k] : firsts[k] + rows, :].astype(F32) + total
    store_parts(total, outs)


def in_vmem(n):
    return [pl.BlockSpec(memory_space=VMEM)] * n


def shape_of(shape, dtype):
    return jax.ShapeDtypeStruct(shape, dtype)


def run(kernel, operands, outs, scratch, flops, name, vmem=12, anywhere=0):
    moved = sum(o.size * o.dtype.itemsize for o in operands) + sum(
        o.size * o.dtype.itemsize for o in outs
    )
    scalar = operands[0].dtype == jnp.int32
    specs = in_vmem(len(operands))
    if scalar:
        specs[0] = pl.BlockSpec(memory_space=pltpu.SMEM)
    return pl.pallas_call(
        kernel,
        out_shape=outs,
        in_specs=specs,
        out_specs=in_vmem(len(outs) - anywhere)
        + [pl.BlockSpec(memory_space=pl.ANY)] * anywhere,
        scratch_shapes=scratch,
        compiler_params=pltpu.CompilerParams(vmem_limit_bytes=vmem << 20),
        cost_estimate=pl.CostEstimate(flops=flops, bytes_accessed=moved, transcendentals=0),
        name=name,
    )(*operands)


def after(value, *tokens):
    return lax.optimization_barrier((value, *tokens))[0]


def body(sizes, tokens, norm_gains, temporal_qkv, temporal_proj, spatial_qkv, spatial_proj, up_weight, down_weight, cotangent):
    n_fsdp, n_ctx, n_tp = sizes
    swap = n_fsdp == 2
    d_model = tokens.shape[3]
    d_part = d_model // n_fsdp
    places = tokens.shape[0]
    block = 2 * (-(-places // 4))
    x, i, z = lax.axis_index("fsdp"), lax.axis_index("ctx"), lax.axis_index("tp")
    core, chip = i % 2, i // 2
    is_source = (z // 2) == core

    def permute_ctx(v, bits):
        return lax.ppermute(v, "ctx", [(a, a ^ bits) for a in range(n_ctx)])

    def permute_tp(v, bits):
        return lax.ppermute(v, "tp", [(a, a ^ bits) for a in range(n_tp)])

    def permute_fsdp(v):
        return lax.ppermute(v, "fsdp", [(0, 1), (1, 0)])

    def along(v, bits, back=False):
        pairs = []
        for a in range(n_ctx):
            for b in (2 * (a % 2), 2 * (a % 2) + 1):
                there, here = a * n_tp + (b ^ bits), a * n_tp + b
                pairs.append((there, here) if back else (here, there))
        return lax.ppermute(v, ("ctx", "tp"), pairs)

    def exclusive(parts, bits):
        low, high = (bits & 1) == 1, (bits & 2) == 2
        parts = [jnp.where(low, parts[d ^ 1], parts[d]) for d in range(4)]
        return [jnp.where(high, parts[d ^ 2], parts[d]) for d in range(4)]

    slot_bits = (z & 2) | ((z & 1) ^ core)
    part_rows = 2 * block

    def to_time(rows):
        t = jnp.transpose(rows, (2, 1, 0, 3))
        t = jnp.pad(t, ((0, 0), (0, 0), (0, 2 * block - places), (0, 0)))
        parts = [t[c, :, b * block : (b + 1) * block] for c in range(2) for b in range(2)]
        parts = exclusive([v.reshape(part_rows, d_model) for v in parts], i)
        got = [parts[0]] + [permute_ctx(parts[e], e) for e in range(1, 4)]
        return exclusive(got, slot_bits)

    def time_sends(own):
        parts = exclusive(own, slot_bits)
        return [parts[0]] + [permute_ctx(parts[e], e) for e in range(1, 4)]

    def time_finish(got):
        got = [v.reshape(2, block, d_model) for v in exclusive(got, i)]
        t = jnp.stack(
            [jnp.concatenate((got[2 * c], got[2 * c + 1]), axis=1)[:, :places] for c in range(2)]
        )
        return jnp.transpose(t, (2, 1, 0, 3))

    def turn(own):
        return [own[0]] + [permute_tp(own[e], e) for e in range(1, 4)]

    rows_n = 8 * block
    flat = (rows_n, d_model)

    def attention_pack(qkv, proj):
        return jnp.concatenate((jnp.transpose(qkv, (1, 2, 0)).reshape(-1, d_part), proj), axis=0)

    def spread_first(shard):
        return jnp.where(is_source, shard, along(shard, 2))

    hid_half = up_weight.shape[1] // 2

    def feed_pack():
        up = lax.dynamic_slice_in_dim(up_weight, chip * hid_half, hid_half, axis=1)
        down = lax.dynamic_slice_in_dim(down_weight, chip * hid_half, hid_half, axis=0)
        return jnp.concatenate((up, down.reshape(d_part, hid_half)), axis=0)

    def feed_full(shard):
        every = lax.all_gather(shard, "fsdp", axis=0)
        up = every[:, :d_part].reshape(d_model, hid_half)
        down = every[:, d_part:].reshape(n_fsdp, hid_half, d_part)
        return [up, jnp.transpose(down, (1, 0, 2)).reshape(hid_half, d_model)]

    def owner_sum(a, b):
        mine = a + permute_tp(b, 1)
        return mine + along(mine, 2, True)

    def other_half(v):
        pairs = []
        for a in range(n_ctx):
            for b in (2 * (a % 2), 2 * (a % 2) + 1):
                pairs.append((a * n_tp + b, (a ^ 2) * n_tp + b))
        return lax.ppermute(v, ("ctx", "tp"), pairs)

    def owner_sends(a, b):
        return along(a, 2, True), along(b, 3, True), along(b, 1)

    def ordered(mine, other):
        return jnp.stack((jnp.where(chip == 0, mine, other), jnp.where(chip == 0, other, mine)))

    def to_pair(both):
        return jnp.where(is_source, both, permute_ctx(both, 1))

    def to_both(mine):
        return to_pair(ordered(mine, permute_ctx(mine, 2)))

    def first_sends(grads):
        send_x, _, send_y, _ = grads
        return permute_fsdp(send_x), permute_ctx(send_y, 2)

    def first_sums(grads, got):
        _, keep_x, _, keep_y = grads
        by_x, by_y = keep_x + got[0], keep_y + got[1]
        return (by_x[0], by_y[0]), (by_x[1], by_y[1])

    def second_sends(send):
        return permute_ctx(send[0], 2), permute_fsdp(send[1])

    def second_sums(keep, got):
        by_x, by_y = keep[0] + got[0], keep[1] + got[1]
        return [jnp.stack((by_x[g], by_y[g])) for g in range(by_x.shape[0])]

    def attention_out(total):
        joined_grad = jnp.stack((total[0, 0], total[1, 0], total[0, 1])).astype(F32)
        return jnp.transpose(joined_grad, (2, 0, 1)), total[1, 1].astype(F32)

    def feed_out(total):
        up = jnp.concatenate((total[0, :d_part], total[1, :d_part]), axis=1)
        down = jnp.concatenate((total[0, d_part:], total[1, d_part:]), axis=0)
        return up.astype(F32), down.astype(F32)

    def attention_grads_wide(grads):
        total = lax.psum_scatter(grads[0], "fsdp", scatter_dimension=2, tiled=True)
        total = total + permute_ctx(total, 2)
        if total.shape[0] == 2:
            mine = owner_sum(total[0], total[1])
        else:
            mine = total[0] + along(total[0], 2, True)
        full = jnp.where(is_source, mine, permute_ctx(mine, 1)).astype(F32)
        inner = full.shape[0] // 4
        joined_grad = full[: 3 * inner].reshape(3, inner, d_part)
        return jnp.transpose(joined_grad, (2, 0, 1)), full[3 * inner :]

    def feed_grads_wide(grads):
        up = lax.psum_scatter(grads[0], "fsdp", scatter_dimension=1, tiled=True)
        down = lax.psum_scatter(grads[1], "fsdp", scatter_dimension=2, tiled=True)
        up = to_both(owner_sum(up[0], up[1]))
        down = to_both(owner_sum(down[0], down[1]))
        return (
            jnp.concatenate((up[0], up[1]), axis=1).astype(F32),
            jnp.concatenate((down[0], down[1]), axis=0).astype(F32),
        )

    pieces = 2 if swap else 1
    width = d_model // pieces
    if swap:
        offsets = jnp.stack((x * width, (1 - x) * width, chip)).astype(jnp.int32)
    else:
        offsets = jnp.stack((0 * chip, chip)).astype(jnp.int32)

    at = jnp.arange(rows_n, dtype=jnp.int32)
    far = jnp.float32(-1e30)
    bias_t = jnp.where((at % block)[:, None] == (at % block)[None, :], 0.0, far).astype(F32)
    owner = jnp.where(at < rows_n // 2, core, 1 - core)
    real = owner * block + at % block < places
    bias_s = jnp.broadcast_to(jnp.where(real, 0.0, far).astype(F32)[None], (rows_n, rows_n))

    two = (2 * rows_n, d_model)
    unit = 2 * rows_n * d_model * d_model

    inner = temporal_qkv.shape[2]

    def shapes(rows, groups):
        all_rows = len(rows) * rows_n
        return (all_rows, d_model), [(all_rows, 3 * inner)] * groups, [(all_rows, inner)] * groups

    def part_shapes(rows):
        if len(rows) == 2:
            return [shape_of(flat, LOW)] * 2
        return [shape_of(flat, LOW)] * 2 + [shape_of(two, LOW)]

    def attend_forward(rows, gain, bias, weights, cut, name):
        groups = len(weights) // pieces
        wide, joined, heads = shapes(rows, groups)
        kept = [shape_of(s, LOW) for s in (wide, *joined, *heads)]
        kept += [shape_of(w.shape, LOW) for w in weights]
        outs = part_shapes(rows) + kept
        got = run(
            functools.partial(attend_forward_kernel, pieces, len(rows) // 2, groups, cut),
            [offsets, *rows, gain, bias, *weights],
            outs,
            [VMEM(s, LOW) for s in (wide, *joined, *heads)]
            + [VMEM(wide, F32), pltpu.SemaphoreType.DMA((len(kept),))],
            6 * unit,
            name,
            16,
            len(kept),
        )
        n = len(part_shapes(rows))
        m = n + 1 + 2 * groups
        return got[:n], got[n:m], got[m:]

    def attend_backward(rows, saved, bias, head, weights, cut, name):
        groups = len(weights) // pieces
        wide, joined, heads = shapes(rows, groups)
        outs = part_shapes(rows)
        n = len(outs)
        if swap:
            outs += [shape_of((2, groups, inner, width), LOW)] * 4
        else:
            outs += [shape_of((groups, 4 * inner, width), LOW)]
        m = len(outs)
        if cut:
            outs += [shape_of(flat, F32), shape_of((1, d_model), F32)]
        got = run(
            functools.partial(attend_backward_kernel, pieces, len(rows) // 2, groups, cut),
            [offsets, bias, *saved, *head, *weights],
            outs,
            [VMEM(s, LOW) for s in (wide, *joined, *heads)] + [VMEM(wide, F32)],
            12 * unit,
            name,
        )
        return got[:n], got[n:m], got[m:]

    def norm_backward(terms, base, gain, carried, name):
        *parts, gain_grad = run(
            functools.partial(norm_back_kernel, len(terms), [lo for _, lo in terms]),
            [v for v, _ in terms] + [base, gain, carried],
            [shape_of((part_rows, d_model), LOW)] * 4 + [shape_of((1, d_model), F32)],
            [],
            20 * rows_n * d_model,
            name,
        )
        return parts, gain_grad

    def sum_parts(terms, name, n=4):
        return run(
            functools.partial(sum_kernel, len(terms), [lo for _, lo in terms]),
            [v for v, _ in terms],
            [shape_of((rows_n // n, d_model), LOW)] * n,
            [],
            (12 * unit if name == "time_sum" else 4 * rows_n * d_model),
            name,
        )

    def other_x(v):
        return permute_fsdp(v) if swap else lax.all_gather(v, "fsdp", axis=1, tiled=True)

    def joined_pieces(first, first_x, second, second_x):
        return [first, first_x, second, second_x] if swap else [first_x, second_x]

    barrier = lax.optimization_barrier

    pack_t = attention_pack(temporal_qkv, temporal_proj)
    got_first_t = along(pack_t, 2)
    pack_s = attention_pack(spatial_qkv, spatial_proj)
    pack_f = feed_pack()
    if swap:
        gain_other = permute_fsdp(norm_gains)
        gains = jnp.where(
            x == 0,
            jnp.concatenate((norm_gains, gain_other), axis=1),
            jnp.concatenate((gain_other, norm_gains), axis=1),
        ).astype(F32)
    else:
        gains = lax.all_gather(norm_gains, "fsdp", axis=1, tiled=True).astype(F32)
    start = jnp.concatenate(to_time(tokens), axis=0)
    got_first_t, start, pack_s, pack_f, gains, cot = barrier(
        (got_first_t, start, pack_s, pack_f, gains, cotangent)
    )
    first_t = jnp.where(is_source, pack_t, got_first_t)
    first_tx = other_x(first_t)
    weights_t = [first_t, first_tx] if swap else [first_tx]
    near_start = permute_tp(start, 1)
    rows_t = [start, permute_ctx(start, 1), near_start, permute_ctx(near_start, 1)]
    got_first_s = along(pack_s, 2)
    cot_time = jnp.concatenate(to_time(cot), axis=0)
    first_tx, rows_t, got_first_s, cot_time = barrier((first_tx, rows_t, got_first_s, cot_time))
    first_s = jnp.where(is_source, pack_s, got_first_s)
    weights_t = [first_t, first_tx] if swap else [first_tx]

    second_s = permute_tp(first_s, 1)
    first_sx = other_x(first_s)
    parts_t, saved_t, weights_t = attend_forward(
        rows_t, gains[0:1], bias_t, weights_t, False, "time_forward"
    )
    parts_t, second_s, first_sx, pack_f, cot_time = barrier(
        (parts_t, second_s, first_sx, pack_f, cot_time)
    )
    got_t = permute_ctx(parts_t[2], 1)
    (chip_t,) = sum_parts(((parts_t[1], 0), (got_t, rows_n)), "time_near", 1)
    near_t = permute_tp(chip_t, 1)
    far_cot_time = permute_ctx(after(cot_time, near_t), 2)
    got_first_f = along(after(pack_f, chip_t), 2)
    second_sx = other_x(second_s)
    sums = sum_parts(((start, 0), (parts_t[0], 0), (got_t, 0), (near_t, 0)), "time_sum")
    sums, got_first_f = barrier((sums, got_first_f))
    own1 = jnp.concatenate(turn(sums), axis=0)
    own1, second_sx, far_cot_time = barrier((own1, second_sx, far_cot_time))
    pair1 = permute_ctx(own1, 1)
    first_f = jnp.where(is_source, pack_f, got_first_f)
    pair1, first_f = barrier((pair1, first_f))
    weights_s = joined_pieces(first_s, first_sx, second_s, second_sx)

    second_f = permute_tp(first_f, 1)
    if swap:
        first_fx = permute_fsdp(first_f)
    parts_s, saved_s, weights_s = attend_forward(
        [own1, pair1], gains[1:2], bias_s, weights_s, True, "space_forward"
    )
    back_s = permute_ctx(parts_s[1], 1)
    (own2,) = sum_parts(((own1, 0), (parts_s[0], 0), (back_s, 0)), "space_sum", 1)
    if swap:
        second_f, first_fx, own2 = barrier((second_f, first_fx, own2))
        second_fx = permute_fsdp(second_f)
        weights_f = [first_f, first_fx, second_f, second_fx]
    else:
        weights_f = [w for v in (first_f, second_f) for w in feed_full(v)]
    far_own2 = permute_ctx(own2, 2)
    rows_f = [own2, permute_ctx(own2, 1), far_own2, permute_ctx(far_own2, 1)]

    both_cot = []
    for d in range(4):
        at_d = slice(d * part_rows, (d + 1) * part_rows)
        both_cot.append(jnp.concatenate((cot_time[at_d], far_cot_time[at_d]), axis=0))
    both_cot = turn(after(both_cot, own2))
    if swap:
        both_cot, second_fx = barrier((both_cot, second_fx))
        weights_f = [first_f, first_fx, second_f, second_fx]
    cot_own = jnp.concatenate([v[:part_rows] for v in both_cot], axis=0)
    far_cot = jnp.concatenate([v[part_rows:] for v in both_cot], axis=0)
    cots = [cot_own, permute_ctx(cot_own, 1), far_cot, permute_ctx(far_cot, 1)]

    if swap:
        outs_f = [shape_of((2 * width, hid_half), LOW)] * 4
    else:
        outs_f = [shape_of((2, width, hid_half), LOW), shape_of((2, hid_half, width), LOW)]
    four = (4 * rows_n, d_model)
    out_own, out_send, out_far, dn3, dn3_send, dn3_far, *grads_f = run(
        functools.partial(feed_kernel, pieces, swap),
        [offsets, gains[2:3], *rows_f, *cots, *weights_f],
        [
            shape_of(flat, F32),
            shape_of(two, LOW),
            shape_of(flat, LOW),
            shape_of(two, LOW),
            shape_of(flat, LOW),
            shape_of(flat, LOW),
            *outs_f,
        ],
        [VMEM(four, LOW), VMEM(four, LOW), VMEM(four, F32), VMEM(four, F32)],
        24 * unit,
        "feed",
        20,
    )
    (chip_sum,) = sum_parts(((dn3_far, 0), (permute_ctx(dn3_send, 1), 0)), "feed_near", 1)
    far3 = permute_ctx(chip_sum, 2)
    far3_pair = permute_ctx(far3, 1)
    got3 = permute_ctx(dn3, 1)
    if swap:
        got_f = permute_fsdp(grads_f[3])
        got_f, far3_pair = barrier((got_f, far3_pair))
        b_f = grads_f[1] + got_f
        got_f = permute_fsdp(grads_f[2])
        add_f = permute_tp(b_f, 1)
    got_out = permute_ctx(out_send, 1)
    (chip_out,) = sum_parts(((out_far, 0), (got_out, rows_n)), "feed_out_near", 1)
    far_out = permute_ctx(after(chip_out, far3), 2)

    parts_s, grads_s, (carried2, gain3) = attend_backward(
        [own1, pair1],
        saved_s,
        bias_s,
        [rows_f[0], rows_f[1], dn3, got3, far3, far3_pair, gains[2:3], cots[0], cots[1]],
        weights_s,
        True,
        "space_backward",
    )
    if swap:
        parts_s, far_out, got_f, add_f = barrier((parts_s, far_out, got_f, add_f))
    got2 = permute_ctx(parts_s[1], 1)
    parts1, gain2 = norm_backward(
        ((parts_s[0], 0), (got2, 0)), own1, gains[1:2], carried2, "space_norm"
    )
    own_t = jnp.concatenate(turn(parts1), axis=0)
    near_own_t = permute_tp(own_t, 1)
    head_t = [own_t, permute_ctx(own_t, 1), near_own_t, permute_ctx(near_own_t, 1)]
    out_parts = sum_parts(((out_own, 0), (got_out, 0), (far_out, 0)), "feed_sum")
    if not swap:
        out_time = turn(out_parts)
    if swap:
        got_sums_s = first_sends(grads_s)
        keep_s, send_s = first_sums(grads_s, after(got_sums_s, own_t))
        got_sums_s = second_sends(send_s)
        a_f = grads_f[0] + got_f + add_f
        add_f = along(after(a_f, near_own_t), 2, True)

    parts_t, grads_t, _ = attend_backward(
        rows_t, saved_t, bias_t, head_t, weights_t, False, "time_backward"
    )
    if swap:
        parts_t, grads_t, got_sums_s, add_f, gain2, out_parts = barrier(
            (parts_t, grads_t, got_sums_s, add_f, gain2, out_parts)
        )
        got_sums_t = first_sends(grads_t)
        sums_s = second_sums(keep_s, got_sums_s)
        add_s = permute_tp(sums_s[1], 1)
    got1 = permute_ctx(parts_t[2], 1)
    (chip1,) = sum_parts(((parts_t[1], 0), (got1, rows_n)), "time_back_near", 1)
    near1 = permute_tp(chip1, 1)
    if swap:
        got_sums_t, near1, add_s = barrier((got_sums_t, near1, add_s))
        keep_t, send_t = first_sums(grads_t, got_sums_t)
        got_sums_t = second_sends(send_t)
    parts0, gain1 = norm_backward(
        ((parts_t[0], 0), (got1, 0), (near1, 0)), start, gains[0:1], own_t, "time_norm"
    )
    gain_all = jnp.concatenate((gain1, gain2, gain3), axis=0)
    if swap:
        a_s = sums_s[0] + add_s
        add_s = along(a_s, 2, True)
        total_f = a_f + add_f
        other_f = other_half(total_f)
        gain_got = permute_ctx(gain_all, 1)
        got_sums_t, add_s, other_f, gain_got = barrier((got_sums_t, add_s, other_f, gain_got))

        def across(v, axes, first, second):
            n = (n_fsdp if axes[0] == "fsdp" else n_ctx, n_tp)
            cells = [(a, b) for a in range(n[0]) for b in range(n[1])]
            pairs = [(a * n[1] + b, (a ^ first) * n[1] + (b ^ second)) for a, b in cells]
            return lax.ppermute(v, axes, pairs)

        (a_t,) = second_sums(keep_t, got_sums_t)
        got_t = along(a_t, 2, True)
        total_s = a_s + add_s
        other_s = other_half(total_s)
        gain_all = gain_all + gain_got
        gain_got = [across(gain_all, ("fsdp", "tp"), *d) for d in ((0, 1), (1, 0), (1, 1))]
        out_time = turn(out_parts)
        got_t, other_s, gain_got, parts0, out_time = barrier(
            (got_t, other_s, gain_got, parts0, out_time)
        )
        total_t = a_t + got_t
        other_t = other_half(total_t)
        gain_all = gain_all + gain_got[0] + (gain_got[1] + gain_got[2])
        gain_got = [across(gain_all, ("ctx", "tp"), *d) for d in ((0, 2), (2, 0), (2, 2))]
        both_f, both_s = ordered(total_f, other_f), ordered(total_s, other_s)
        up_grad, down_grad = feed_out(to_pair(both_f))
        s_qkv, s_proj = attention_out(to_pair(both_s))
        both_rows = [jnp.concatenate(pair, axis=0) for pair in zip(out_time, parts0)]
        got_both = time_sends(both_rows)
        other_t, gain_got, got_both, up_grad, down_grad, s_qkv, s_proj = barrier(
            (other_t, gain_got, got_both, up_grad, down_grad, s_qkv, s_proj)
        )
        both_t = ordered(total_t, other_t)
        pair_t = permute_ctx(both_t, 1)
        gain_all = gain_all + gain_got[0] + (gain_got[1] + gain_got[2])
        block_out = time_finish([v[:part_rows] for v in got_both])
        tokens_grad = time_finish([v[part_rows:] for v in got_both]).astype(F32)
        t_qkv, t_proj = attention_out(jnp.where(is_source, both_t, pair_t))
        gain_grads = lax.dynamic_slice_in_dim(gain_all, x * d_part, d_part, axis=1)
    else:
        tokens_grad = time_finish(time_sends(parts0)).astype(F32)
        block_out = time_finish(time_sends(out_time))
        up_grad, down_grad = feed_grads_wide(grads_f)
        s_qkv, s_proj = attention_grads_wide(grads_s)
        t_qkv, t_proj = attention_grads_wide(grads_t)
        for bits in (1, 2):
            gain_all = gain_all + permute_ctx(gain_all, bits)
        for bits in (1, 2):
            gain_all = gain_all + permute_tp(gain_all, bits)
        gain_grads = lax.psum_scatter(gain_all, "fsdp", scatter_dimension=1, tiled=True)
    return (
        block_out,
        tokens_grad,
        gain_grads,
        t_qkv,
        t_proj,
        s_qkv,
        s_proj,
        up_grad,
        down_grad,
    )


def solution(mesh):
    rows = P("tp", "ctx", "fsdp", None)
    weights = (
        P(None, "fsdp"),
        P("fsdp", None, "tp"),
        P("tp", "fsdp"),
        P("fsdp", None, "tp"),
        P("tp", "fsdp"),
        P("fsdp", "tp"),
        P("tp", "fsdp"),
    )
    sizes = (mesh.shape["fsdp"], mesh.shape["ctx"], mesh.shape["tp"])
    return jax.shard_map(
        functools.partial(body, sizes),
        mesh=mesh,
        in_specs=(rows, *weights, rows),
        out_specs=(rows, rows, *weights),
        check_vma=False,
    )
```

```python
import functools

import jax
import jax.numpy as jnp
from jax import lax
from jax.experimental import pallas as pl
from jax.experimental.pallas import tpu as pltpu
from jax.sharding import PartitionSpec as P

HEAD_DIM = 64
EPSILON = 1e-06
SCALE = HEAD_DIM ** (-0.5)
F32 = jnp.float32
LOW = jnp.bfloat16
VMEM = pltpu.VMEM


def dot(a, b, ca, cb):
    return lax.dot_general(a, b, (((ca,), (cb,)), ((), ())), preferred_element_type=F32)


def statistics(rows):
    center = rows - jnp.mean(rows, axis=-1, keepdims=True)
    rate = lax.rsqrt(jnp.mean(center * center, axis=-1, keepdims=True) + EPSILON)
    return center * rate, rate


def norm_back(grad, gain, hat, rate):
    t = grad * gain
    return rate * (
        t
        - jnp.mean(t, axis=-1, keepdims=True)
        - hat * jnp.mean(t * hat, axis=-1, keepdims=True)
    )


def to_blocks(own, pair, frames_cut):
    if not frames_cut:
        return jnp.concatenate((own, pair), axis=0)
    n = own.shape[0] // 8
    return jnp.concatenate(
        [
            rows[(2 * d + f) * n : (2 * d + f + 1) * n]
            for f in range(2)
            for rows in (own, pair)
            for d in range(4)
        ],
        axis=0,
    )


def from_blocks(rows, frames_cut):
    half = rows.shape[0] // 2
    if not frames_cut:
        return rows[:half], rows[half:]
    n = half // 8
    return tuple(
        jnp.concatenate(
            [
                rows[f * half + (4 * side + d) * n : f * half + (4 * side + d + 1) * n]
                for d in range(4)
                for f in range(2)
            ],
            axis=0,
        )
        for side in range(2)
    )


def split_store(chip, refs, piece, group, units):
    send_x, keep_x, send_y, keep_y = refs
    to_x = keep_x if piece == 0 else send_x
    to_x[0, group] = jnp.where(chip == 0, units[0], units[1])
    to_x[1, group] = jnp.where(chip == 0, units[1], units[0])
    keep_y[piece, group] = jnp.where(chip == 0, units[2], units[3])
    send_y[piece, group] = jnp.where(chip == 0, units[3], units[2])


def columns(off_ref, piece, width):
    return pl.ds(pl.multiple_of(off_ref[piece], 128), width)


def store_partial(total, outs, frames_cut):
    n, halves = total.shape[0], len(outs) - 1
    first, second = from_blocks(total[: n // halves, :], frames_cut)
    outs[0][...] = first.astype(LOW)
    if halves == 1:
        outs[1][...] = second.astype(LOW)
        return
    half = n // 4
    outs[2][:half, :] = second.astype(LOW)
    first, second = from_blocks(total[n // 2 :, :], frames_cut)
    outs[1][...] = first.astype(LOW)
    outs[2][half:, :] = second.astype(LOW)


def attend_forward_kernel(pieces, halves, groups, frames_cut, *refs):
    off = refs[0]
    rows_in = refs[1 : 1 + 2 * halves]
    rest = list(refs[1 + 2 * halves :])
    gain, bias = rest.pop(0), rest.pop(0)
    weights = [[rest.pop(0) for _ in range(pieces)] for _ in range(groups)]
    parts_out = [rest.pop(0) for _ in range(1 + halves)]
    saved_at = [rest.pop(0) for _ in range(1 + 2 * groups)]
    kept_at = [rest.pop(0) for _ in range(groups * pieces)]
    normed = rest.pop(0)
    joined, out = [rest.pop(0) for _ in range(groups)], [rest.pop(0) for _ in range(groups)]
    total, sems = rest
    copies = []

    def leave(source, target):
        copy = pltpu.make_async_copy(source, target, sems.at[len(copies)])
        copy.start()
        copies.append(copy)

    for g in range(groups):
        for p in range(pieces):
            leave(weights[g][p], kept_at[g * pieces + p])
    two = normed.shape[0] // halves
    for h in range(halves):
        rows = to_blocks(
            rows_in[2 * h][...].astype(F32), rows_in[2 * h + 1][...].astype(F32), frames_cut
        )
        hat, _ = statistics(rows)
        normed[h * two : (h + 1) * two, :] = (hat * gain[...]).astype(LOW)
    leave(normed, saved_at[0])
    width = weights[0][0].shape[1]
    heads3 = joined[0].shape[1]
    for g in range(groups):
        acc = None
        for p in range(pieces):
            term = dot(normed[:, columns(off, p, width)], weights[g][p][:heads3, :], 1, 1)
            acc = term if acc is None else acc + term
        joined[g][...] = acc.astype(LOW)
        leave(joined[g], saved_at[1 + g])
    block = two // 2
    inner = heads3 // 3

    def one_block(b, carry):
        at = pl.ds(pl.multiple_of(b * block, 16), block)
        for g in range(groups):
            rows3 = joined[g][at, :]
            parts = []
            for h in range(inner // HEAD_DIM):
                lo = h * HEAD_DIM
                q = rows3[:, lo : lo + HEAD_DIM]
                k = rows3[:, inner + lo : inner + lo + HEAD_DIM]
                v = rows3[:, 2 * inner + lo : 2 * inner + lo + HEAD_DIM]
                s = dot(q * LOW(SCALE), k, 1, 1) + bias[...]
                e = jnp.exp(s - jnp.max(s, axis=-1, keepdims=True))
                w = (e * (1.0 / jnp.sum(e, axis=-1, keepdims=True))).astype(LOW)
                parts.append(dot(w, v, 1, 0))
            out[g][at, :] = jnp.concatenate(parts, axis=1).astype(LOW)
        return carry

    lax.fori_loop(0, 2 * halves, one_block, 0)
    for g in range(groups):
        leave(out[g], saved_at[1 + groups + g])
    for p in range(pieces):
        acc = dot(out[0][...], weights[0][p][heads3:, :], 1, 0)
        for g in range(1, groups):
            acc = acc + dot(out[g][...], weights[g][p][heads3:, :], 1, 0)
        total[:, columns(off, p, width)] = acc
    store_partial(total, parts_out, frames_cut)
    for copy in copies:
        copy.wait()


def attend_backward_kernel(pieces, halves, groups, frames_cut, *refs):
    off, bias, normed = refs[:3]
    rest = list(refs[3:])
    joined, out = [rest.pop(0) for _ in range(groups)], [rest.pop(0) for _ in range(groups)]
    n_head = 9 if frames_cut else 2 * halves
    head = [rest.pop(0) for _ in range(n_head)]
    weights = [[rest.pop(0) for _ in range(pieces)] for _ in range(groups)]
    parts_out = [rest.pop(0) for _ in range(1 + halves)]
    grads = [rest.pop(0) for _ in range(4 if pieces == 2 else 1)]
    if frames_cut:
        carried, gain_grad = rest.pop(0), rest.pop(0)
    upstream = rest.pop(0)
    djoined, dout = [rest.pop(0) for _ in range(groups)], [rest.pop(0) for _ in range(groups)]
    total = rest.pop(0)
    two = upstream.shape[0] // halves
    half = two // 2
    if frames_cut:
        base_own, base_pair, grad_l, grad_r, far_own, far_pair, gain, cot_own, cot_pair = head
        both = []
        for lo, base, far_sum, cot in (
            (0, base_own, far_own, cot_own),
            (half, base_pair, far_pair, cot_pair),
        ):
            at = slice(lo, lo + half)
            far = slice(half - lo, 2 * half - lo)
            hat, rate = statistics(base[...].astype(F32))
            dn = grad_l[at, :].astype(F32) + grad_r[far, :].astype(F32) + far_sum[...].astype(F32)
            dx = cot[...].astype(F32) + norm_back(dn, gain[...], hat, rate)
            if lo == 0:
                carried[...] = dx
                gain_grad[...] = jnp.sum(dn * hat, axis=0, keepdims=True)
            both.append(dx)
        upstream[...] = to_blocks(both[0], both[1], frames_cut).astype(LOW)
    else:
        for r in range(2 * halves):
            upstream[r * half : (r + 1) * half, :] = head[r][...]
    width = weights[0][0].shape[1]
    heads3 = joined[0].shape[1]
    inner = heads3 // 3
    for g in range(groups):
        acc = None
        for p in range(pieces):
            term = dot(upstream[:, columns(off, p, width)], weights[g][p][heads3:, :], 1, 1)
            acc = term if acc is None else acc + term
        dout[g][...] = acc.astype(LOW)

    def one_block(b, carry):
        at = pl.ds(pl.multiple_of(b * half, 16), half)
        for g in range(groups):
            rows3 = joined[g][at, :]
            do3 = dout[g][at, :]
            dqs, dks, dvs = [], [], []
            for h in range(inner // HEAD_DIM):
                lo = h * HEAD_DIM
                q = rows3[:, lo : lo + HEAD_DIM]
                k = rows3[:, inner + lo : inner + lo + HEAD_DIM]
                v = rows3[:, 2 * inner + lo : 2 * inner + lo + HEAD_DIM]
                do = do3[:, lo : lo + HEAD_DIM]
                s = dot(q * LOW(SCALE), k, 1, 1) + bias[...]
                e = jnp.exp(s - jnp.max(s, axis=-1, keepdims=True))
                w = e * (1.0 / jnp.sum(e, axis=-1, keepdims=True))
                dw = dot(do, v, 1, 1)
                ds = (w * (dw - jnp.sum(w * dw, axis=-1, keepdims=True))).astype(LOW)
                dqs.append(dot(ds, k, 1, 0) * SCALE)
                dks.append(dot(ds, q, 0, 0) * SCALE)
                dvs.append(dot(w.astype(LOW), do, 0, 0))
            djoined[g][at, :] = jnp.concatenate(dqs + dks + dvs, axis=1).astype(LOW)
        return carry

    lax.fori_loop(0, 2 * halves, one_block, 0, unroll=3 - halves)
    chip = off[pieces]
    for p in range(pieces):
        cols = columns(off, p, width)
        wide = normed[:, cols]
        dy = upstream[:, cols]
        acc = None
        for g in range(groups):
            value = dot(djoined[g][...], wide, 0, 0).astype(LOW)
            proj = dot(out[g][...], dy, 0, 0).astype(LOW)
            if pieces == 2:
                units = [value[u * inner : (u + 1) * inner] for u in range(3)] + [proj]
                split_store(chip, grads, p, g, units)
            else:
                grads[0][g, :heads3] = value
                grads[0][g, heads3:] = proj
            term = dot(djoined[g][...], weights[g][p][:heads3, :], 1, 0)
            acc = term if acc is None else acc + term
        total[:, cols] = acc
    store_partial(total, parts_out, frames_cut)


def feed_kernel(pieces, packed, *refs):
    off, gain = refs[:2]
    rows_in, cots = refs[2:6], refs[6:10]
    at = 10
    n_w = 2 * pieces * (1 if packed else 2)
    weights = refs[at : at + n_w]
    at += n_w
    out_own, out_send, out_far, dn_near, dn_send, dn_far = refs[at : at + 6]
    at += 6
    n_g = 4 if packed else 2
    grads = refs[at : at + n_g]
    normed, cot, total, dtotal = refs[at + n_g :]
    n = rows_in[0].shape[0]
    for r in range(4):
        rows_at = slice(r * n, (r + 1) * n)
        hat, _ = statistics(rows_in[r][...].astype(F32))
        normed[rows_at, :] = (hat * gain[...]).astype(LOW)
        cot[rows_at, :] = cots[r][...]
    for c in range(2):
        ups, downs = [], []
        for p in range(pieces):
            if packed:
                w = weights[c * pieces + p]
                wide = w.shape[0] // 2
                ups.append(w[:wide, :])
                downs.append(w[wide:, :])
            else:
                ups.append(weights[2 * (c * pieces + p)][...])
                downs.append(weights[2 * (c * pieces + p) + 1][...])
        width = ups[0].shape[0]
        hidden = dact = None
        for p in range(pieces):
            cols = columns(off, p, width)
            term = dot(normed[:, cols], ups[p], 1, 0)
            dterm = dot(cot[:, cols], downs[p], 1, 1)
            hidden = term if hidden is None else hidden + term
            dact = dterm if dact is None else dact + dterm
        cdf = 0.5 * (1.0 + lax.erf(hidden * (2.0**-0.5)))
        act = (hidden * cdf).astype(LOW)
        slope = cdf + hidden * (jnp.exp(-0.5 * hidden * hidden) * (2.0 * jnp.pi) ** -0.5)
        dhid = (dact * slope).astype(LOW)
        for p in range(pieces):
            cols = columns(off, p, width)
            term = dot(act, downs[p], 1, 0)
            dterm = dot(dhid, ups[p], 1, 1)
            if c == 0:
                total[:, cols] = term
                dtotal[:, cols] = dterm
            else:
                total[:, cols] += term
                dtotal[:, cols] += dterm
            up_grad = dot(normed[:, cols], dhid, 0, 0).astype(LOW)
            down_grad = dot(act, cot[:, cols], 0, 0).astype(LOW)
            if packed:
                grads[2 * p + c][:width, :] = up_grad
                grads[2 * p + c][width:, :] = down_grad
            else:
                grads[0][c] = up_grad
                grads[1][c] = down_grad
    out_own[...] = rows_in[0][...].astype(F32) + total[:n, :]
    out_send[:n, :] = total[n : 2 * n, :].astype(LOW)
    out_send[n:, :] = total[3 * n :, :].astype(LOW)
    out_far[...] = total[2 * n : 3 * n, :].astype(LOW)
    dn_near[...] = dtotal[: 2 * n, :].astype(LOW)
    dn_far[...] = dtotal[2 * n : 3 * n, :].astype(LOW)
    dn_send[...] = dtotal[3 * n :, :].astype(LOW)


def store_parts(rows, outs):
    n = rows.shape[0] // len(outs)
    for d, out in enumerate(outs):
        out[...] = rows[d * n : (d + 1) * n].astype(out.dtype)


def norm_back_kernel(n, firsts, *refs):
    base, gain, carried = refs[n : n + 3]
    outs = refs[n + 3 :]
    rows = base.shape[0]
    hat, rate = statistics(base[...].astype(F32))
    dn = refs[n - 1][firsts[n - 1] : firsts[n - 1] + rows, :].astype(F32)
    for k in range(n - 2, -1, -1):
        dn = refs[k][firsts[k] : firsts[k] + rows, :].astype(F32) + dn
    store_parts(carried[...].astype(F32) + norm_back(dn, gain[...], hat, rate), outs[:-1])
    outs[-1][...] = jnp.sum(dn * hat, axis=0, keepdims=True)


def sum_kernel(n, firsts, *refs):
    outs = refs[n:]
    rows = outs[0].shape[0] * len(outs)
    total = refs[n - 1][firsts[n - 1] : firsts[n - 1] + rows, :].astype(F32)
    for k in range(n - 2, -1, -1):
        total = refs[k][firsts[k] : firsts[k] + rows, :].astype(F32) + total
    store_parts(total, outs)


def in_vmem(n):
    return [pl.BlockSpec(memory_space=VMEM)] * n


def shape_of(shape, dtype):
    return jax.ShapeDtypeStruct(shape, dtype)


def run(kernel, operands, outs, scratch, flops, name, vmem=12, anywhere=0):
    moved = sum(o.size * o.dtype.itemsize for o in operands) + sum(
        o.size * o.dtype.itemsize for o in outs
    )
    scalar = operands[0].dtype == jnp.int32
    specs = in_vmem(len(operands))
    if scalar:
        specs[0] = pl.BlockSpec(memory_space=pltpu.SMEM)
    return pl.pallas_call(
        kernel,
        out_shape=outs,
        in_specs=specs,
        out_specs=in_vmem(len(outs) - anywhere)
        + [pl.BlockSpec(memory_space=pl.ANY)] * anywhere,
        scratch_shapes=scratch,
        compiler_params=pltpu.CompilerParams(vmem_limit_bytes=vmem << 20),
        cost_estimate=pl.CostEstimate(flops=flops, bytes_accessed=moved, transcendentals=0),
        name=name,
    )(*operands)


def after(value, *tokens):
    return lax.optimization_barrier((value, *tokens))[0]


def body(sizes, tokens, norm_gains, temporal_qkv, temporal_proj, spatial_qkv, spatial_proj, up_weight, down_weight, cotangent):
    n_fsdp, n_ctx, n_tp = sizes
    swap = n_fsdp == 2
    d_model = tokens.shape[3]
    d_part = d_model // n_fsdp
    places = tokens.shape[0]
    block = 2 * (-(-places // 4))
    x, i, z = lax.axis_index("fsdp"), lax.axis_index("ctx"), lax.axis_index("tp")
    core, chip = i % 2, i // 2
    is_source = (z // 2) == core

    def permute_ctx(v, bits):
        return lax.ppermute(v, "ctx", [(a, a ^ bits) for a in range(n_ctx)])

    def permute_tp(v, bits):
        return lax.ppermute(v, "tp", [(a, a ^ bits) for a in range(n_tp)])

    def permute_fsdp(v):
        return lax.ppermute(v, "fsdp", [(0, 1), (1, 0)])

    def along(v, bits, back=False):
        pairs = []
        for a in range(n_ctx):
            for b in (2 * (a % 2), 2 * (a % 2) + 1):
                there, here = a * n_tp + (b ^ bits), a * n_tp + b
                pairs.append((there, here) if back else (here, there))
        return lax.ppermute(v, ("ctx", "tp"), pairs)

    def exclusive(parts, bits):
        low, high = (bits & 1) == 1, (bits & 2) == 2
        parts = [jnp.where(low, parts[d ^ 1], parts[d]) for d in range(4)]
        return [jnp.where(high, parts[d ^ 2], parts[d]) for d in range(4)]

    slot_bits = (z & 2) | ((z & 1) ^ core)
    part_rows = 2 * block

    def to_time(rows):
        t = jnp.transpose(rows, (2, 1, 0, 3))
        t = jnp.pad(t, ((0, 0), (0, 0), (0, 2 * block - places), (0, 0)))
        parts = [t[c, :, b * block : (b + 1) * block] for c in range(2) for b in range(2)]
        parts = exclusive([v.reshape(part_rows, d_model) for v in parts], i)
        got = [parts[0]] + [permute_ctx(parts[e], e) for e in range(1, 4)]
        return exclusive(got, slot_bits)

    def time_sends(own):
        parts = exclusive(own, slot_bits)
        return [parts[0]] + [permute_ctx(parts[e], e) for e in range(1, 4)]

    def time_finish(got):
        got = [v.reshape(2, block, d_model) for v in exclusive(got, i)]
        t = jnp.stack(
            [jnp.concatenate((got[2 * c], got[2 * c + 1]), axis=1)[:, :places] for c in range(2)]
        )
        return jnp.transpose(t, (2, 1, 0, 3))

    def turn(own):
        return [own[0]] + [permute_tp(own[e], e) for e in range(1, 4)]

    rows_n = 8 * block
    flat = (rows_n, d_model)

    def attention_pack(qkv, proj):
        return jnp.concatenate((jnp.transpose(qkv, (1, 2, 0)).reshape(-1, d_part), proj), axis=0)

    def spread_first(shard):
        return jnp.where(is_source, shard, along(shard, 2))

    hid_half = up_weight.shape[1] // 2

    def feed_pack():
        up = lax.dynamic_slice_in_dim(up_weight, chip * hid_half, hid_half, axis=1)
        down = lax.dynamic_slice_in_dim(down_weight, chip * hid_half, hid_half, axis=0)
        return jnp.concatenate((up, down.reshape(d_part, hid_half)), axis=0)

    def feed_full(shard):
        every = lax.all_gather(shard, "fsdp", axis=0)
        up = every[:, :d_part].reshape(d_model, hid_half)
        down = every[:, d_part:].reshape(n_fsdp, hid_half, d_part)
        return [up, jnp.transpose(down, (1, 0, 2)).reshape(hid_half, d_model)]

    def owner_sum(a, b):
        mine = a + permute_tp(b, 1)
        return mine + along(mine, 2, True)

    def other_half(v):
        pairs = []
        for a in range(n_ctx):
            for b in (2 * (a % 2), 2 * (a % 2) + 1):
                pairs.append((a * n_tp + b, (a ^ 2) * n_tp + b))
        return lax.ppermute(v, ("ctx", "tp"), pairs)

    def owner_sends(a, b):
        return along(a, 2, True), along(b, 3, True), along(b, 1)

    def ordered(mine, other):
        return jnp.stack((jnp.where(chip == 0, mine, other), jnp.where(chip == 0, other, mine)))

    def to_pair(both):
        return jnp.where(is_source, both, permute_ctx(both, 1))

    def to_both(mine):
        return to_pair(ordered(mine, permute_ctx(mine, 2)))

    def first_sends(grads):
        send_x, _, send_y, _ = grads
        return permute_fsdp(send_x), permute_ctx(send_y, 2)

    def first_sums(grads, got):
        _, keep_x, _, keep_y = grads
        by_x, by_y = keep_x + got[0], keep_y + got[1]
        return (by_x[0], by_y[0]), (by_x[1], by_y[1])

    def second_sends(send):
        return permute_ctx(send[0], 2), permute_fsdp(send[1])

    def second_sums(keep, got):
        by_x, by_y = keep[0] + got[0], keep[1] + got[1]
        return [jnp.stack((by_x[g], by_y[g])) for g in range(by_x.shape[0])]

    def attention_out(total):
        joined_grad = jnp.stack((total[0, 0], total[1, 0], total[0, 1])).astype(F32)
        return jnp.transpose(joined_grad, (2, 0, 1)), total[1, 1].astype(F32)

    def feed_out(total):
        up = jnp.concatenate((total[0, :d_part], total[1, :d_part]), axis=1)
        down = jnp.concatenate((total[0, d_part:], total[1, d_part:]), axis=0)
        return up.astype(F32), down.astype(F32)

    def attention_grads_wide(grads):
        total = lax.psum_scatter(grads[0], "fsdp", scatter_dimension=2, tiled=True)
        total = total + permute_ctx(total, 2)
        if total.shape[0] == 2:
            mine = owner_sum(total[0], total[1])
        else:
            mine = total[0] + along(total[0], 2, True)
        full = jnp.where(is_source, mine, permute_ctx(mine, 1)).astype(F32)
        inner = full.shape[0] // 4
        joined_grad = full[: 3 * inner].reshape(3, inner, d_part)
        return jnp.transpose(joined_grad, (2, 0, 1)), full[3 * inner :]

    def feed_grads_wide(grads):
        up = lax.psum_scatter(grads[0], "fsdp", scatter_dimension=1, tiled=True)
        down = lax.psum_scatter(grads[1], "fsdp", scatter_dimension=2, tiled=True)
        up = to_both(owner_sum(up[0], up[1]))
        down = to_both(owner_sum(down[0], down[1]))
        return (
            jnp.concatenate((up[0], up[1]), axis=1).astype(F32),
            jnp.concatenate((down[0], down[1]), axis=0).astype(F32),
        )

    pieces = 2 if swap else 1
    width = d_model // pieces
    if swap:
        offsets = jnp.stack((x * width, (1 - x) * width, chip)).astype(jnp.int32)
    else:
        offsets = jnp.stack((0 * chip, chip)).astype(jnp.int32)

    at = jnp.arange(rows_n, dtype=jnp.int32)
    far = jnp.float32(-1e30)
    bias_t = jnp.where((at % block)[:, None] == (at % block)[None, :], 0.0, far).astype(F32)
    owner = jnp.where(at < rows_n // 2, core, 1 - core)
    real = owner * block + at % block < places
    bias_s = jnp.broadcast_to(jnp.where(real, 0.0, far).astype(F32)[None], (rows_n, rows_n))

    two = (2 * rows_n, d_model)
    unit = 2 * rows_n * d_model * d_model

    inner = temporal_qkv.shape[2]

    def shapes(rows, groups):
        all_rows = len(rows) * rows_n
        return (all_rows, d_model), [(all_rows, 3 * inner)] * groups, [(all_rows, inner)] * groups

    def part_shapes(rows):
        if len(rows) == 2:
            return [shape_of(flat, LOW)] * 2
        return [shape_of(flat, LOW)] * 2 + [shape_of(two, LOW)]

    def attend_forward(rows, gain, bias, weights, cut, name):
        groups = len(weights) // pieces
        wide, joined, heads = shapes(rows, groups)
        kept = [shape_of(s, LOW) for s in (wide, *joined, *heads)]
        kept += [shape_of(w.shape, LOW) for w in weights]
        outs = part_shapes(rows) + kept
        got = run(
            functools.partial(attend_forward_kernel, pieces, len(rows) // 2, groups, cut),
            [offsets, *rows, gain, bias, *weights],
            outs,
            [VMEM(s, LOW) for s in (wide, *joined, *heads)]
            + [VMEM(wide, F32), pltpu.SemaphoreType.DMA((len(kept),))],
            6 * unit,
            name,
            16,
            len(kept),
        )
        n = len(part_shapes(rows))
        m = n + 1 + 2 * groups
        return got[:n], got[n:m], got[m:]

    def attend_backward(rows, saved, bias, head, weights, cut, name):
        groups = len(weights) // pieces
        wide, joined, heads = shapes(rows, groups)
        outs = part_shapes(rows)
        n = len(outs)
        if swap:
            outs += [shape_of((2, groups, inner, width), LOW)] * 4
        else:
            outs += [shape_of((groups, 4 * inner, width), LOW)]
        m = len(outs)
        if cut:
            outs += [shape_of(flat, F32), shape_of((1, d_model), F32)]
        got = run(
            functools.partial(attend_backward_kernel, pieces, len(rows) // 2, groups, cut),
            [offsets, bias, *saved, *head, *weights],
            outs,
            [VMEM(s, LOW) for s in (wide, *joined, *heads)] + [VMEM(wide, F32)],
            12 * unit,
            name,
        )
        return got[:n], got[n:m], got[m:]

    def norm_backward(terms, base, gain, carried, name):
        *parts, gain_grad = run(
            functools.partial(norm_back_kernel, len(terms), [lo for _, lo in terms]),
            [v for v, _ in terms] + [base, gain, carried],
            [shape_of((part_rows, d_model), LOW)] * 4 + [shape_of((1, d_model), F32)],
            [],
            20 * rows_n * d_model,
            name,
        )
        return parts, gain_grad

    def sum_parts(terms, name, n=4):
        return run(
            functools.partial(sum_kernel, len(terms), [lo for _, lo in terms]),
            [v for v, _ in terms],
            [shape_of((rows_n // n, d_model), LOW)] * n,
            [],
            (12 * unit if name == "time_sum" else 4 * rows_n * d_model),
            name,
        )

    def other_x(v):
        return permute_fsdp(v) if swap else lax.all_gather(v, "fsdp", axis=1, tiled=True)

    def joined_pieces(first, first_x, second, second_x):
        return [first, first_x, second, second_x] if swap else [first_x, second_x]

    barrier = lax.optimization_barrier

    pack_t = attention_pack(temporal_qkv, temporal_proj)
    got_first_t = along(pack_t, 2)
    pack_s = attention_pack(spatial_qkv, spatial_proj)
    pack_f = feed_pack()
    if swap:
        gain_other = permute_fsdp(norm_gains)
        gains = jnp.where(
            x == 0,
            jnp.concatenate((norm_gains, gain_other), axis=1),
            jnp.concatenate((gain_other, norm_gains), axis=1),
        ).astype(F32)
    else:
        gains = lax.all_gather(norm_gains, "fsdp", axis=1, tiled=True).astype(F32)
    start = jnp.concatenate(to_time(tokens), axis=0)
    got_first_t, start, pack_s, pack_f, gains, cot = barrier(
        (got_first_t, start, pack_s, pack_f, gains, cotangent)
    )
    first_t = jnp.where(is_source, pack_t, got_first_t)
    first_tx = other_x(first_t)
    weights_t = [first_t, first_tx] if swap else [first_tx]
    near_start = permute_tp(start, 1)
    rows_t = [start, permute_ctx(start, 1), near_start, permute_ctx(near_start, 1)]
    got_first_s = along(pack_s, 2)
    cot_time = jnp.concatenate(to_time(cot), axis=0)
    first_tx, rows_t, got_first_s, cot_time = barrier((first_tx, rows_t, got_first_s, cot_time))
    first_s = jnp.where(is_source, pack_s, got_first_s)
    weights_t = [first_t, first_tx] if swap else [first_tx]

    second_s = permute_tp(first_s, 1)
    first_sx = other_x(first_s)
    parts_t, saved_t, weights_t = attend_forward(
        rows_t, gains[0:1], bias_t, weights_t, False, "time_forward"
    )
    parts_t, second_s, first_sx, pack_f, cot_time = barrier(
        (parts_t, second_s, first_sx, pack_f, cot_time)
    )
    got_t = permute_ctx(parts_t[2], 1)
    (chip_t,) = sum_parts(((parts_t[1], 0), (got_t, rows_n)), "time_near", 1)
    near_t = permute_tp(chip_t, 1)
    far_cot_time = permute_ctx(after(cot_time, near_t), 2)
    got_first_f = along(after(pack_f, chip_t), 2)
    second_sx = other_x(second_s)
    sums = sum_parts(((start, 0), (parts_t[0], 0), (got_t, 0), (near_t, 0)), "time_sum")
    sums, got_first_f = barrier((sums, got_first_f))
    own1 = jnp.concatenate(turn(sums), axis=0)
    own1, second_sx, far_cot_time = barrier((own1, second_sx, far_cot_time))
    pair1 = permute_ctx(own1, 1)
    first_f = jnp.where(is_source, pack_f, got_first_f)
    pair1, first_f = barrier((pair1, first_f))
    weights_s = joined_pieces(first_s, first_sx, second_s, second_sx)

    second_f = permute_tp(first_f, 1)
    if swap:
        first_fx = permute_fsdp(first_f)
    parts_s, saved_s, weights_s = attend_forward(
        [own1, pair1], gains[1:2], bias_s, weights_s, True, "space_forward"
    )
    back_s = permute_ctx(parts_s[1], 1)
    (own2,) = sum_parts(((own1, 0), (parts_s[0], 0), (back_s, 0)), "space_sum", 1)
    if swap:
        second_f, first_fx, own2 = barrier((second_f, first_fx, own2))
        second_fx = permute_fsdp(second_f)
        weights_f = [first_f, first_fx, second_f, second_fx]
    else:
        weights_f = [w for v in (first_f, second_f) for w in feed_full(v)]
    far_own2 = permute_ctx(own2, 2)
    rows_f = [own2, permute_ctx(own2, 1), far_own2, permute_ctx(far_own2, 1)]

    both_cot = []
    for d in range(4):
        at_d = slice(d * part_rows, (d + 1) * part_rows)
        both_cot.append(jnp.concatenate((cot_time[at_d], far_cot_time[at_d]), axis=0))
    both_cot = turn(after(both_cot, own2))
    if swap:
        both_cot, second_fx = barrier((both_cot, second_fx))
        weights_f = [first_f, first_fx, second_f, second_fx]
    cot_own = jnp.concatenate([v[:part_rows] for v in both_cot], axis=0)
    far_cot = jnp.concatenate([v[part_rows:] for v in both_cot], axis=0)
    cots = [cot_own, permute_ctx(cot_own, 1), far_cot, permute_ctx(far_cot, 1)]

    if swap:
        outs_f = [shape_of((2 * width, hid_half), LOW)] * 4
    else:
        outs_f = [shape_of((2, width, hid_half), LOW), shape_of((2, hid_half, width), LOW)]
    four = (4 * rows_n, d_model)
    out_own, out_send, out_far, dn3, dn3_send, dn3_far, *grads_f = run(
        functools.partial(feed_kernel, pieces, swap),
        [offsets, gains[2:3], *rows_f, *cots, *weights_f],
        [
            shape_of(flat, F32),
            shape_of(two, LOW),
            shape_of(flat, LOW),
            shape_of(two, LOW),
            shape_of(flat, LOW),
            shape_of(flat, LOW),
            *outs_f,
        ],
        [VMEM(four, LOW), VMEM(four, LOW), VMEM(four, F32), VMEM(four, F32)],
        24 * unit,
        "feed",
        20,
    )
    (chip_sum,) = sum_parts(((dn3_far, 0), (permute_ctx(dn3_send, 1), 0)), "feed_near", 1)
    far3 = permute_ctx(chip_sum, 2)
    far3_pair = permute_ctx(far3, 1)
    got3 = permute_ctx(dn3, 1)
    if swap:
        got_f = permute_fsdp(grads_f[3])
        got_f, far3_pair = barrier((got_f, far3_pair))
        b_f = grads_f[1] + got_f
        got_f = permute_fsdp(grads_f[2])
        add_f = permute_tp(b_f, 1)
    got_out = permute_ctx(out_send, 1)
    (chip_out,) = sum_parts(((out_far, 0), (got_out, rows_n)), "feed_out_near", 1)
    far_out = permute_ctx(after(chip_out, far3), 2)

    parts_s, grads_s, (carried2, gain3) = attend_backward(
        [own1, pair1],
        saved_s,
        bias_s,
        [rows_f[0], rows_f[1], dn3, got3, far3, far3_pair, gains[2:3], cots[0], cots[1]],
        weights_s,
        True,
        "space_backward",
    )
    if swap:
        parts_s, far_out, got_f, add_f = barrier((parts_s, far_out, got_f, add_f))
    got2 = permute_ctx(parts_s[1], 1)
    parts1, gain2 = norm_backward(
        ((parts_s[0], 0), (got2, 0)), own1, gains[1:2], carried2, "space_norm"
    )
    own_t = jnp.concatenate(turn(parts1), axis=0)
    near_own_t = permute_tp(own_t, 1)
    head_t = [own_t, permute_ctx(own_t, 1), near_own_t, permute_ctx(near_own_t, 1)]
    out_parts = sum_parts(((out_own, 0), (got_out, 0), (far_out, 0)), "feed_sum")
    if not swap:
        out_time = turn(out_parts)
    if swap:
        got_sums_s = first_sends(grads_s)
        keep_s, send_s = first_sums(grads_s, after(got_sums_s, own_t))
        got_sums_s = second_sends(send_s)
        a_f = grads_f[0] + got_f + add_f
        add_f = along(after(a_f, near_own_t), 2, True)

    parts_t, grads_t, _ = attend_backward(
        rows_t, saved_t, bias_t, head_t, weights_t, False, "time_backward"
    )
    if swap:
        parts_t, grads_t, got_sums_s, add_f, gain2, out_parts = barrier(
            (parts_t, grads_t, got_sums_s, add_f, gain2, out_parts)
        )
        got_sums_t = first_sends(grads_t)
        sums_s = second_sums(keep_s, got_sums_s)
        add_s = permute_tp(sums_s[1], 1)
    got1 = permute_ctx(parts_t[2], 1)
    (chip1,) = sum_parts(((parts_t[1], 0), (got1, rows_n)), "time_back_near", 1)
    near1 = permute_tp(chip1, 1)
    if swap:
        got_sums_t, near1, add_s = barrier((got_sums_t, near1, add_s))
        keep_t, send_t = first_sums(grads_t, got_sums_t)
        got_sums_t = second_sends(send_t)
    parts0, gain1 = norm_backward(
        ((parts_t[0], 0), (got1, 0), (near1, 0)), start, gains[0:1], own_t, "time_norm"
    )
    gain_all = jnp.concatenate((gain1, gain2, gain3), axis=0)
    if swap:
        a_s = sums_s[0] + add_s
        add_s = along(a_s, 2, True)
        total_f = a_f + add_f
        other_f = other_half(total_f)
        gain_got = permute_ctx(gain_all, 1)
        got_sums_t, add_s, other_f, gain_got = barrier((got_sums_t, add_s, other_f, gain_got))

        def across(v, axes, first, second):
            n = (n_fsdp if axes[0] == "fsdp" else n_ctx, n_tp)
            cells = [(a, b) for a in range(n[0]) for b in range(n[1])]
            pairs = [(a * n[1] + b, (a ^ first) * n[1] + (b ^ second)) for a, b in cells]
            return lax.ppermute(v, axes, pairs)

        (a_t,) = second_sums(keep_t, got_sums_t)
        got_t = along(a_t, 2, True)
        total_s = a_s + add_s
        other_s = other_half(total_s)
        gain_all = gain_all + gain_got
        gain_got = [across(gain_all, ("fsdp", "tp"), *d) for d in ((0, 1), (1, 0), (1, 1))]
        out_time = turn(out_parts)
        got_t, other_s, gain_got, parts0, out_time = barrier(
            (got_t, other_s, gain_got, parts0, out_time)
        )
        total_t = a_t + got_t
        other_t = other_half(total_t)
        gain_all = gain_all + gain_got[0] + (gain_got[1] + gain_got[2])
        gain_got = [across(gain_all, ("ctx", "tp"), *d) for d in ((0, 2), (2, 0), (2, 2))]
        both_f, both_s = ordered(total_f, other_f), ordered(total_s, other_s)
        up_grad, down_grad = feed_out(to_pair(both_f))
        s_qkv, s_proj = attention_out(to_pair(both_s))
        both_rows = [jnp.concatenate(pair, axis=0) for pair in zip(out_time, parts0)]
        got_both = time_sends(both_rows)
        other_t, gain_got, got_both, up_grad, down_grad, s_qkv, s_proj = barrier(
            (other_t, gain_got, got_both, up_grad, down_grad, s_qkv, s_proj)
        )
        both_t = ordered(total_t, other_t)
        pair_t = permute_ctx(both_t, 1)
        gain_all = gain_all + gain_got[0] + (gain_got[1] + gain_got[2])
        block_out = time_finish([v[:part_rows] for v in got_both])
        tokens_grad = time_finish([v[part_rows:] for v in got_both]).astype(F32)
        t_qkv, t_proj = attention_out(jnp.where(is_source, both_t, pair_t))
        gain_grads = lax.dynamic_slice_in_dim(gain_all, x * d_part, d_part, axis=1)
    else:
        tokens_grad = time_finish(time_sends(parts0)).astype(F32)
        block_out = time_finish(time_sends(out_time))
        up_grad, down_grad = feed_grads_wide(grads_f)
        s_qkv, s_proj = attention_grads_wide(grads_s)
        t_qkv, t_proj = attention_grads_wide(grads_t)
        for bits in (1, 2):
            gain_all = gain_all + permute_ctx(gain_all, bits)
        for bits in (1, 2):
            gain_all = gain_all + permute_tp(gain_all, bits)
        gain_grads = lax.psum_scatter(gain_all, "fsdp", scatter_dimension=1, tiled=True)
    return (
        block_out,
        tokens_grad,
        gain_grads,
        t_qkv,
        t_proj,
        s_qkv,
        s_proj,
        up_grad,
        down_grad,
    )


def solution(mesh):
    rows = P("tp", "ctx", "fsdp", None)
    weights = (
        P(None, "fsdp"),
        P("fsdp", None, "tp"),
        P("tp", "fsdp"),
        P("fsdp", None, "tp"),
        P("tp", "fsdp"),
        P("fsdp", "tp"),
        P("tp", "fsdp"),
    )
    sizes = (mesh.shape["fsdp"], mesh.shape["ctx"], mesh.shape["tp"])
    return jax.shard_map(
        functools.partial(body, sizes),
        mesh=mesh,
        in_specs=(rows, *weights, rows),
        out_specs=(rows, rows, *weights),
        check_vma=False,
    )
```
